256 devices in a mesh: row: 16 (over y, z_lo, core), col: 16 (over z_hi, x).
Axes of the slice: x: 4, y: 4, z: 8 (z_hi: 4, z_lo: 2; z = z_hi * 2 + z_lo), core: 2. Of those that a mesh axis runs over, the one named last changes fastest.
Arguments:
- affinity: float32 [16384, 16384], P('row', 'col'), may hold values from 0.1 to 2600, as said below
- keep_words: int32 [16384, 5], P('row'), may hold values from 0 to 1073741823, as said below
Outputs:
- normalized: float32 [16384, 16384], P('row', 'col')
- degree: float32 [16384], P('row')
The draws below stay inside these ranges and needn't reach their ends.
Inputs may be any that keep to these rules, and one draw needn't show every extreme that they name: `affinity`: all entries are positive. `keep_words`: bit b of word w in row i is 1 where the block of 128 columns numbered 30 * w + b is kept for row i. The block that holds column i is always kept in row i. Bits for block numbers of 128 or more carry no meaning.
All inputs are finite; a program needn't handle non-finite values.
Results may differ from the reference program's by a relative error of at most 0.0003.
Values sent between devices are 32-bit elements; how exact they have to be, the bound alone decides.
A program may use at most 64 MiB of HBM per device.

```python
import math
import jax
import jax.numpy as jnp
from jax import lax

ROWS_DEV = 1024
TILE = 128
SEGMENTS = 16384
TILES = 128
WORDS = 5


def draw_affinity(key, part):
    base_key, row_key, col_key = jax.random.split(jax.random.fold_in(key, 11), 3)
    position = jnp.arange(SEGMENTS, dtype=jnp.float32) / SEGMENTS
    base_draw = jax.random.uniform(base_key, (SEGMENTS, SEGMENTS), jnp.float32, 0.1, 1.0)
    spread = math.log(10.0)
    growth = 3.0
    row_scale = jnp.exp(jax.random.uniform(row_key, (SEGMENTS,), jnp.float32, 0.0, spread)) * growth ** position
    col_scale = jnp.exp(jax.random.uniform(col_key, (SEGMENTS,), jnp.float32, 0.0, spread)) * growth ** position
    return base_draw * row_scale[:, None] * col_scale[None, :]


def draw_keep_words(key, part):
    packed_words = jax.random.randint(jax.random.fold_in(key, 23), (SEGMENTS, WORDS), 0, 1073741824, dtype=jnp.int32)
    own_tile = jnp.arange(SEGMENTS, dtype=jnp.int32) // TILE
    word_index = jnp.arange(WORDS, dtype=jnp.int32)
    own_bit = jnp.left_shift(jnp.int32(1), own_tile % 30)
    forced = jnp.where(word_index[None, :] == (own_tile // 30)[:, None], own_bit[:, None], 0).astype(jnp.int32)
    return jnp.bitwise_or(packed_words, forced)


def setup_inputs(seed: int = 0) -> dict:
    arg_keys = jax.random.split(jax.random.key(seed), 3)
    affinity = draw_affinity(jax.random.fold_in(arg_keys[2], 71), 0)
    keep_words = draw_keep_words(jax.random.fold_in(arg_keys[2], 71), 0)
    return {"affinity": affinity, "keep_words": keep_words}


def unpack_tiles(keep_words):
    shifts = jnp.arange(30, dtype=jnp.int32)
    bit_table = jnp.right_shift(keep_words[:, :, None], shifts[None, None, :]) & 1
    bit_table = bit_table.reshape(keep_words.shape[0], keep_words.shape[1] * 30)
    return bit_table[:, :TILES].astype(jnp.float32)

def reference(affinity, keep_words):
    tile_mask = unpack_tiles(keep_words)
    block_rows = ROWS_DEV
    starts = jnp.arange(SEGMENTS // block_rows, dtype=jnp.int32) * block_rows

    def symmetric_rows(first_row):
        own_rows = lax.dynamic_slice_in_dim(affinity, first_row, block_rows, 0)
        own_mask = lax.dynamic_slice_in_dim(tile_mask, first_row, block_rows, 0)
        across_cols = lax.dynamic_slice_in_dim(affinity, first_row, block_rows, 1)
        across_mask = lax.dynamic_slice_in_dim(tile_mask, first_row // TILE, block_rows // TILE, 1)
        pruned_own = own_rows * jnp.repeat(own_mask, TILE, axis=1)
        pruned_across = across_cols * jnp.repeat(across_mask, TILE, axis=1)
        return 0.5 * (pruned_own + pruned_across.T)

    def row_degree(first_row):
        return lax.optimization_barrier(jnp.sum(symmetric_rows(first_row), axis=1))
    degree_full = lax.map(row_degree, starts).reshape(SEGMENTS)
    inverse_root = lax.rsqrt(degree_full)

    def normal_rows(first_row):
        left_scale = lax.dynamic_slice_in_dim(inverse_root, first_row, block_rows, 0)
        return SEGMENTS * symmetric_rows(first_row) * left_scale[:, None] * inverse_root[None, :]
    normalized = lax.map(normal_rows, starts).reshape(SEGMENTS, SEGMENTS)
    return (normalized, degree_full / SEGMENTS)
```

```python
import functools

import jax
import jax.numpy as jnp
from jax import lax
from jax.experimental import pallas as pl
from jax.experimental.pallas import tpu as pltpu
from jax.sharding import PartitionSpec as P

TILE = 128
SIDE = 16
CHUNKS = 32
LOGICAL = pl.DeviceIdType.LOGICAL
OFFSETS = (
    (0, 0), (1, 0), (0, 1), (3, 0), (0, 3), (1, 1), (3, 3), (1, 3),
    (3, 1), (2, 0), (0, 2), (2, 1), (1, 2), (2, 3), (3, 2), (2, 2),
)


def packed(values):
    word = sum(v << (2 * n) for n, v in enumerate(values))
    return word - (1 << 32) if word >= 1 << 31 else word


X_STEPS = packed([o[0] for o in OFFSETS])
Y_STEPS = packed([o[1] for o in OFFSETS])


def kernel(aff, words, s_out, deg_out, block, mid, arrived, far_words, mask_rows, far_mask,
           col_sums, far_sums, row_sums, shares, half, half_far,
           load_sem, word_sem, leg_send, leg_recv, hop_send, final_sem,
           sum_sem, share_send, share_recv, half_sem, out_sem):
    row = lax.axis_index("row")
    col = lax.axis_index("col")
    me = row * SIDE + col
    partner = col * SIDE + row
    y, low, core = row // 4, (row // 2) % 2, row % 2
    high, x = col // 4, col % 4
    on_diagonal = row == col
    size = block.shape[0]
    chunk = size // CHUNKS
    groups = size // TILE

    def rows(n):
        return pl.ds(pl.multiple_of(n * chunk, chunk), chunk)

    def group(n):
        return pl.ds(pl.multiple_of(n * TILE, TILE), TILE)

    def place(cx, cy):
        return (cy * 4 + low * 2 + core) * SIDE + high * 4 + cx

    def steps(n):
        shift = 2 * (n % 16)
        return (X_STEPS >> shift) & 3, (Y_STEPS >> shift) & 3

    def mirror(device):
        return (device % SIDE) * SIDE + device // SIDE

    def to_partner(src, dst, sems):
        @pl.when(on_diagonal)
        def _():
            pltpu.make_async_copy(src, dst, sems.at[1]).start()

        @pl.when(jnp.logical_not(on_diagonal))
        def _():
            pltpu.make_async_remote_copy(
                src, dst, sems.at[0], sems.at[1], device_id=partner, device_id_type=LOGICAL
            ).start()

    def wait(ref, sem):
        pltpu.make_async_copy(ref, ref, sem).wait()

    def load(n):
        return pltpu.make_async_copy(aff.at[group(n)], block.at[group(n)], load_sem.at[n])

    to_partner(words, far_words, word_sem)

    def leg(n, carry):
        dx, dy = steps(n)
        relay = place((x + dx) % 4, (y + dy) % 4)
        direct = (n % 16 == 0) | (relay == partner)

        @pl.when(direct)
        def _():
            pltpu.make_async_remote_copy(
                aff.at[rows(n)], arrived.at[rows(n)], leg_send.at[n], final_sem.at[n // 4],
                device_id=partner, device_id_type=LOGICAL,
            ).start()

        @pl.when(jnp.logical_not(direct))
        def _():
            pltpu.make_async_remote_copy(
                aff.at[rows(n)], mid.at[rows(n)], leg_send.at[n], leg_recv.at[n],
                device_id=relay, device_id_type=LOGICAL,
            ).start()

        return carry

    def legs(first, last):
        @pl.when(jnp.logical_not(on_diagonal))
        def _():
            lax.fori_loop(first, last, leg, 0)

    def hop_of(n):
        dx, dy = steps(n)
        source = place((x + 4 - dx) % 4, (y + 4 - dy) % 4)
        target = mirror(source)
        return target, (n % 16 != 0) & (source != target) & (target != me)

    def hop(n, carry):
        target, used = hop_of(n)

        @pl.when(used)
        def _():
            wait(mid.at[rows(n)], leg_recv.at[n])
            pltpu.make_async_remote_copy(
                mid.at[rows(n)], arrived.at[rows(n)], hop_send.at[n], final_sem.at[n // 4],
                device_id=target, device_id_type=LOGICAL,
            ).start()

        return carry

    legs(0, CHUNKS // 2)

    def start_load(n, carry):
        load(n).start()
        return carry

    lax.fori_loop(0, groups, start_load, 0)

    @pl.when(on_diagonal)
    def _():
        def own(n, carry):
            pltpu.make_async_copy(aff.at[group(n)], arrived.at[group(n)], final_sem.at[n]).start()
            return carry

        lax.fori_loop(0, groups, own, 0)

    for t in range(groups):
        tile = col * groups + t
        bits = (words[pl.ds(tile // 30, 1), :] >> (tile % 30)) & 1
        mask_rows[t : t + 1, :] = bits.astype(jnp.float32)
    col_sums[...] = jnp.zeros_like(col_sums)

    def prune(n, carry):
        load(n).wait()
        mask = mask_rows[:, group(n)].T
        total = jnp.zeros((TILE, TILE), jnp.float32)
        for t in range(groups):
            lanes = slice(t * TILE, (t + 1) * TILE)
            kept = block[group(n), lanes] * mask[:, t : t + 1]
            block[group(n), lanes] = kept
            total += kept
            col_sums[:, lanes] += jnp.sum(kept, axis=0, keepdims=True)
        row_sums[:, group(n)] = jnp.sum(total.T, axis=0, keepdims=True)
        return carry

    lax.fori_loop(0, groups, prune, 0)
    to_partner(col_sums, far_sums, sum_sem)
    legs(CHUNKS // 2, CHUNKS)
    lax.fori_loop(0, 8, hop, 0)

    wait(far_sums, sum_sem.at[1])
    shares[col] = row_sums[...] + far_sums[...]

    def share(n, carry):
        other = (col + 1 + n) % SIDE
        pltpu.make_async_remote_copy(
            shares.at[col], shares.at[col], share_send.at[n], share_recv.at[col],
            device_id=row * SIDE + other, device_id_type=LOGICAL,
        ).start()
        return carry

    lax.fori_loop(0, SIDE - 1, share, 0)
    lax.fori_loop(8, 20, hop, 0)

    def share_in(n, carry):
        other = (col + 1 + n) % SIDE
        wait(shares.at[other], share_recv.at[other])
        return carry

    lax.fori_loop(0, SIDE - 1, share_in, 0)
    total = shares[0]
    for n in range(1, SIDE):
        total += shares[n]
    half[...] = 0.5 * total
    to_partner(half, half_far, half_sem)
    lax.fori_loop(20, CHUNKS, hop, 0)

    wait(far_words, word_sem.at[1])
    for t in range(groups):
        tile = row * groups + t
        bits = (far_words[pl.ds(tile // 30, 1), :] >> (tile % 30)) & 1
        far_mask[t : t + 1, :] = bits.astype(jnp.float32)

    def store(n):
        return pltpu.make_async_copy(block.at[:, group(n)], s_out.at[:, group(n)], out_sem.at[n])

    def finish(n, carry):
        wait(arrived.at[group(n)], final_sem.at[n])
        for t in range(groups):
            span = slice(t * TILE, (t + 1) * TILE)
            mirrored = arrived[group(n), span].T * far_mask[t : t + 1, group(n)]
            block[span, group(n)] = 0.5 * (block[span, group(n)] + mirrored)
        store(n).start()
        return carry

    lax.fori_loop(0, groups, finish, 0)
    wait(half_far, half_sem.at[1])
    deg_out[0:1, :] = half[...]
    deg_out[1:2, :] = half_far[...]

    @pl.when(jnp.logical_not(on_diagonal))
    def _():
        def sent(n, carry):
            wait(mid.at[rows(n)], leg_send.at[n])
            return carry

        lax.fori_loop(0, CHUNKS, sent, 0)
        wait(far_words, word_sem.at[0])
        wait(far_sums, sum_sem.at[0])
        wait(half_far, half_sem.at[0])

    def hopped(n, carry):
        _, used = hop_of(n)

        @pl.when(used)
        def _():
            wait(mid.at[rows(n)], hop_send.at[n])

        return carry

    lax.fori_loop(0, CHUNKS, hopped, 0)

    def share_out(n, carry):
        wait(shares.at[col], share_send.at[n])
        return carry

    lax.fori_loop(0, SIDE - 1, share_out, 0)

    def stored(n, carry):
        store(n).wait()
        return carry

    lax.fori_loop(0, groups, stored, 0)


def on_device(affinity, keep_words):
    size, _ = affinity.shape
    groups = size // TILE
    words = jnp.pad(keep_words.T, ((0, 8 - keep_words.shape[1]), (0, 0)))
    vec = pltpu.VMEM((1, size), jnp.float32)
    dma = pltpu.SemaphoreType.DMA
    symmetric, degrees = pl.pallas_call(
        kernel,
        out_shape=(
            jax.ShapeDtypeStruct((size, size), jnp.float32),
            jax.ShapeDtypeStruct((2, size), jnp.float32),
        ),
        in_specs=[pl.BlockSpec(memory_space=pl.ANY), pl.BlockSpec(memory_space=pltpu.VMEM)],
        out_specs=(pl.BlockSpec(memory_space=pl.ANY), pl.BlockSpec(memory_space=pltpu.VMEM)),
        scratch_shapes=[
            pltpu.VMEM((size, size), jnp.float32),
            pltpu.VMEM((size, size), jnp.float32),
            pltpu.VMEM((size, size), jnp.float32),
            pltpu.VMEM((8, size), jnp.int32),
            pltpu.VMEM((groups, size), jnp.float32),
            pltpu.VMEM((groups, size), jnp.float32),
            vec, vec, vec,
            pltpu.VMEM((SIDE, 1, size), jnp.float32),
            vec, vec,
            dma((groups,)), dma((2,)),
            dma((CHUNKS,)), dma((CHUNKS,)), dma((CHUNKS,)), dma((groups,)),
            dma((2,)), dma((SIDE - 1,)), dma((SIDE,)), dma((2,)), dma((groups,)),
        ],
        compiler_params=pltpu.CompilerParams(has_side_effects=True, vmem_limit_bytes=24 << 20),
        name="exchange",
    )(affinity, words)
    total = size * SIDE
    left, right = lax.rsqrt(degrees[0]), lax.rsqrt(degrees[1])
    normalized = total * symmetric * left[:, None] * right[None, :]
    return normalized, degrees[0] / total


def solution(mesh):
    in_specs = (P("row", "col"), P("row", None))
    out_specs = (P("row", "col"), P("row"))
    return jax.shard_map(
        on_device, mesh=mesh, in_specs=in_specs, out_specs=out_specs, check_vma=False
    )
```

```python
import functools

import jax
import jax.numpy as jnp
from jax import lax
from jax.experimental import pallas as pl
from jax.experimental.pallas import tpu as pltpu
from jax.sharding import PartitionSpec as P

TILE = 128
SIDE = 16
CHUNKS = 32
FIRST = 8
BEFORE_SUMS = 12
LOGICAL = pl.DeviceIdType.LOGICAL
OFFSETS = (
    (0, 0), (1, 0), (0, 1), (3, 0), (0, 3), (1, 1), (3, 3), (1, 3),
    (3, 1), (2, 0), (0, 2), (2, 1), (1, 2), (2, 3), (3, 2), (2, 2),
)


def packed(values):
    word = sum(v << (2 * n) for n, v in enumerate(values))
    return word - (1 << 32) if word >= 1 << 31 else word


X_STEPS = packed([o[0] for o in OFFSETS])
Y_STEPS = packed([o[1] for o in OFFSETS])


def kernel(aff, words, s_out, deg_out, block, mid, arrived, far_words, mask_rows, far_mask,
           col_sums, row_sums, row_shares, col_shares, near, far,
           load_sem, word_sem, leg_send, leg_recv, hop_send, final_sem,
           row_send, row_recv, col_send, col_recv, pair_sem, out_sem):
    row = lax.axis_index("row")
    col = lax.axis_index("col")
    me = row * SIDE + col
    partner = col * SIDE + row
    y, low, core = row // 4, (row // 2) % 2, row % 2
    high, x = col // 4, col % 4
    on_diagonal = row == col
    size = block.shape[0]
    chunk = size // CHUNKS
    groups = size // TILE

    def rows(n):
        return pl.ds(pl.multiple_of(n * chunk, chunk), chunk)

    def group(n):
        return pl.ds(pl.multiple_of(n * TILE, TILE), TILE)

    def place(cx, cy):
        return (cy * 4 + low * 2 + core) * SIDE + high * 4 + cx

    def steps(n):
        shift = 2 * (n % 16)
        return (X_STEPS >> shift) & 3, (Y_STEPS >> shift) & 3

    def mirror(device):
        return (device % SIDE) * SIDE + device // SIDE

    def to_partner(src, dst, sems):
        @pl.when(on_diagonal)
        def _():
            pltpu.make_async_copy(src, dst, sems.at[1]).start()

        @pl.when(jnp.logical_not(on_diagonal))
        def _():
            pltpu.make_async_remote_copy(
                src, dst, sems.at[0], sems.at[1], device_id=partner, device_id_type=LOGICAL
            ).start()

    def wait(ref, sem):
        pltpu.make_async_copy(ref, ref, sem).wait()

    def load(n):
        return pltpu.make_async_copy(aff.at[group(n)], block.at[group(n)], load_sem.at[n])

    to_partner(words, far_words, word_sem)

    def leg(n, carry):
        dx, dy = steps(n)
        relay = place((x + dx) % 4, (y + dy) % 4)
        direct = (n % 16 == 0) | (relay == partner)

        @pl.when(direct)
        def _():
            pltpu.make_async_remote_copy(
                aff.at[rows(n)], arrived.at[rows(n)], leg_send.at[n], final_sem.at[n // 4],
                device_id=partner, device_id_type=LOGICAL,
            ).start()

        @pl.when(jnp.logical_not(direct))
        def _():
            pltpu.make_async_remote_copy(
                aff.at[rows(n)], mid.at[rows(n)], leg_send.at[n], leg_recv.at[n],
                device_id=relay, device_id_type=LOGICAL,
            ).start()

        return carry

    def legs(first, last):
        @pl.when(jnp.logical_not(on_diagonal))
        def _():
            lax.fori_loop(first, last, leg, 0)

    def hop_of(n):
        dx, dy = steps(n)
        source = place((x + 4 - dx) % 4, (y + 4 - dy) % 4)
        target = mirror(source)
        return target, (n % 16 != 0) & (source != target) & (target != me)

    def hop(n, carry):
        target, used = hop_of(n)

        @pl.when(used)
        def _():
            wait(mid.at[rows(n)], leg_recv.at[n])
            pltpu.make_async_remote_copy(
                mid.at[rows(n)], arrived.at[rows(n)], hop_send.at[n], final_sem.at[n // 4],
                device_id=target, device_id_type=LOGICAL,
            ).start()

        return carry

    legs(0, FIRST)

    def start_load(n, carry):
        load(n).start()
        return carry

    lax.fori_loop(0, groups, start_load, 0)

    @pl.when(on_diagonal)
    def _():
        def own(n, carry):
            pltpu.make_async_copy(aff.at[group(n)], arrived.at[group(n)], final_sem.at[n]).start()
            return carry

        lax.fori_loop(0, groups, own, 0)

    for t in range(groups):
        tile = col * groups + t
        bits = (words[pl.ds(tile // 30, 1), :] >> (tile % 30)) & 1
        mask_rows[t : t + 1, :] = bits.astype(jnp.float32)
    col_sums[...] = jnp.zeros_like(col_sums)

    def prune(n, carry):
        load(n).wait()
        mask = mask_rows[:, group(n)].T
        total = jnp.zeros((TILE, TILE), jnp.float32)
        for t in range(groups):
            lanes = slice(t * TILE, (t + 1) * TILE)
            kept = block[group(n), lanes] * mask[:, t : t + 1]
            block[group(n), lanes] = kept
            total += kept
            col_sums[:, lanes] += jnp.sum(kept, axis=0, keepdims=True)
        row_sums[:, group(n)] = jnp.sum(total.T, axis=0, keepdims=True)
        return carry

    lax.fori_loop(0, groups, prune, 0)
    row_shares[col] = row_sums[...]
    col_shares[row] = col_sums[...]

    def share(n, carry):
        other = (col + 1 + n) % SIDE
        pltpu.make_async_remote_copy(
            row_shares.at[col], row_shares.at[col], row_send.at[n], row_recv.at[col],
            device_id=row * SIDE + other, device_id_type=LOGICAL,
        ).start()
        other = (row + 1 + n) % SIDE
        pltpu.make_async_remote_copy(
            col_shares.at[row], col_shares.at[row], col_send.at[n], col_recv.at[row],
            device_id=other * SIDE + col, device_id_type=LOGICAL,
        ).start()
        return carry

    lax.fori_loop(0, SIDE - 1, share, 0)
    legs(FIRST, CHUNKS)
    lax.fori_loop(0, BEFORE_SUMS, hop, 0)

    def share_in(n, carry):
        other = (col + 1 + n) % SIDE
        wait(row_shares.at[other], row_recv.at[other])
        other = (row + 1 + n) % SIDE
        wait(col_shares.at[other], col_recv.at[other])
        return carry

    lax.fori_loop(0, SIDE - 1, share_in, 0)
    row_total, col_total = row_shares[0], col_shares[0]
    for n in range(1, SIDE):
        row_total += row_shares[n]
        col_total += col_shares[n]
    near[0] = row_total
    near[1] = col_total
    to_partner(near, far, pair_sem)
    lax.fori_loop(BEFORE_SUMS, CHUNKS, hop, 0)

    wait(far_words, word_sem.at[1])
    for t in range(groups):
        tile = row * groups + t
        bits = (far_words[pl.ds(tile // 30, 1), :] >> (tile % 30)) & 1
        far_mask[t : t + 1, :] = bits.astype(jnp.float32)

    def store(n):
        return pltpu.make_async_copy(block.at[:, group(n)], s_out.at[:, group(n)], out_sem.at[n])

    def finish(n, carry):
        wait(arrived.at[group(n)], final_sem.at[n])
        for t in range(groups):
            span = slice(t * TILE, (t + 1) * TILE)
            mirrored = arrived[group(n), span].T * far_mask[t : t + 1, group(n)]
            block[span, group(n)] = 0.5 * (block[span, group(n)] + mirrored)
        store(n).start()
        return carry

    lax.fori_loop(0, groups, finish, 0)
    wait(far, pair_sem.at[1])
    deg_out[0:1, :] = 0.5 * (near[0] + far[1])
    deg_out[1:2, :] = 0.5 * (far[0] + near[1])

    @pl.when(jnp.logical_not(on_diagonal))
    def _():
        def sent(n, carry):
            wait(mid.at[rows(n)], leg_send.at[n])
            return carry

        lax.fori_loop(0, CHUNKS, sent, 0)
        wait(far_words, word_sem.at[0])
        wait(far, pair_sem.at[0])

    def hopped(n, carry):
        _, used = hop_of(n)

        @pl.when(used)
        def _():
            wait(mid.at[rows(n)], hop_send.at[n])

        return carry

    lax.fori_loop(0, CHUNKS, hopped, 0)

    def share_out(n, carry):
        wait(row_shares.at[col], row_send.at[n])
        wait(col_shares.at[row], col_send.at[n])
        return carry

    lax.fori_loop(0, SIDE - 1, share_out, 0)

    def stored(n, carry):
        store(n).wait()
        return carry

    lax.fori_loop(0, groups, stored, 0)


def on_device(affinity, keep_words):
    size, _ = affinity.shape
    groups = size // TILE
    words = keep_words.T
    vec = pltpu.VMEM((1, size), jnp.float32)
    dma = pltpu.SemaphoreType.DMA
    symmetric, degrees = pl.pallas_call(
        kernel,
        out_shape=(
            jax.ShapeDtypeStruct((size, size), jnp.float32),
            jax.ShapeDtypeStruct((2, size), jnp.float32),
        ),
        in_specs=[pl.BlockSpec(memory_space=pltpu.HBM), pl.BlockSpec(memory_space=pltpu.VMEM)],
        out_specs=(pl.BlockSpec(memory_space=pl.ANY), pl.BlockSpec(memory_space=pltpu.VMEM)),
        scratch_shapes=[
            pltpu.VMEM((size, size), jnp.float32),
            pltpu.VMEM((size, size), jnp.float32),
            pltpu.VMEM((size, size), jnp.float32),
            pltpu.VMEM(words.shape, jnp.int32),
            pltpu.VMEM((groups, size), jnp.float32),
            pltpu.VMEM((groups, size), jnp.float32),
            vec, vec,
            pltpu.VMEM((SIDE, 1, size), jnp.float32),
            pltpu.VMEM((SIDE, 1, size), jnp.float32),
            pltpu.VMEM((2, 1, size), jnp.float32),
            pltpu.VMEM((2, 1, size), jnp.float32),
            dma((groups,)), dma((2,)),
            dma((CHUNKS,)), dma((CHUNKS,)), dma((CHUNKS,)), dma((groups,)),
            dma((SIDE - 1,)), dma((SIDE,)), dma((SIDE - 1,)), dma((SIDE,)), dma((2,)), dma((groups,)),
        ],
        compiler_params=pltpu.CompilerParams(has_side_effects=True, vmem_limit_bytes=24 << 20),
        name="exchange",
    )(affinity, words)
    total = size * SIDE
    left, right = lax.rsqrt(degrees[0]), lax.rsqrt(degrees[1])
    normalized = total * symmetric * left[:, None] * right[None, :]
    return normalized, degrees[0] / total


def solution(mesh):
    in_specs = (P("row", "col"), P("row", None))
    out_specs = (P("row", "col"), P("row"))
    return jax.shard_map(
        on_device, mesh=mesh, in_specs=in_specs, out_specs=out_specs, check_vma=False
    )
```

```python
import functools

import jax
import jax.numpy as jnp
from jax import lax
from jax.experimental import pallas as pl
from jax.experimental.pallas import tpu as pltpu
from jax.sharding import PartitionSpec as P

TILE = 128
SIDE = 16
CHUNKS = 32
FIRST = 8
BEFORE_SUMS = 12
LOGICAL = pl.DeviceIdType.LOGICAL
DIRECT = 127
MAX_RELAYED = 114
SENDS = (
    0x1fff07bf83bfc1cfe0dff06bf833fc18fe0bff05bf82bfc14fe09ff04bf823fc10fe07ff03bf81bfc0cfe05ff02bf813fc08fe03ff01bf80bfc04fe01ff00bf803fc00fe0,
    0x1fff07bf83bfc1cfe0dff06bf833fc18fe0bff05bf82bfc14fe097f04d2563fc0ffe0820abbf81bfc0cfe05ff02bf813fc08fe03ff01bf80bfc04fe01ff00bf803fc00fe0,
    0x171219bf83cb83d561e290ed3074902206458f180093284383e1b9d0d8d85844d52e1a160a460ce2c732619100c4706030251031861bc505a243f06e50508420d00824001,
    0x1fff07bf83bfc12373e7f06ff820627afe0cff03cbcf1fc0d2d3bff05bf8184e630745119a46cc40a95fe0a7f04ff8000691fe077f01c5cd7fc0613347f017f8021264fe0,
    0x1ff107b803bb81cd80dea06b40339418c60be105b002b7814b809da04ac0235410a607d003a601b1c0b860542025e810dc07640600299700a9c0448019a008a0024400180,
    0x1fff07bf83bfc1cfe0dff06bf833fc18fe0bff05bf82bfc14fe09ff04bf823fc10fe07ff03bf81bfc0cfe05ff02bf813fc08fe03ff01bf80bfc04fe01ff00bf803fc00fe0,
    0x15024fa18be09a6029ec116519b801b6426dbc117f834e8586e2bb515598a8c4535e292c14558a0a44f4e2724104025a844c3e259b124a88e4042fe040931040861440002,
    0x1eff07c36f9fc132b2dff06bf833fc17fe071195bf81a3655fe0c05ed3f8040e6a1528ff0781421fc091327ff01c348832e509267f04807460a4bfe0003ba3f8020246fe0,
    0x1882564807a846afe0e1e1ecd8ee3c3a323182354707058721813ff058a0e840731a308033c50602c6e10327f03448561c2614c6051a0287e248208c2830a408fc1080020,
    0x1fff07bf80e3b3dfe0792b73f837fc1afe0300f348db3fc18fe0bff05bf82bfc0b216a7f04ff825fc11fe01988c3f8123acefe067f02bf80bfc04fe040cb0bf8000b41fe0,
    0x1fff07bf83bfc1cfe0dff06bf833fc18fe0bff05bf82bfc14fe09ff04bf823fc10fe07ff03bf81bfc0cfe05ff02bf813fc08fe03ff01bf80bfc04fe01ff00bf803fc00fe0,
    0x1fff07bf83bfc1cfe0dff06bf833fc18fe0bff05bf8020354fe09ff04bf823fc10fe07ff03bf81bfc0cfe05ff02bf813fc07fe037f017f809fc03fe017f0542fd062e0fe0,
    0x12ff07c39f2ad8a0ab17f02022f7341a960c4805e30383d16800abb050fb22659368092f041601ea40e4c06a100c1bd87c0b3a0f043a4c80e5c0626020e07401c22c000a0,
    0x1f8dbe45dec2af3117f508f674601efc991dc98ea34710e2d0d7605bddf468e22709792f8c55c5e9e2e4115928a816d2422303040e89405cc3224131aff0083c421220031,
    0x1ecd17ca9f9305b962d4a16648b120578e2f1855a30ab10548429c0149f0a2ec507227b61399084016d60262e12d5094a0494c242310403ce80463a229811098864440022,
    0x1fff07bf83bfc1cfe0dff06bf833fc18fe0bff05bf82bfc14fe09ff04bf823fc10fe07ff03bf81bfc0cfe05ff02bf813fc08fe03ff01bf80bfc04fe01ff00bf803fc00fe0,
    0x1fff07bf83bfc1cfe0dff06bf833fc18fe0bff05bf82bfc14fe09ff04bf823fc10fe07ff03bf81bfc0cfe05ff02bf80600800ec4ff023f80ffc06fe02ff013f805fc01fe0,
    0x1c7f05bf829fc0101cf958f89c7a4a33fe097f0708c63fc1b1d187f03ff834362efe06ff033f815fc0b1f94ff023f80ffc190f137f05c1c49fc150311ff00bf801fc05015,
    0x1f9767bf83a598c126700270ab3651930c248c7689b102dd924cc116104bae41961ec38310c3baa39941ac90c6445b20298f12c084734430a052b0ec5066181b0009c200c,
    0x1508db4b5fe639e2fce96e706636579a29cc93e60972eba7623ca10e4c7f243b911bc80ce3c5f1c2b8c13c595b9c470a1f8843f48ac1907c81b830bc104e041f000395573,
    0x19044fca037059a78c8034e5d330d9961adbb56558328b59150c98b6bd2b1c818d10d5866a7f81411a604d61e6785010498302d38d613f83a18050cc1006842338040000c,
    0x1690aa4654c12b8fe0a7f0718659fc0afe02ff07e177d03bd7bddbbe8ff834e7b96ddbb4ed99743fc1561d9acec90e62a3b049d7a1eb8ef566ba82fd393e88574806a005d,
    0x14032d8d8aa645e069fb56f5a378cda5fe0a1816d8b74c1b95ad99611d13b0a9b750d8256c8a0a24c4f2027226b5035471ac1c2319690a3562c431ed10b68443521c4008d,
    0x1787dfd54fca27d4f3703cf12cf6927a453ca198807707e773d3b1c9a487941b75353a179ccb4cc33d22938929c08cda426c1f320bf2c6cc623c81733889943cc20a60013,
    0x1f8d57862ba2d5a261c920f0528c01d8221b900d8786a21541c19875486862195018178b0b42a9c282c1215845241a94202804a387094304614220612015001076000100a,
    0x19ff07c95a5fc1e2368ff074859ffc0efe06ff0707db63accfe0d0db2ff83232c9fe047f0605d8dfc171562ff0584d89fc1511617f007f8281ad00b6504b1c1d8602c0fe0,
    0x168c52c5a85fc0e3cef9f378f1ba74c812ae1c307f8125ddb366d1a364c9b05cd72c6b15354a18e49d426699234889a240d01e678e3106b9830ca166308314398608c0fe0,
    0x1583b5496bed3c4056f33f759784127c63edb0f697f8206795dec2df5d67acafd455e9a9f0005e4a3d14fe826f3d279c8fcd43e620f28f79273c837e399f18b78a4bc30fe,
    0x1f8a3b842fa24fefe0dff063f82ffc16fe0aff0343ae9fc13fe06065f041e5fc1a0e75045c7f80c09790c787f03ff80e0ce502b2023aff813fc08fe017f007f80604e0fe0,
    0x1d05bd425fe477e21b409af47ef83b7b1bb883b900df2337817bb8add84ee82360017507b4c4c581f6b0db485dc844601a2e0df384d981eca0b6f091085e8c0eda022201b,
    0x1101568cafed9fe6afeb47f19bf6c9f962fc307dd7becb9f55afa2c7cd53e4a5f14ef8105bd2bdc8ded42f6207acebd46de932f41779cabcc45e51af20978c2bc209e000f,
    0x1f9dbf8e5fa6ee4fe0e1abeccdf462f92f7c14bdc9dec4af523771afaca7e842e921f1ff04c7de43ae615f88dbc065de2eed157608b9437c40be1fe0507ba025c003e7057,
    0x1fbf20ff829bd1e7c4ebd26de134ec9974417f061c92ee0966c4e03655a926d0926640ff0459101fc106247b0239791ab88cac85ad2296112a8884e43a5219110a4084308,
    0x1d14f78e47a6e3c351c9989016304fd62f1a1688c05368eb7415a9eacca4602bd1315708f34ad643e21fe0613abcce4e3aa5195486888457e2ba80b1303883f81607ca01e,
    0x1281204013a60ff04ce173bc2b8814de00cd963e8a9f250f826749655c91ec44e2086a8f3d071ce39531a790c3c459e028e314a7093b441d818eb0a700652819d1fc06047,
    0x1a0ba484d0ffc11114e09bf8f4fab77b59bd2ade546f09b774bbb24dbc3d181a9547b505a4d16d0128507481fd8c151c7b6d3bb59cda4cec206862bb212dfc07043f60014,
    0x1f0a7fca0324c09fe04022cc702e8484fe0b20254e1286881fe0918244b90c04b02a4794208015c489d12f68f27043d8389b0cf58b2682bd4248710428520c193009e0004,
    0x127f00ff805fc1ba590ff003f83d12bd875e42aea0d7302b87f5bbdad9dd6ae6b46f59b4ac98d62bab05b57abab94d7e5fad515626aad2d5472a9355419a9cb54c12a5035,
    0x1e1137d927cbd3a206eac4e479b69d371c6aa34d069a079388aa71a4d9faa6f54c309938545a294552f5aa3124948a4835281a26a55043a4e28cb38a18830839926940069,
    0x1e14b7bf83e12ad05518cdec9d9012e6077d11b0815f242d81f6b8eb002ed427f61b6081a942fea32d417698ab77f82426d1116807b3c359c16cc096583b24158e06c4016,
    0x1e890fbf8382036120f8934c40344c8c02eb96650ab244d9124c7916387b1639891ac38c6185b361c390c12886103b15fc030acc050d42044211006100263410500421001,
    0x19a6efcafa497be1fe8a3ec1177a37cf43d69feb0f75677bc17e51cea4df506bb6311d89f1ccf6a562631dd07f509c721bc52dd214edc2fb1fc031fd7088885f4217a005d,
    0x167f02ff813fc08fe02ff00ff803fc1e52eea87713bb499d94aec2475d13ac81d53eea1e74ceba471c0fe089a740bbb7394f2ae7127347b9431df246388718238809c200e,
    0x1cb6d63f83e4fde25eaff0748f9ffc1c21ed8ff6877ac37d419e98bf48579dfc1113e808f33f81a1fcb0debb5d242f9013cafe0383f1bf809fc0505e17f00c0f81fc0101e,
    0x1f853bf22000dfefe0ab726d3b3299974aca246491b22898108b8216350338600c3ecd17060b016798a3ac9a9224e33a00f624041b638680e6985180319610c30628022ec,
    0x1f90fe0947c3ffd1df905db426f833eb07b482dd876aa375419a301dcc5eb627fa07f41ecbc4eae2e3905f708d303e941b510f1385d400fca134407a102d040e86036001a,
    0x1f947e3f83c4df1fe067f04c18ba49fc22fd907a7f8343df91cfb8d79bf82c31f516fa0a7c84bde21e4fe06877ac33c5fc0a0af801107f801fc0e00240479c1bca09e302f,
    0x197f075e7f8effb75f37f00ff834e7f971fc37f8bf82edbf66bfab4ffc55e8cff365f8b1fc187debfee5bf6acfb14ffc02eb4df523f840ed283e83bf39bf94afc1fc041df,
    0x1a0b64ff825fc11fe0787643f81dfc0d0ccfed22c2b19fc1ed64ee922423399c8afe030366f31080988fe0d6221ff80bfc0202ccdf262e907fc17b64b59207f82b5c80fe0,
    0x1f89a78451c0f1007ce48a8ff83a1e9a8f5c44ada0d761a8d05cabfacde564eab16b5c85a3d75589aab475501e2016126ea6038280c106d6e12820d5380e041d680e80015,
    0x191c3fc723c351d188a87190126268f0307e0b438291610830297963ec521a50f4083d0943099f2210a207c0742071d208970c8b016180926046100938540819ca1100027,
    0x1dff0702616677afe0e86e63f82ffc16fe0aff053f827fc12fe08ff0780d21fc0ffe077f07c2ff20fe20db6ff033f815fc09fe047f01ff80dfc05fe027f00ff803fc00fe0,
    0x13844f2a131fc1e480f91674f02dfc14fe0dd226a89333c97944ac524df923fc127247ff041991bfc0bfe02014b959188c89fe051c220b10a4086fe018a2001905fc01fe0,
    0x1f91eb3f8322bbea3557f0767d7936bb975d4aae22d47fc176f5b33ad58d68b6a0fe09aaac94d6096af455690cb8fd5672a82d5395a98a54a46a41f548cc885d620ba1115,
    0x16034f3f837fc1afe0cff05bf82bfc14fe09ff047f81ffc1814e4993483356354714a77f023f83e1844fe029430bf8063cd70ce6862c02b7c0841fe03012a82341fc1d002,
    0x1f05cc475fe27e727bc05e5c2719fc0b117a85ef0264c16ca0f7703e2017060ec2036d83c900f0bfc00fe0a04ed81642039d075d02ae40d660fb2039780cc0175a07a901d,
    0x1f8174d402c55914c0ea63f803b894fb487d233e511f080f73e7a9d3d0e1e468f03077973b8a9da4cec2475913a879d238e818718131c51cc24e50e720638819c208e0007,
    0x180deb426940f4105afa8b793db89adb4b6d24b651db08ad7436b20b54fda87ad33b691cb44dd9e6ace336618b2cbd925add03e415b1ca58c4ec5256211b0c85843ec0156,
    0x1fff07bf83bfc1cfe0dff06bf833fc18fe0bff05bf82bfc14fe09ff04bf823fc0b0ae87f03ff81dfc0dfe067f02bf813fc08fe03ff01bf80bfc04fe01ff00bf803fc00fe0,
    0x1f7f077f837fc1afe0ca5b5bf829fc12fe0c22b43f81bfc0cfe0a9fb7c0cd5fc0015b99db44d591fc0f31637f05c0ff807ce2f627f02ca5924ec71f61ff00bf80a3ac1fe0,
    0x1d2306c833274183609ce242492e580e88463e229c12c440920843121d512a341e527ea83d0600c888102b29b2483808548f0c018f247f81a080212458107139fe01e0044,
    0x1fbe8f9e47aea3c711db68e9ac72ce38651baf8d9646aaa344f19a48c914627e303b179b8b8bc5a522c2515918a88452362817138a8984c4a1e240d11858881c420a20011,
    0x1dff06bf83eacf8fe0b7f057f827fc1e50770474bf823fc1d4c787f03ff83890edfe067f06511c6016bfe057f05cf9e878e102a003327f80ffc0814737f013f80a1ce2fe0,
    0x1fff07bf83bfc1cfe0dff06bf833fc18fe0b7f057f827fc12fe08ff043f81dfc0dfe067f02ff815fc09fe0babba3f80ffc1453737f017f809fc03fe07a7b8bf803fc00fe0,
    0x1fff07bf83bfc1cfe0dff06bf833fc18fe0bff05bf82bfc14fe09ff04bf823fc10fe07ff03bf81bfc0cfe05ff02bf813fc08fe03ff01bf80bfc04fe01ff00bf803fc00fe0,
    0x1f7f077f839fc1bfe0d7f067f831fc17fe0b7f057f829fc13fe08ff043f83ea32ffe077f037f819fc1239d5ff02bf813fc08fe03ff01bf80bfc04fe01ff00bf803fc00fe0,
    0x1fa20f9007a783c381d1a0e4c04e48782c1d8d6dc986c4835221a1009878e63c251631881c8706230220c378a090221c202808d6860c0031810210835830a808400869001,
    0x1eff06bf8300380014bff05bf83e967e473aff0710cf67e74fe097f064f4e1fc1337389a9b8bcd65a692933129bff81bfc051f367f01064d5fc0313347f00834cffc01033,
    0x1fcd07a603b2c1c940dc906a40331c188c0bc50562029081382093f045f02ca990760739035b818d00f6045b00297812b4085603a9019380a900444019e008d8025000020,
    0x1fff07bf83bfc1cfe0dff06bf833fc18fe0bff05bf82bfc14fe09ff04bf823fc10fe07ff03bf81bfc0cfe05ff02bf813fc08fe03ff01bf80bfc04fe01ff00bf803fc00fe0,
    0x1dff06bf83ce45c6a2cb1163f82cb854562928141289c845f10d69f15ff8167055fe09ff024c8ba19a72828ff0148088384ffe018b1083899fc0afe047f004188c0520022,
    0x1eae97c5778b65e13dd2b96554b0a65b11dba79592ca61fb5472a21944f49e6a4e2f2906eb09ca017a001357f03427560fa9252302ea0848e324301d2899102c840a41012,
    0x181001812a4798100af924389b3c391d341509070c856359b301d170e0b06e5436281a930d0906644311e1388608019e34240a068b0b048521c390e4000020284a0c23021,
    0x1fff07bf83bfc1cfe0dff0042775fc19fe0c7f05ff82dfc15fe0a7f04ff825fc11fe087f03ff81dfc0dfe067f02ff815fc09fe047f01ff80dfc05fe027f00ff805fc00fe0,
    0x1fff07bf83bfc1cfe0dff06bf833fc18fe0bff05bf82bfc14fe09ff04bf823fc10fe07ff03bf81bfc0cfe05ff02bf813fc08fe03ff01bf80bfc04fe01ff00bf803fc00fe0,
    0x1fff07bf83bfc1cfe0dff06bf833fc18fe0bff05bf82bfc14fe09ff04bf81612d1fe087f03ff81dfc0dfe067f02bf813fc08fe03ff01bf80bfc04fe01ff00bf803fc00fe0,
    0x1f7f077f839fc1bfe0d7f067f831fc17fe0b7f057f81405f4fe09ff04bf83e3111fe087f03ff81dfc0dfe067f02ff813fc08fe03ff01bf80bfc04fe01ff00bf803fc00fe0,
    0x11ff0781cbe03e0051eb582c3678ce01fe0db28698432ba18590baa8593c2a9a144909a2848fc227a1039079b838cc1a620c2d0515824941042071d030c81454081e02070,
    0x1f5417690b9405b9e2d4d16660b12857922b4715630a9105382293e145e0a0e84f6c27321357898b04b522526125189080473a231a114a88848431421091043080145f086,
    0x1fff07bf83bfc1cfe0dff06bf833fc18fe0bff05bf82bfc14fe09ff04bf823fc10fe07ff03bf81bfc0cfe05ff02bf813fc08fe03ff01bf80bfc04fe01ff00bf803fc00fe0,
    0x1f7f077f83e149cfe0dff06bf833fc101ecc7f02c5b2ffc040ec08145bf82bfc14fe09ff04bf823fc0ffe077f037f819fc0208c57f027f811fc07fe037f017f807fc00fe0,
    0x1403c14160ffc04fe0fa2abcd67c6eae2b9d38e65bf184b376dc92fe07f816432a199100c455f1a029047ce8d8f06452279b151c088982f2c162305ca838d00c400393011,
    0x1f9c1b42b3c686b08ce981f0b0d00d9b2a3b247e498f0447720391d7d470e8307032f98a1c448f5fc0c2af30260c0b1e1c6a28f7051a418ce41e51cf202180030229e2023,
    0x1d81a084dc21aff49cf23e75173883993dcc1ce5cd72c67952fca15e4c9f244b9121c80fe3c771c378d19c60be2c57002fea13cd00a2447101f870dc305e1427080f8305c,
    0x108049ff81a41bf2842ff02c735e719e520ea7030c238941b44050c6e8f8327018340b97024536c4c0810d3066d48028380408d98c00ff8242011080802008134001ae000,
    0x1fff07bf83bfc1cfe0dff06bf833fc18fe0bff05bf82bfc14fe09ff0001665fc11fe087f03ff81dfc0dfe067f02ff815fc09fe047f01ff80dfc05fe027f00ff805fc01fe0,
    0x1fb1139a3bcbc5d5a2e2c16d509448da4e232476528a085b8462ba213cfb6245563e261d6d4e8966da12eea1a14cb8a4504832d69011cbb4855a328d48c514388025a2022,
    0x160b927f83e6fbe35de99ef0c7765fba2ddc95ed824f053ab13250795c9f501a5525d208f9c2c8c0a5423d990ec87f623bb01bd185f8427de33a20bb70beb4574a0240039,
    0x1582703f81005c306a10257cd90801de2e408057520f88c7b423d1f1e4e8f07077343b181d4b0e850732639111c470e0346f1637091b440d8186a0a348419c18cc0465003,
    0x1aff04bf83e3f5e1da87f03bf81bfc1d1bae0cd5025762f4cfe057f027f8342b58056c89d5c468dfc160fa986d442e9e134b07a402d0ff80e06c503a17f0100581fc0101a,
    0x198d57eabbd4dc7fe0ed177273b72dda90ecc5762139c21577aeb3775583a8b5d254e8a77411396194f3ce37f034db9861c922e40f714638821ca06a17f003f80611c104e,
    0x1fb5f4406bcd3dd67ee32f48a5f6c7da61e78ebe57fb0b3d751e70bbd937985b690b7aa4f1c76c5fc08097a22f4ce7882365077819f34af963fca17e307f0c1f8007c1017,
    0x107f02411e47d9f0cbe8559009e0699b08b7986714014691a4c069566518184d8b24c41165ce80e39851ac30e458b0300d6e04b18a6548804219e104a0904c28020d91020,
    0x1486ffc0ecdfc1e197514ef45dce03fc1572ff020977626f91b2c0c96845ec2a570f798995435e41e510d2a05bb82ca012ed0520ff03c1dd806430bd202bac048402e003d,
    0x1fb37f993fac5fb60fd2f7e573eeb5f558f9ab78ff80e4ddc3029287e0b0ac48542228267b90bc5fc111e278b134f3d82441fe050512cd3d25de806228c7903bcc004000f,
    0x1fb5ff5a7f6cff965fbb0ffbf82abffc3fbd7f05bf826b7edfe092cfabf822afe6fe02ff03d57dca7ec51fc1ddd0dec7fc0b4ff817ba537c5fc0845f0ff01ce7c1fc041df,
    0x1daf22ff83ee59a5c427f079c332b482fe0eb6661612eac96524aa8251392698924a48a4241191e8880fe0721234f9186c9c6ac51422489103c8718430a21431061081004,
    0x1f988f0ad36529a274c12a5c8d3c4bbd2d1b10a649c683e9523198ea446d243e2e19480c8b05d142a8f151489a1c450a1e8d111186a2c3c4416880b1084a000d0c0a24011,
    0x1d8e3a028be1c9a1a7c9035c61f03cd4167f0624c51e024f61c66883f429242ccc0e75063bc51b810821aa70932429ea39c508788321019c0044b0e630221c298608c1024,
    0x1f8ea786d2c96fd194a24bcd1df62e91457d0aa48d4e0666f437720be04d2e228d3d761cbacc4d25a6a357cff01c94ea1e851f3301c1064c00688337197b8806380781277,
    0x1f132f4917844bb20577f033f8323cb71c5b0d2abf82830b216588a2c049741809fe0c0403c415a1cab0c54052fc034ffc0608520328c114bfc1504017f00409660000fe0,
    0x1fb6af9ad74a327fe027f0653e45fc1d6950ff0719d76cab7635ab0acd7d64bab15b5c26cc16541fc0f57572aab54d6c972c4d55a3aa8fd5262a81f5a24c984d4a1ea3075,
    0x128d4fd2095fc1e462ea217108b6805a3e220b4e4f0b07457382b1b154d0a864533021852c8b8a258502a21074bca09c4c4d22260f12c708215291820024a0508e20460c2,
    0x1310dec37fe2bbe11de87eb84e5a232c0f9586ce42fd41728099b83fe85d8e0f38156b09b5445a81ec3053986b482da212c1033003dc01db80faf056282c900e5206c2019,
    0x1202779ba7ad13c629dae4d10319fc1a56999e644db1c6599529c264dd1a56618202eb214a4ab0e499540991f4987b2079251ac18a63cea42198d389f81328da400d88fe0,
    0x1b7f07d3f70434517ef26ef52f50335c49dda3e905eb48bb943daa0ed0ff667ba309e89dec91e440fcf39d71bec1165a6ba10baba38b0cf5663a003a517ea4b74e57a629d,
    0x1a43575b38bfc04fe094053dfab8d5db68e73b50ff834cdcc70acb277c99b0c1ca66abae707f82cadd552e9a874533a091cd42ef12303f81679c936e41971cab8c21c204e,
    0x1b14f486581fc1e2b3a13f4c97a247cf21ed939e48cea834c1deb909b86cd637df0d480bfa86788226915e1879a047ba168d13f308f9c1f8a07c20ffe04a681d300a8101f,
    0x1fa27f903f6d19a66c99e7e193226def32fbb1630bbd455e924f3907f1aa32c5165ecaae6187bda95145ac20c7f401c629f258c4204043bc4096004f82a614b21c918b42c,
    0x1d84e389f7e2b7807c693ce407fc1f7d698511ecc2ed243a81fd38eef18e34b71751828bed92e0827a30fda81e5106220386fe0817c3c9e041ba109d60fc4826c00bab05b,
    0x1c9f7d0ebf4405236f8977fc7170345028f07f058589e49f51229871307bfc30bd165e0a2ec495635f70e53831205bc6084d1ae2887b8194819e208f5022a4094201e6005,
    0x127f07cffd626e8097ab1d8ff83c7be2fe00ff074eff873fb37f07f068d7e8bb7933fc18fdcbfec5bf32bf914fc49fe04bef23f710fb47fd83bea1bf319da467ca0be7017,
    0x1fa0617f809fc1e3ec17f072193a7994748dc0249ba347181fe0cbd25de12ce8957049b62459920c88f5c472c2355118a08b4c45232250910749832c399218b90630800c4,
    0x1e82e7d4451fc1e4f1e01e1bf834a699058aa1a48ed3682b0354c1eadced6c72b437599aac4cd5e5eae2d51ff0348d583eab1d550daa45d4e26a5115101a103d4212a0015,
    0x1eff07c6b3c319816ce7f02410f7fc1614cd7f0504b33fc1210cbff057f8201d8702370664ff823fc0ffe0605637f80c0d8bfe020262bf811fc02fe018161400c20180fe0,
    0x1f21a43f83a7e8ffe0e1da6cdd1bfc1a31467f02bf8325a89fe03ff05ca50dfc04fe01ff00bf83e6301fe007f0149dd02bf5234c149d894e8467321390d9c45cdc1a6b033,
    0x1f9d674d32a619e705896671b15e559b6a5d332e5915c4d9860561165d795441965a540f61c6b28b0a616c9aa2945324a0a412c82728c3b1a94a20405a42841b1288a002c,
    0x1fafef9777ab7bc59d0ff06d5f74abb953dc27edd376c97b549da21ecd07647fb03dd79deb8e75a6bb1435619eacbf5457a929d412e9c874c3ba51bd20be8c4f440fa003d,
    0x1b896d84359fc0600ea876fc527c253d10950652ff813fc1c0e947f01ff836193a0a92ff0503349fc120adc844c02345fc180699824c40a5c0da10066826bc0241fc0300d,
    0x1d89cac07721b360b9f97c78b63a571c298d13c60962e471221888fc407607fc1509978dc3866182f0a158489c2046280b270f8306c142e081302078981c83f8020b0d019,
    0x129440c28040c1f06af19374c1b85cdb2c6d15364a1b04cd7246b113540ba840d31e688e33c699c30cd16660a34bf81624d0fe008b428418008890e640631c298c10c4066,
    0x1ea58d4fd78923b451d218fc7eb282383d1b9d8d8dc5862b43319978c8b45456b129181389c855e462e1d168d89065562a221554888a0347c3b460b1086a940c400ea3011,
    0x1fff07bf83bfc1cfe0dff06bf833fc18fe0bff05bf82bfc14fe09ff04bf823fc10fe07ff03bf81bfc0cfe05ff02bf813fc08fe03ff01bf809fc03fe017f007f801fc0518a,
    0x1c1fb7cc4e5fc163b6f159c7f81ffc0823730dbf47cea6ed41fa998b37f819fc102d6714b7064d3fc0b236d8a9a87587fc1a0f338db1455b20e64116106b5c14c20760096,
    0x1e913fd003440fe3a0c0f3d871f8701b320c9705469e830f32c0bff044a8202cef1471807b4901640125687093b041d21cea1603063a0480a14e408710338409ce1c00007,
    0x1c12b7c0efc3af7236894a746dec3ecf234a8eb7065da368503fa0db6c5de42e3311a70ab305d3426eb136408a2845b222e90f6306a1c35a00ee2094184b04158002c4037,
    0x121635102b081753cb0ff044e2964d5c547da93e939de65794a7ba33d911e680f23e781c3b8d9da60ec2c748472899d044e61a7f8411449ce295e022e8010c29c40ce0027,
    0x1e7f06ff835fc18fe0bff05bf82bfc1f497f20bd3f83a76f2fe08ff04cc5e1fc0ffe06ff033f817fc0afe0715ba7f8322b64157107ba3f80ffc0005737f017f807fc01fe0,
)
RELAYS = (
    0x1f87c1a23a1fb381f3361eb341e336cc85ebc074cb86c1cb2a1c3281bb261b3241ab1888878d8076dd35e1cb66fd8dc1d0eed83f03686e3ab5cf58541d96c39b58f48745a8f259354f40705b9663834e143ea590cc1a1603734ef78e25285c379481634cf68dc560d8558d4d2bc6148c8838d0d23c4130d05084ad1bc833940108c6d13c4a010a500c250340f00805,
    0x1ff3dcef37ccf2fca70981cc34,
    0x1f93a4e1364d1324c12e4b12a4a124489204791a4591447316c3112c33044,
    0x7f4f53b4dd354cd314b52949d2548d2147d1d4650f42d0941d0540d3d1f7014,
    0x722b8aa2b1642995e2689a55896540945288c519445,
    0x779f77d3ef7b3e7793df75ddcf9cd7353c771cc4ff5b73d5af2f3ed67cdd65cd5693bf7358f2f5b76d5af6b594dfca76758ce7d976357cd9c876155f1fd7d5d37751b7557d4f1757e0724551d3f4dd3d5732f53327513270d31745524c3d14c5c0dc330f01504c1c,
    0x1f97a5e17e9d9745f27c0c97a9e8305e02e5da76081740aa5c5c81a5c0209b8145b01c931589a828052485980c92a6401962022600115e0680250a5ad500050250033480,
    0x1ef75dcf455,
    0x11b8c6,
    0x7fef7b9edfb5ecfb1ebfadeafa9e9fa5e8f9fe7799e5f93e478fe378be2787e17adbaee9b9ec1e7eddb66d5b3ecbb26c5b0ec1b,
    0x76ae8f83d8f43c8f03b8ec3c26a3f0683e8663b26439a76188f4180e49c05e3b8629a85c3a05a3985837a6418856380543785236a5c140ce5684e3605c630d69585294b4a349928484ad20ce618ce11b4e8219244106821081190081842403c0400c01,
    0x73abebf6f5bb6e5b76d5b36c5af6b5a969da568da16cf9f675b1e6d996af9569f93645a3e3d9fe778d69c57e4f8b6745353f8be6c4d5255514c4751d8f1374b11f47117431,
    0x1f3fafe3faee3b6ed3b2ee8b0ebbb82aba8ed8a4ed0a0e7bb0273ac26b98e5ba825392e9890e808ee339c22b88e6082b1382e4880e,
    0x5d796dbb5ed3b36c7b,
    0x7e7f1fa7e1f67c9f07b9ec7a9e87fbe6791fcf89faf79f8f71f2f69d87bbe8f59e4c51e2c49e0c41dec39dac631c031d4c5810c29d203810f21ca02bc6019c201302703007,
    0x1ee378bff58a7f387ff18be2d8ae278450d4861d86e178941d74e2107c1b03617764098541371623d4c0793c0d73417d574b706430144570ec17,
    0x1d9f27b9e8791e2781da761d6751d2741ce731c8711ee6a1be191a267992b71966498e631bc1fb8a621ba119bcee1006e0762,
    0x176118360b8,
    0x7e8f23a8e2368d2328c22e83a0a8133e4033c4,
    0x7981f05c073f4,
    0x1d0b22c0ae2b0a8290a02789c260942388a2188e9108022258d,
    0x67695a7c8da167da1c6d9965d9564d9163d8d6fd4b6fc096f43b0e41b91db70d413915bf49ce53cc2130d9f3bc016ac1b3,
    0x1624881a028,
    0x1f6799de6d9965f9,
    0x46e6182e,
    0x1fdb54c51fe6f97ef593eed91ee5a14dd9d4d5b36bd9ba5683a5d154,
    0x1f1ba6e1b46c9b06cb6e6b36c6a9a8699a46b0626a868181a6179a41885c6631e1699815a546584e9434e648660790c6380860ac46,
    0x1fdbd6edb96ddb56b5a969da568da166d9764d9163d8b61d836,
    0x7c5e9785fbf65d17cf01f050afaf,
    0x7f7f5fb7fff97cfedfdde7f87dbf67cffd5f3785cbf,
    0x1fbfe7f1fa7e1f67d1f27b9ec7a9e8791de769d6751d0739ca719c6b,
    0x7b7e5f77d5f37c5ef7b5eb7a5e778de177def075db7ac3f165fd1ec577e477155f51cc537c46f145ed13deb15e11ea46712de513e631845b1644975c49d4441a554f12c4582d452074310c811,
    0x783d0f03b1be1c86c3f9767e2e6170ca3a1063b0a62791a459124310841106c,
    0x1851b4550f4,
    0x1b11cc,
    0x7b4c56f57551525435,
    0x1e8b82d8b22c0aa2809a240822,
    0x7d0ec390cc2d2b4290aca70a4b13fd5bd940fa8593dbcf3547dd28cd30440dd34235274bc,
    0x645815454354932429,
    0x1ad6959d6156d535,
    0x62af9bc6,
    0x7fef7bbee7b7ed7b3ec7afeb7abe57e9e8795e3f81aed87e,
    0x1fbbceebb8edbb4ecbbcbc3aeeb3aaea3a6e93a2e839ee4058e53b05630ce2bae5599c798c6e80dc3,
    0x15f89ee583a,
    0x7efebf8fd3f2f52d0b3bc8f1bfe7,
    0x1d7ebf8fd5b27c1f,
    0x44b,
    0x7d0fffdfeff9fdff5fcfdbc5f31fbfedfafe9f9fe5f8fe1f7fdbffd59f57ff9fd11fcd0ffbd81e,
    0x1fb3cceb36cd332cc32ecabeccab26c9322c831ec731ac5b14cc9d2c9be62432223b3c1d0cccbb6cda1fa1c8eadc0e8d89e4d8b6e3835edd39cdb0cac6b58da8e835b4c6534ed90de32b4461b5a358c0d,
    0x47c,
    0x12b02c,
    0x798a71389723c7f19c5711c2f07c0f01c,
    0x6498250d3344d,
    0x7ddef79dd773dc77f3bf7d3b77b3af793a7773d4e7dccf1397799bce3d876d37f6b3775bda4d9d5f673df253966fc8cebc84d5d7cd3d4763c74cfd6f1b3671935cd535e0fc4ccbc44cf334c5c2cc931ccdd14c332f413,
    0x1f27e52a385,
    0x1c57fd765bd0f655,
    0x1fabcaeab8afbaaa9aa2a6a96a4a90a2282a,
    0x4d6,
    0x7eee374dcb6eda35aa5a8ed4286d137e12304cf93c112fa1,
    0x79ddf6bad773dc76fdb76bda767d9763d875fd7759d5f53d3f49d,
    0x5cb6ad8bfbd4b19ccb2afaf,
    0x1fefdbeef9bdef3bc6efbb6e9b66d7b4ecfb36cbb1ec5b,
    0x1d2face336cd332cc32ecb320bab28c9b24c8b20c731aca818c5b280530cc98027,
    0x7ffe71587e559ad91d3745dfcbdf,
    0x1f87c1e8781d8741c8701b86a1e32819876c90621cb2ec806cc706ac6866ce2d818b20ccad61505ec485cc405ac3858c3056c6aca1530814b10b91c61431e5106073b1e7330ab69c2161d6741e02810e729c6c59067508472100c2084409c0e00402,
    0x754cd2f4ecfbbe4f73e6f5395333d6f138d2f3d72fbb4eb3b6e9385273af29b94e33972137ce1c74db386d9354e3f7ed337fd1366cf36fcd367cb34d11f24cdf3505f14c7417014,
    0x169164410c419004,
    0x7f4f53b4f7394ef334e7314df2f4b535cad33ca52fc9d254af234851f4751b46517455134450f4350b42507436058,
    0x7cdf2b8ddb7aad372de2b0dbb76ab368dd2a6dcaa4d8370a6b56dba92db2aaa92a0a7a9aa52ba2e0b62d0b02b8ac2a8a82989a588965789456892560905488c5408852884518805,
    0x759ce719b669996a1a8f77cafb1cbf2dca727c8f19e7f1dc579576ed176f0fe6717c5709e4f05e3f0bc2703e1dc3c0781305c1c,
    0x7e0817c0797a06178059740417203970021465b82c0a8280982402a620225e0015c0125a00a5805800950120,
    0x1fd7d5ed795dd755cd715bd6b5a567595635855f5755b5765b966579565193e4b926459,
    0x1f3baee3b6ed3b2ec3aeeb3a8e9ba2e7b9ce6b98e5b94e4b90e3b8ce2396641886,
    0x71fbff1ab7ebfa7d1a269df5fd5f4fcff0e87ff4c3f0681f,
    0x1f9bc3f1ba3e9b83d8f86d0f23d9b03b8f46b0ea3c9a83a2b0698e4a7aa43b9a2372a03f058ab19e3e05c5529c3c86a668ec1a1983a064658e4189943804c548e0670503685e638d61698c3485860948f28ce139c83498a141881120a61846310c861042300c66084260042d,
    0x1fdbd6edb96ddb56cdbb1e4716d4731c46f6bc6d6b46b6ac696a46bac7a31b7a76af9f185a7e7461e6d9de645315f9115d95e3f8f1558be2c49e3585e2441e1d85105831,
    0x1ebf4fc3ecfabe8f83def73d8f4bccf2bc8f13c4b0bc0f,
    0x7dfeff9fdfffbd7f3ff6d379ee5b87d7b27cf7,
    0x1f9fc7e9f67d1f27b9ea799f8fdbe47d3e07cbec4bbecf71e6f93da79120f73d67811af49d8f6114453ce043ce4300a433ca7280242bc6021c401bc2013c0003c07,
    0x1fdfb7ddf37aeef7ade9b9de578ddf775d975dd37fc3fff4117e43dfdc330efcf79c23036e7f7417077d302f0d0478d92c097378900509f1c09517c501d4350641f0c011,
    0x688f93c4923a4e1367d1f07b9dedb1ea7a1e4792e07f0783e8743e05c7c8f6159e86d0666b8f2189b0171966b86c3498aab04e6a8ea131a8129a610a866a0e41cb82698e2101a0188dc1,
    0x777c5f38ade37,
    0x1,
    0x7f8fe7d9ee799d6719be6598e6197e5d9665594e5193e4d92e49916439e501c,
    0x7e5,
    0x1fdbd6edb96ddb56cdab6a5a768d9f6759b665976559363d8d675fd455d3745cf7ec3902df7025f101dc57b4037ac017a4270,
    0x7e9f27a9e2769d2729c26698a5e9,
    0x7f5de7d5ed739b66b9e56999e5b9,
    0x1fa8861184e,
    0x1febdaccf132dad39ce7b94e3374c76159b364d73,
    0x7a6e1b66d1b26f8706f06e6e8781b1b61a9a66d0626c8606c06e169a8bb0566a862b49a8141b839870339a415aec3a0da188ea469caa78ceb60cc62854950fef40c46104c3,
    0x6d6a5a768d9f6a69965d956645365c516545113c57e3d8d12d8b1,
    0x7a2e0be7d8bc7d0a67c8b0289ee279ec261ea251e8298927908e731e228088778867709a209d825092238807308a2,
    0x1fef37,
    0x70bc9eaba1fe091fc07afa089f80d8207c81e7c02e061ea059e8041e60880a778087700474808010027,
    0x1fdfd7edf97ddf57cdf17bded79de578de177ddd76dd9755d3785b3b6d8d615b75cd6d1bd4b70e836,
    0x7e4f13a4f9744fbba5c12a5f3a25797ed717ea61545417ca397eb314a5217cf19741fb301096a101661,
    0x7b4e51bc,
    0x1f93c4c12c4a1244811c4610883108419024,
    0x1df35c,
    0x1,
    0x1fd7d5ed795dd755cd7f8c56f5b56b5bcbfca5675956157d5d5f71b5657f05d7b055535cc115ac0f5940d52d610255f01d5b05c17b4429e154d005490,
    0x1b96c5a968591605715a532465,
    0x575,
    0x4caa982a,
    0x71e3f89e,
    0x7e1f07a1e0761d0721c06e1b06a1a066190621805e17054d6874360561c0d21b0d01a8ce198cc14012738c63000c5,
    0x1,
    0x52f23c67,
    0x7dfeff9fdff5fbfebfa7e1f7fc9f2dc5f,
    0x1,
    0x6508417087d30f4a5edc8f0ccaf22c1fe7489077914170921c83c4f91e2f8710c43e,
    0x1db34ccb30cbb2c5b32aca326c9322c831ec733e36b246f0f836314bd8d89c8e6388d4c719a34b163430cb598ec50ccc40ce638cac1886c108410a02c,
    0x1e737cd731cbf2dca727c8f1dc6715c4f0fc2f07c1703c460b807058,
    0x1fb3cceb38c8b0cc0b204,
    0x7fcf73bcdf35cc72fcaf3feefb9ed7b1e07314,
    0x1f37ade376dcb6edb368d9362d835ed6b56d434cd2346d0b429,
    0x7fdf77bde777dbf6bd9f65d8f61d7f5dd6f7f0f419decb925f772d4b3257712bca54b49f8a493d9ca5276232849987c978475d26c95894d72375322f512348361f4192c872,
    0x7efd93cfebf8fdbfe5bbfa51b50473d4f4bccf,
    0x7f5f57759d655855b55d4d506475,
    0x11a84afb82a,
    0x1febdaeeb9adeb5aceafab6a7a8e9fa5e91a2e83a,
    0x1fbbce8a72cc32cc9a929931ec731ca5b16a3b3e35286cf0fa3,
    0x65ed771db76bda767d9763d875fd4f63a,
    0x7ebeaf6bc2dcb51faf,
    0x1feff7,
    0x76cd32eca326c831ac6314c4b0ac23120380a0,
    0x1b729c9f23c7f1dce6dbcc6d9ca6d5c473f21f19af4b100f2d0a4270ec8fa943928c3725fc9ad49d01651fccaf25c0ff,
)


def unpack(number, bits):
    values = []
    while number > 1:
        values.append(number & ((1 << bits) - 1))
        number >>= bits
    return values


def kernel(aff, words, s_out, deg_out, table, block, mid, arrived, far_words, mask_rows, far_mask,
           col_sums, row_sums, row_shares, col_shares, near, far,
           load_sem, word_sem, leg_send, leg_recv, hop_send, final_sem,
           row_send, row_recv, col_send, col_recv, pair_sem, out_sem):
    row = lax.axis_index("row")
    col = lax.axis_index("col")
    me = row * SIDE + col
    partner = col * SIDE + row
    y, low, core = row // 4, (row // 2) % 2, row % 2
    high, x = col // 4, col % 4
    on_diagonal = row == col
    size = block.shape[0]
    chunk = size // CHUNKS
    groups = size // TILE

    def rows(n):
        return pl.ds(pl.multiple_of(n * chunk, chunk), chunk)

    def group(n):
        return pl.ds(pl.multiple_of(n * TILE, TILE), TILE)

    def place(cx, cy, cc):
        return (cy * 4 + low * 2 + cc) * SIDE + high * 4 + cx

    def mirror(device):
        return (device % SIDE) * SIDE + device // SIDE

    def to_partner(src, dst, sems):
        @pl.when(on_diagonal)
        def _():
            pltpu.make_async_copy(src, dst, sems.at[1]).start()

        @pl.when(jnp.logical_not(on_diagonal))
        def _():
            pltpu.make_async_remote_copy(
                src, dst, sems.at[0], sems.at[1], device_id=partner, device_id_type=LOGICAL
            ).start()

    def wait(ref, sem):
        pltpu.make_async_copy(ref, ref, sem).wait()

    def load(n):
        return pltpu.make_async_copy(aff.at[group(n)], block.at[group(n)], load_sem.at[n])

    to_partner(words, far_words, word_sem)

    kind = (((high % 2) * 4 + (y + 4 - high) % 4) * 4 + x) * 4 + low * 2 + core
    for outer in range(16):
        @pl.when(kind // 8 == outer)
        def _():
            for inner in range(8):
                @pl.when(kind % 8 == inner)
                def _():
                    sends = unpack(SENDS[outer * 8 + inner], 17)
                    relays = unpack(RELAYS[outer * 8 + inner], 10)
                    for n, value in enumerate(sends):
                        table[n] = value
                    table[CHUNKS] = len(relays)
                    for n, value in enumerate(relays):
                        table[CHUNKS + 1 + n] = value

    relayed = table[CHUNKS]

    def leg(n, carry):
        entry = table[n]
        relay = place(entry & 3, (y + ((entry >> 2) & 3)) % 4, (entry >> 4) & 1)
        slot = (entry >> 5) & 127
        number = entry >> 12

        @pl.when(slot == DIRECT)
        def _():
            pltpu.make_async_remote_copy(
                aff.at[rows(number)], arrived.at[rows(number)], leg_send.at[n], final_sem.at[number // 4],
                device_id=partner, device_id_type=LOGICAL,
            ).start()

        @pl.when(slot != DIRECT)
        def _():
            pltpu.make_async_remote_copy(
                aff.at[rows(number)], mid.at[rows(slot)], leg_send.at[n], leg_recv.at[slot],
                device_id=relay, device_id_type=LOGICAL,
            ).start()

        return carry

    def legs(first, last):
        @pl.when(jnp.logical_not(on_diagonal))
        def _():
            lax.fori_loop(first, last, leg, 0)

    def hop(n, carry):
        @pl.when(n < relayed)
        def _():
            entry = table[CHUNKS + 1 + n]
            source = place(entry & 3, (y + ((entry >> 2) & 3)) % 4, (entry >> 4) & 1)
            number = entry >> 5
            wait(mid.at[rows(n)], leg_recv.at[n])
            pltpu.make_async_remote_copy(
                mid.at[rows(n)], arrived.at[rows(number)], hop_send.at[n], final_sem.at[number // 4],
                device_id=mirror(source), device_id_type=LOGICAL,
            ).start()

        return carry

    legs(0, FIRST)

    def start_load(n, carry):
        load(n).start()
        return carry

    lax.fori_loop(0, groups, start_load, 0)

    @pl.when(on_diagonal)
    def _():
        def own(n, carry):
            pltpu.make_async_copy(aff.at[group(n)], arrived.at[group(n)], final_sem.at[n]).start()
            return carry

        lax.fori_loop(0, groups, own, 0)

    for t in range(groups):
        tile = col * groups + t
        bits = (words[pl.ds(tile // 30, 1), :] >> (tile % 30)) & 1
        mask_rows[t : t + 1, :] = bits.astype(jnp.float32)
    col_sums[...] = jnp.zeros_like(col_sums)

    def prune(n, carry):
        load(n).wait()
        mask = mask_rows[:, group(n)].T
        total = jnp.zeros((TILE, TILE), jnp.float32)
        for t in range(groups):
            lanes = slice(t * TILE, (t + 1) * TILE)
            kept = block[group(n), lanes] * mask[:, t : t + 1]
            block[group(n), lanes] = kept
            total += kept
            col_sums[:, lanes] += jnp.sum(kept, axis=0, keepdims=True)
        row_sums[:, group(n)] = jnp.sum(total.T, axis=0, keepdims=True)
        return carry

    lax.fori_loop(0, groups, prune, 0)
    row_shares[col] = row_sums[...]
    col_shares[row] = col_sums[...]

    def share(n, carry):
        other = (col + 1 + n) % SIDE
        pltpu.make_async_remote_copy(
            row_shares.at[col], row_shares.at[col], row_send.at[n], row_recv.at[col],
            device_id=row * SIDE + other, device_id_type=LOGICAL,
        ).start()
        other = (row + 1 + n) % SIDE
        pltpu.make_async_remote_copy(
            col_shares.at[row], col_shares.at[row], col_send.at[n], col_recv.at[row],
            device_id=other * SIDE + col, device_id_type=LOGICAL,
        ).start()
        return carry

    lax.fori_loop(0, SIDE - 1, share, 0)
    legs(FIRST, CHUNKS)
    lax.fori_loop(0, BEFORE_SUMS, hop, 0)

    def share_in(n, carry):
        other = (col + 1 + n) % SIDE
        wait(row_shares.at[other], row_recv.at[other])
        other = (row + 1 + n) % SIDE
        wait(col_shares.at[other], col_recv.at[other])
        return carry

    lax.fori_loop(0, SIDE - 1, share_in, 0)
    row_total, col_total = row_shares[0], col_shares[0]
    for n in range(1, SIDE):
        row_total += row_shares[n]
        col_total += col_shares[n]
    near[0] = row_total
    near[1] = col_total
    to_partner(near, far, pair_sem)
    lax.fori_loop(BEFORE_SUMS, MAX_RELAYED, hop, 0)

    wait(far_words, word_sem.at[1])
    for t in range(groups):
        tile = row * groups + t
        bits = (far_words[pl.ds(tile // 30, 1), :] >> (tile % 30)) & 1
        far_mask[t : t + 1, :] = bits.astype(jnp.float32)

    def store(n):
        return pltpu.make_async_copy(block.at[:, group(n)], s_out.at[:, group(n)], out_sem.at[n])

    def finish(n, carry):
        wait(arrived.at[group(n)], final_sem.at[n])
        for t in range(groups):
            span = slice(t * TILE, (t + 1) * TILE)
            mirrored = arrived[group(n), span].T * far_mask[t : t + 1, group(n)]
            block[span, group(n)] = 0.5 * (block[span, group(n)] + mirrored)
        store(n).start()
        return carry

    lax.fori_loop(0, groups, finish, 0)
    wait(far, pair_sem.at[1])
    deg_out[0:1, :] = 0.5 * (near[0] + far[1])
    deg_out[1:2, :] = 0.5 * (far[0] + near[1])

    @pl.when(jnp.logical_not(on_diagonal))
    def _():
        def sent(n, carry):
            wait(mid.at[rows(n)], leg_send.at[n])
            return carry

        lax.fori_loop(0, CHUNKS, sent, 0)
        wait(far_words, word_sem.at[0])
        wait(far, pair_sem.at[0])

    def hopped(n, carry):
        @pl.when(n < relayed)
        def _():
            wait(mid.at[rows(n)], hop_send.at[n])

        return carry

    lax.fori_loop(0, MAX_RELAYED, hopped, 0)

    def share_out(n, carry):
        wait(row_shares.at[col], row_send.at[n])
        wait(col_shares.at[row], col_send.at[n])
        return carry

    lax.fori_loop(0, SIDE - 1, share_out, 0)

    def stored(n, carry):
        store(n).wait()
        return carry

    lax.fori_loop(0, groups, stored, 0)


def on_device(affinity, keep_words):
    size, _ = affinity.shape
    groups = size // TILE
    words = keep_words.T
    vec = pltpu.VMEM((1, size), jnp.float32)
    dma = pltpu.SemaphoreType.DMA
    symmetric, degrees = pl.pallas_call(
        kernel,
        out_shape=(
            jax.ShapeDtypeStruct((size, size), jnp.float32),
            jax.ShapeDtypeStruct((2, size), jnp.float32),
        ),
        in_specs=[pl.BlockSpec(memory_space=pltpu.HBM), pl.BlockSpec(memory_space=pltpu.VMEM)],
        out_specs=(pl.BlockSpec(memory_space=pl.ANY), pl.BlockSpec(memory_space=pltpu.VMEM)),
        scratch_shapes=[
            pltpu.SMEM((CHUNKS + 1 + MAX_RELAYED,), jnp.int32),
            pltpu.VMEM((size, size), jnp.float32),
            pltpu.VMEM((MAX_RELAYED * size // CHUNKS, size), jnp.float32),
            pltpu.VMEM((size, size), jnp.float32),
            pltpu.VMEM(words.shape, jnp.int32),
            pltpu.VMEM((groups, size), jnp.float32),
            pltpu.VMEM((groups, size), jnp.float32),
            vec, vec,
            pltpu.VMEM((SIDE, 1, size), jnp.float32),
            pltpu.VMEM((SIDE, 1, size), jnp.float32),
            pltpu.VMEM((2, 1, size), jnp.float32),
            pltpu.VMEM((2, 1, size), jnp.float32),
            dma((groups,)), dma((2,)),
            dma((CHUNKS,)), dma((MAX_RELAYED,)), dma((MAX_RELAYED,)), dma((groups,)),
            dma((SIDE - 1,)), dma((SIDE,)), dma((SIDE - 1,)), dma((SIDE,)), dma((2,)), dma((groups,)),
        ],
        compiler_params=pltpu.CompilerParams(has_side_effects=True, vmem_limit_bytes=47 << 20),
        name="exchange",
    )(affinity, words)
    total = size * SIDE
    left, right = lax.rsqrt(degrees[0]), lax.rsqrt(degrees[1])
    normalized = total * symmetric * left[:, None] * right[None, :]
    return normalized, degrees[0] / total


def solution(mesh):
    in_specs = (P("row", "col"), P("row", None))
    out_specs = (P("row", "col"), P("row"))
    return jax.shard_map(
        on_device, mesh=mesh, in_specs=in_specs, out_specs=out_specs, check_vma=False
    )
```

```python
import functools

import jax
import jax.numpy as jnp
from jax import lax
from jax.experimental import pallas as pl
from jax.experimental.pallas import tpu as pltpu
from jax.sharding import PartitionSpec as P

TILE = 128
SIDE = 16
CHUNKS = 32
LOGICAL = pl.DeviceIdType.LOGICAL
DIRECT = 127
MAX_RELAYED = 114
SENDS = (
    0x1fff07bf83bfc1cfe0dff06bf833fc18fe0bff05bf82bfc14fe09ff04bf823fc10fe07ff03bf81bfc0cfe05ff02bf813fc08fe03ff01bf80bfc04fe01ff00bf803fc00fe0,
    0x1fff07bf83bfc1cfe0dff06bf833fc18fe0bff05bf82bfc14fe097f04d2563fc0ffe0820abbf81bfc0cfe05ff02bf813fc08fe03ff01bf80bfc04fe01ff00bf803fc00fe0,
    0x171219bf83cb83d561e290ed3074902206458f180093284383e1b9d0d8d85844d52e1a160a460ce2c732619100c4706030251031861bc505a243f06e50508420d00824001,
    0x1fff07bf83bfc12373e7f06ff820627afe0cff03cbcf1fc0d2d3bff05bf8184e630745119a46cc40a95fe0a7f04ff8000691fe077f01c5cd7fc0613347f017f8021264fe0,
    0x1ff107b803bb81cd80dea06b40339418c60be105b002b7814b809da04ac0235410a607d003a601b1c0b860542025e810dc07640600299700a9c0448019a008a0024400180,
    0x1fff07bf83bfc1cfe0dff06bf833fc18fe0bff05bf82bfc14fe09ff04bf823fc10fe07ff03bf81bfc0cfe05ff02bf813fc08fe03ff01bf80bfc04fe01ff00bf803fc00fe0,
    0x15024fa18be09a6029ec116519b801b6426dbc117f834e8586e2bb515598a8c4535e292c14558a0a44f4e2724104025a844c3e259b124a88e4042fe040931040861440002,
    0x1eff07c36f9fc132b2dff06bf833fc17fe071195bf81a3655fe0c05ed3f8040e6a1528ff0781421fc091327ff01c348832e509267f04807460a4bfe0003ba3f8020246fe0,
    0x1882564807a846afe0e1e1ecd8ee3c3a323182354707058721813ff058a0e840731a308033c50602c6e10327f03448561c2614c6051a0287e248208c2830a408fc1080020,
    0x1fff07bf80e3b3dfe0792b73f837fc1afe0300f348db3fc18fe0bff05bf82bfc0b216a7f04ff825fc11fe01988c3f8123acefe067f02bf80bfc04fe040cb0bf8000b41fe0,
    0x1fff07bf83bfc1cfe0dff06bf833fc18fe0bff05bf82bfc14fe09ff04bf823fc10fe07ff03bf81bfc0cfe05ff02bf813fc08fe03ff01bf80bfc04fe01ff00bf803fc00fe0,
    0x1fff07bf83bfc1cfe0dff06bf833fc18fe0bff05bf8020354fe09ff04bf823fc10fe07ff03bf81bfc0cfe05ff02bf813fc07fe037f017f809fc03fe017f0542fd062e0fe0,
    0x12ff07c39f2ad8a0ab17f02022f7341a960c4805e30383d16800abb050fb22659368092f041601ea40e4c06a100c1bd87c0b3a0f043a4c80e5c0626020e07401c22c000a0,
    0x1f8dbe45dec2af3117f508f674601efc991dc98ea34710e2d0d7605bddf468e22709792f8c55c5e9e2e4115928a816d2422303040e89405cc3224131aff0083c421220031,
    0x1ecd17ca9f9305b962d4a16648b120578e2f1855a30ab10548429c0149f0a2ec507227b61399084016d60262e12d5094a0494c242310403ce80463a229811098864440022,
    0x1fff07bf83bfc1cfe0dff06bf833fc18fe0bff05bf82bfc14fe09ff04bf823fc10fe07ff03bf81bfc0cfe05ff02bf813fc08fe03ff01bf80bfc04fe01ff00bf803fc00fe0,
    0x1fff07bf83bfc1cfe0dff06bf833fc18fe0bff05bf82bfc14fe09ff04bf823fc10fe07ff03bf81bfc0cfe05ff02bf80600800ec4ff023f80ffc06fe02ff013f805fc01fe0,
    0x1c7f05bf829fc0101cf958f89c7a4a33fe097f0708c63fc1b1d187f03ff834362efe06ff033f815fc0b1f94ff023f80ffc190f137f05c1c49fc150311ff00bf801fc05015,
    0x1f9767bf83a598c126700270ab3651930c248c7689b102dd924cc116104bae41961ec38310c3baa39941ac90c6445b20298f12c084734430a052b0ec5066181b0009c200c,
    0x1508db4b5fe639e2fce96e706636579a29cc93e60972eba7623ca10e4c7f243b911bc80ce3c5f1c2b8c13c595b9c470a1f8843f48ac1907c81b830bc104e041f000395573,
    0x19044fca037059a78c8034e5d330d9961adbb56558328b59150c98b6bd2b1c818d10d5866a7f81411a604d61e6785010498302d38d613f83a18050cc1006842338040000c,
    0x1690aa4654c12b8fe0a7f0718659fc0afe02ff07e177d03bd7bddbbe8ff834e7b96ddbb4ed99743fc1561d9acec90e62a3b049d7a1eb8ef566ba82fd393e88574806a005d,
    0x14032d8d8aa645e069fb56f5a378cda5fe0a1816d8b74c1b95ad99611d13b0a9b750d8256c8a0a24c4f2027226b5035471ac1c2319690a3562c431ed10b68443521c4008d,
    0x1787dfd54fca27d4f3703cf12cf6927a453ca198807707e773d3b1c9a487941b75353a179ccb4cc33d22938929c08cda426c1f320bf2c6cc623c81733889943cc20a60013,
    0x1f8d57862ba2d5a261c920f0528c01d8221b900d8786a21541c19875486862195018178b0b42a9c282c1215845241a94202804a387094304614220612015001076000100a,
    0x19ff07c95a5fc1e2368ff074859ffc0efe06ff0707db63accfe0d0db2ff83232c9fe047f0605d8dfc171562ff0584d89fc1511617f007f8281ad00b6504b1c1d8602c0fe0,
    0x168c52c5a85fc0e3cef9f378f1ba74c812ae1c307f8125ddb366d1a364c9b05cd72c6b15354a18e49d426699234889a240d01e678e3106b9830ca166308314398608c0fe0,
    0x1583b5496bed3c4056f33f759784127c63edb0f697f8206795dec2df5d67acafd455e9a9f0005e4a3d14fe826f3d279c8fcd43e620f28f79273c837e399f18b78a4bc30fe,
    0x1f8a3b842fa24fefe0dff063f82ffc16fe0aff0343ae9fc13fe06065f041e5fc1a0e75045c7f80c09790c787f03ff80e0ce502b2023aff813fc08fe017f007f80604e0fe0,
    0x1d05bd425fe477e21b409af47ef83b7b1bb883b900df2337817bb8add84ee82360017507b4c4c581f6b0db485dc844601a2e0df384d981eca0b6f091085e8c0eda022201b,
    0x1101568cafed9fe6afeb47f19bf6c9f962fc307dd7becb9f55afa2c7cd53e4a5f14ef8105bd2bdc8ded42f6207acebd46de932f41779cabcc45e51af20978c2bc209e000f,
    0x1f9dbf8e5fa6ee4fe0e1abeccdf462f92f7c14bdc9dec4af523771afaca7e842e921f1ff04c7de43ae615f88dbc065de2eed157608b9437c40be1fe0507ba025c003e7057,
    0x1fbf20ff829bd1e7c4ebd26de134ec9974417f061c92ee0966c4e03655a926d0926640ff0459101fc106247b0239791ab88cac85ad2296112a8884e43a5219110a4084308,
    0x1d14f78e47a6e3c351c9989016304fd62f1a1688c05368eb7415a9eacca4602bd1315708f34ad643e21fe0613abcce4e3aa5195486888457e2ba80b1303883f81607ca01e,
    0x1281204013a60ff04ce173bc2b8814de00cd963e8a9f250f826749655c91ec44e2086a8f3d071ce39531a790c3c459e028e314a7093b441d818eb0a700652819d1fc06047,
    0x1a0ba484d0ffc11114e09bf8f4fab77b59bd2ade546f09b774bbb24dbc3d181a9547b505a4d16d0128507481fd8c151c7b6d3bb59cda4cec206862bb212dfc07043f60014,
    0x1f0a7fca0324c09fe04022cc702e8484fe0b20254e1286881fe0918244b90c04b02a4794208015c489d12f68f27043d8389b0cf58b2682bd4248710428520c193009e0004,
    0x127f00ff805fc1ba590ff003f83d12bd875e42aea0d7302b87f5bbdad9dd6ae6b46f59b4ac98d62bab05b57abab94d7e5fad515626aad2d5472a9355419a9cb54c12a5035,
    0x1e1137d927cbd3a206eac4e479b69d371c6aa34d069a079388aa71a4d9faa6f54c309938545a294552f5aa3124948a4835281a26a55043a4e28cb38a18830839926940069,
    0x1e14b7bf83e12ad05518cdec9d9012e6077d11b0815f242d81f6b8eb002ed427f61b6081a942fea32d417698ab77f82426d1116807b3c359c16cc096583b24158e06c4016,
    0x1e890fbf8382036120f8934c40344c8c02eb96650ab244d9124c7916387b1639891ac38c6185b361c390c12886103b15fc030acc050d42044211006100263410500421001,
    0x19a6efcafa497be1fe8a3ec1177a37cf43d69feb0f75677bc17e51cea4df506bb6311d89f1ccf6a562631dd07f509c721bc52dd214edc2fb1fc031fd7088885f4217a005d,
    0x167f02ff813fc08fe02ff00ff803fc1e52eea87713bb499d94aec2475d13ac81d53eea1e74ceba471c0fe089a740bbb7394f2ae7127347b9431df246388718238809c200e,
    0x1cb6d63f83e4fde25eaff0748f9ffc1c21ed8ff6877ac37d419e98bf48579dfc1113e808f33f81a1fcb0debb5d242f9013cafe0383f1bf809fc0505e17f00c0f81fc0101e,
    0x1f853bf22000dfefe0ab726d3b3299974aca246491b22898108b8216350338600c3ecd17060b016798a3ac9a9224e33a00f624041b638680e6985180319610c30628022ec,
    0x1f90fe0947c3ffd1df905db426f833eb07b482dd876aa375419a301dcc5eb627fa07f41ecbc4eae2e3905f708d303e941b510f1385d400fca134407a102d040e86036001a,
    0x1f947e3f83c4df1fe067f04c18ba49fc22fd907a7f8343df91cfb8d79bf82c31f516fa0a7c84bde21e4fe06877ac33c5fc0a0af801107f801fc0e00240479c1bca09e302f,
    0x197f075e7f8effb75f37f00ff834e7f971fc37f8bf82edbf66bfab4ffc55e8cff365f8b1fc187debfee5bf6acfb14ffc02eb4df523f840ed283e83bf39bf94afc1fc041df,
    0x1a0b64ff825fc11fe0787643f81dfc0d0ccfed22c2b19fc1ed64ee922423399c8afe030366f31080988fe0d6221ff80bfc0202ccdf262e907fc17b64b59207f82b5c80fe0,
    0x1f89a78451c0f1007ce48a8ff83a1e9a8f5c44ada0d761a8d05cabfacde564eab16b5c85a3d75589aab475501e2016126ea6038280c106d6e12820d5380e041d680e80015,
    0x191c3fc723c351d188a87190126268f0307e0b438291610830297963ec521a50f4083d0943099f2210a207c0742071d208970c8b016180926046100938540819ca1100027,
    0x1dff0702616677afe0e86e63f82ffc16fe0aff053f827fc12fe08ff0780d21fc0ffe077f07c2ff20fe20db6ff033f815fc09fe047f01ff80dfc05fe027f00ff803fc00fe0,
    0x13844f2a131fc1e480f91674f02dfc14fe0dd226a89333c97944ac524df923fc127247ff041991bfc0bfe02014b959188c89fe051c220b10a4086fe018a2001905fc01fe0,
    0x1f91eb3f8322bbea3557f0767d7936bb975d4aae22d47fc176f5b33ad58d68b6a0fe09aaac94d6096af455690cb8fd5672a82d5395a98a54a46a41f548cc885d620ba1115,
    0x16034f3f837fc1afe0cff05bf82bfc14fe09ff047f81ffc1814e4993483356354714a77f023f83e1844fe029430bf8063cd70ce6862c02b7c0841fe03012a82341fc1d002,
    0x1f05cc475fe27e727bc05e5c2719fc0b117a85ef0264c16ca0f7703e2017060ec2036d83c900f0bfc00fe0a04ed81642039d075d02ae40d660fb2039780cc0175a07a901d,
    0x1f8174d402c55914c0ea63f803b894fb487d233e511f080f73e7a9d3d0e1e468f03077973b8a9da4cec2475913a879d238e818718131c51cc24e50e720638819c208e0007,
    0x180deb426940f4105afa8b793db89adb4b6d24b651db08ad7436b20b54fda87ad33b691cb44dd9e6ace336618b2cbd925add03e415b1ca58c4ec5256211b0c85843ec0156,
    0x1fff07bf83bfc1cfe0dff06bf833fc18fe0bff05bf82bfc14fe09ff04bf823fc0b0ae87f03ff81dfc0dfe067f02bf813fc08fe03ff01bf80bfc04fe01ff00bf803fc00fe0,
    0x1f7f077f837fc1afe0ca5b5bf829fc12fe0c22b43f81bfc0cfe0a9fb7c0cd5fc0015b99db44d591fc0f31637f05c0ff807ce2f627f02ca5924ec71f61ff00bf80a3ac1fe0,
    0x1d2306c833274183609ce242492e580e88463e229c12c440920843121d512a341e527ea83d0600c888102b29b2483808548f0c018f247f81a080212458107139fe01e0044,
    0x1fbe8f9e47aea3c711db68e9ac72ce38651baf8d9646aaa344f19a48c914627e303b179b8b8bc5a522c2515918a88452362817138a8984c4a1e240d11858881c420a20011,
    0x1dff06bf83eacf8fe0b7f057f827fc1e50770474bf823fc1d4c787f03ff83890edfe067f06511c6016bfe057f05cf9e878e102a003327f80ffc0814737f013f80a1ce2fe0,
    0x1fff07bf83bfc1cfe0dff06bf833fc18fe0b7f057f827fc12fe08ff043f81dfc0dfe067f02ff815fc09fe0babba3f80ffc1453737f017f809fc03fe07a7b8bf803fc00fe0,
    0x1fff07bf83bfc1cfe0dff06bf833fc18fe0bff05bf82bfc14fe09ff04bf823fc10fe07ff03bf81bfc0cfe05ff02bf813fc08fe03ff01bf80bfc04fe01ff00bf803fc00fe0,
    0x1f7f077f839fc1bfe0d7f067f831fc17fe0b7f057f829fc13fe08ff043f83ea32ffe077f037f819fc1239d5ff02bf813fc08fe03ff01bf80bfc04fe01ff00bf803fc00fe0,
    0x1fa20f9007a783c381d1a0e4c04e48782c1d8d6dc986c4835221a1009878e63c251631881c8706230220c378a090221c202808d6860c0031810210835830a808400869001,
    0x1eff06bf8300380014bff05bf83e967e473aff0710cf67e74fe097f064f4e1fc1337389a9b8bcd65a692933129bff81bfc051f367f01064d5fc0313347f00834cffc01033,
    0x1fcd07a603b2c1c940dc906a40331c188c0bc50562029081382093f045f02ca990760739035b818d00f6045b00297812b4085603a9019380a900444019e008d8025000020,
    0x1fff07bf83bfc1cfe0dff06bf833fc18fe0bff05bf82bfc14fe09ff04bf823fc10fe07ff03bf81bfc0cfe05ff02bf813fc08fe03ff01bf80bfc04fe01ff00bf803fc00fe0,
    0x1dff06bf83ce45c6a2cb1163f82cb854562928141289c845f10d69f15ff8167055fe09ff024c8ba19a72828ff0148088384ffe018b1083899fc0afe047f004188c0520022,
    0x1eae97c5778b65e13dd2b96554b0a65b11dba79592ca61fb5472a21944f49e6a4e2f2906eb09ca017a001357f03427560fa9252302ea0848e324301d2899102c840a41012,
    0x181001812a4798100af924389b3c391d341509070c856359b301d170e0b06e5436281a930d0906644311e1388608019e34240a068b0b048521c390e4000020284a0c23021,
    0x1fff07bf83bfc1cfe0dff0042775fc19fe0c7f05ff82dfc15fe0a7f04ff825fc11fe087f03ff81dfc0dfe067f02ff815fc09fe047f01ff80dfc05fe027f00ff805fc00fe0,
    0x1fff07bf83bfc1cfe0dff06bf833fc18fe0bff05bf82bfc14fe09ff04bf823fc10fe07ff03bf81bfc0cfe05ff02bf813fc08fe03ff01bf80bfc04fe01ff00bf803fc00fe0,
    0x1fff07bf83bfc1cfe0dff06bf833fc18fe0bff05bf82bfc14fe09ff04bf81612d1fe087f03ff81dfc0dfe067f02bf813fc08fe03ff01bf80bfc04fe01ff00bf803fc00fe0,
    0x1f7f077f839fc1bfe0d7f067f831fc17fe0b7f057f81405f4fe09ff04bf83e3111fe087f03ff81dfc0dfe067f02ff813fc08fe03ff01bf80bfc04fe01ff00bf803fc00fe0,
    0x11ff0781cbe03e0051eb582c3678ce01fe0db28698432ba18590baa8593c2a9a144909a2848fc227a1039079b838cc1a620c2d0515824941042071d030c81454081e02070,
    0x1f5417690b9405b9e2d4d16660b12857922b4715630a9105382293e145e0a0e84f6c27321357898b04b522526125189080473a231a114a88848431421091043080145f086,
    0x1fff07bf83bfc1cfe0dff06bf833fc18fe0bff05bf82bfc14fe09ff04bf823fc10fe07ff03bf81bfc0cfe05ff02bf813fc08fe03ff01bf80bfc04fe01ff00bf803fc00fe0,
    0x1f7f077f83e149cfe0dff06bf833fc101ecc7f02c5b2ffc040ec08145bf82bfc14fe09ff04bf823fc0ffe077f037f819fc0208c57f027f811fc07fe037f017f807fc00fe0,
    0x1403c14160ffc04fe0fa2abcd67c6eae2b9d38e65bf184b376dc92fe07f816432a199100c455f1a029047ce8d8f06452279b151c088982f2c162305ca838d00c400393011,
    0x1f9c1b42b3c686b08ce981f0b0d00d9b2a3b247e498f0447720391d7d470e8307032f98a1c448f5fc0c2af30260c0b1e1c6a28f7051a418ce41e51cf202180030229e2023,
    0x1d81a084dc21aff49cf23e75173883993dcc1ce5cd72c67952fca15e4c9f244b9121c80fe3c771c378d19c60be2c57002fea13cd00a2447101f870dc305e1427080f8305c,
    0x108049ff81a41bf2842ff02c735e719e520ea7030c238941b44050c6e8f8327018340b97024536c4c0810d3066d48028380408d98c00ff8242011080802008134001ae000,
    0x1fff07bf83bfc1cfe0dff06bf833fc18fe0bff05bf82bfc14fe09ff0001665fc11fe087f03ff81dfc0dfe067f02ff815fc09fe047f01ff80dfc05fe027f00ff805fc01fe0,
    0x1fb1139a3bcbc5d5a2e2c16d509448da4e232476528a085b8462ba213cfb6245563e261d6d4e8966da12eea1a14cb8a4504832d69011cbb4855a328d48c514388025a2022,
    0x160b927f83e6fbe35de99ef0c7765fba2ddc95ed824f053ab13250795c9f501a5525d208f9c2c8c0a5423d990ec87f623bb01bd185f8427de33a20bb70beb4574a0240039,
    0x1582703f81005c306a10257cd90801de2e408057520f88c7b423d1f1e4e8f07077343b181d4b0e850732639111c470e0346f1637091b440d8186a0a348419c18cc0465003,
    0x1aff04bf83e3f5e1da87f03bf81bfc1d1bae0cd5025762f4cfe057f027f8342b58056c89d5c468dfc160fa986d442e9e134b07a402d0ff80e06c503a17f0100581fc0101a,
    0x198d57eabbd4dc7fe0ed177273b72dda90ecc5762139c21577aeb3775583a8b5d254e8a77411396194f3ce37f034db9861c922e40f714638821ca06a17f003f80611c104e,
    0x1fb5f4406bcd3dd67ee32f48a5f6c7da61e78ebe57fb0b3d751e70bbd937985b690b7aa4f1c76c5fc08097a22f4ce7882365077819f34af963fca17e307f0c1f8007c1017,
    0x107f02411e47d9f0cbe8559009e0699b08b7986714014691a4c069566518184d8b24c41165ce80e39851ac30e458b0300d6e04b18a6548804219e104a0904c28020d91020,
    0x1486ffc0ecdfc1e197514ef45dce03fc1572ff020977626f91b2c0c96845ec2a570f798995435e41e510d2a05bb82ca012ed0520ff03c1dd806430bd202bac048402e003d,
    0x1fb37f993fac5fb60fd2f7e573eeb5f558f9ab78ff80e4ddc3029287e0b0ac48542228267b90bc5fc111e278b134f3d82441fe050512cd3d25de806228c7903bcc004000f,
    0x1fb5ff5a7f6cff965fbb0ffbf82abffc3fbd7f05bf826b7edfe092cfabf822afe6fe02ff03d57dca7ec51fc1ddd0dec7fc0b4ff817ba537c5fc0845f0ff01ce7c1fc041df,
    0x1daf22ff83ee59a5c427f079c332b482fe0eb6661612eac96524aa8251392698924a48a4241191e8880fe0721234f9186c9c6ac51422489103c8718430a21431061081004,
    0x1f988f0ad36529a274c12a5c8d3c4bbd2d1b10a649c683e9523198ea446d243e2e19480c8b05d142a8f151489a1c450a1e8d111186a2c3c4416880b1084a000d0c0a24011,
    0x1d8e3a028be1c9a1a7c9035c61f03cd4167f0624c51e024f61c66883f429242ccc0e75063bc51b810821aa70932429ea39c508788321019c0044b0e630221c298608c1024,
    0x1f8ea786d2c96fd194a24bcd1df62e91457d0aa48d4e0666f437720be04d2e228d3d761cbacc4d25a6a357cff01c94ea1e851f3301c1064c00688337197b8806380781277,
    0x1f132f4917844bb20577f033f8323cb71c5b0d2abf82830b216588a2c049741809fe0c0403c415a1cab0c54052fc034ffc0608520328c114bfc1504017f00409660000fe0,
    0x1fb6af9ad74a327fe027f0653e45fc1d6950ff0719d76cab7635ab0acd7d64bab15b5c26cc16541fc0f57572aab54d6c972c4d55a3aa8fd5262a81f5a24c984d4a1ea3075,
    0x128d4fd2095fc1e462ea217108b6805a3e220b4e4f0b07457382b1b154d0a864533021852c8b8a258502a21074bca09c4c4d22260f12c708215291820024a0508e20460c2,
    0x1310dec37fe2bbe11de87eb84e5a232c0f9586ce42fd41728099b83fe85d8e0f38156b09b5445a81ec3053986b482da212c1033003dc01db80faf056282c900e5206c2019,
    0x1202779ba7ad13c629dae4d10319fc1a56999e644db1c6599529c264dd1a56618202eb214a4ab0e499540991f4987b2079251ac18a63cea42198d389f81328da400d88fe0,
    0x1b7f07d3f70434517ef26ef52f50335c49dda3e905eb48bb943daa0ed0ff667ba309e89dec91e440fcf39d71bec1165a6ba10baba38b0cf5663a003a517ea4b74e57a629d,
    0x1a43575b38bfc04fe094053dfab8d5db68e73b50ff834cdcc70acb277c99b0c1ca66abae707f82cadd552e9a874533a091cd42ef12303f81679c936e41971cab8c21c204e,
    0x1b14f486581fc1e2b3a13f4c97a247cf21ed939e48cea834c1deb909b86cd637df0d480bfa86788226915e1879a047ba168d13f308f9c1f8a07c20ffe04a681d300a8101f,
    0x1fa27f903f6d19a66c99e7e193226def32fbb1630bbd455e924f3907f1aa32c5165ecaae6187bda95145ac20c7f401c629f258c4204043bc4096004f82a614b21c918b42c,
    0x1d84e389f7e2b7807c693ce407fc1f7d698511ecc2ed243a81fd38eef18e34b71751828bed92e0827a30fda81e5106220386fe0817c3c9e041ba109d60fc4826c00bab05b,
    0x1c9f7d0ebf4405236f8977fc7170345028f07f058589e49f51229871307bfc30bd165e0a2ec495635f70e53831205bc6084d1ae2887b8194819e208f5022a4094201e6005,
    0x127f07cffd626e8097ab1d8ff83c7be2fe00ff074eff873fb37f07f068d7e8bb7933fc18fdcbfec5bf32bf914fc49fe04bef23f710fb47fd83bea1bf319da467ca0be7017,
    0x1fa0617f809fc1e3ec17f072193a7994748dc0249ba347181fe0cbd25de12ce8957049b62459920c88f5c472c2355118a08b4c45232250910749832c399218b90630800c4,
    0x1e82e7d4451fc1e4f1e01e1bf834a699058aa1a48ed3682b0354c1eadced6c72b437599aac4cd5e5eae2d51ff0348d583eab1d550daa45d4e26a5115101a103d4212a0015,
    0x1eff07c6b3c319816ce7f02410f7fc1614cd7f0504b33fc1210cbff057f8201d8702370664ff823fc0ffe0605637f80c0d8bfe020262bf811fc02fe018161400c20180fe0,
    0x1f21a43f83a7e8ffe0e1da6cdd1bfc1a31467f02bf8325a89fe03ff05ca50dfc04fe01ff00bf83e6301fe007f0149dd02bf5234c149d894e8467321390d9c45cdc1a6b033,
    0x1f9d674d32a619e705896671b15e559b6a5d332e5915c4d9860561165d795441965a540f61c6b28b0a616c9aa2945324a0a412c82728c3b1a94a20405a42841b1288a002c,
    0x1fafef9777ab7bc59d0ff06d5f74abb953dc27edd376c97b549da21ecd07647fb03dd79deb8e75a6bb1435619eacbf5457a929d412e9c874c3ba51bd20be8c4f440fa003d,
    0x1b896d84359fc0600ea876fc527c253d10950652ff813fc1c0e947f01ff836193a0a92ff0503349fc120adc844c02345fc180699824c40a5c0da10066826bc0241fc0300d,
    0x1d89cac07721b360b9f97c78b63a571c298d13c60962e471221888fc407607fc1509978dc3866182f0a158489c2046280b270f8306c142e081302078981c83f8020b0d019,
    0x129440c28040c1f06af19374c1b85cdb2c6d15364a1b04cd7246b113540ba840d31e688e33c699c30cd16660a34bf81624d0fe008b428418008890e640631c298c10c4066,
    0x1ea58d4fd78923b451d218fc7eb282383d1b9d8d8dc5862b43319978c8b45456b129181389c855e462e1d168d89065562a221554888a0347c3b460b1086a940c400ea3011,
    0x1fff07bf83bfc1cfe0dff06bf833fc18fe0bff05bf82bfc14fe09ff04bf823fc10fe07ff03bf81bfc0cfe05ff02bf813fc08fe03ff01bf809fc03fe017f007f801fc0518a,
    0x1c1fb7cc4e5fc163b6f159c7f81ffc0823730dbf47cea6ed41fa998b37f819fc102d6714b7064d3fc0b236d8a9a87587fc1a0f338db1455b20e64116106b5c14c20760096,
    0x1e913fd003440fe3a0c0f3d871f8701b320c9705469e830f32c0bff044a8202cef1471807b4901640125687093b041d21cea1603063a0480a14e408710338409ce1c00007,
    0x1c12b7c0efc3af7236894a746dec3ecf234a8eb7065da368503fa0db6c5de42e3311a70ab305d3426eb136408a2845b222e90f6306a1c35a00ee2094184b04158002c4037,
    0x121635102b081753cb0ff044e2964d5c547da93e939de65794a7ba33d911e680f23e781c3b8d9da60ec2c748472899d044e61a7f8411449ce295e022e8010c29c40ce0027,
    0x1e7f06ff835fc18fe0bff05bf82bfc1f497f20bd3f83a76f2fe08ff04cc5e1fc0ffe06ff033f817fc0afe0715ba7f8322b64157107ba3f80ffc0005737f017f807fc01fe0,
)
RELAYS = (
    0x1f87c1a23a1fb381f3361eb341e336cc85ebc074cb86c1cb2a1c3281bb261b3241ab1888878d8076dd35e1cb66fd8dc1d0eed83f03686e3ab5cf58541d96c39b58f48745a8f259354f40705b9663834e143ea590cc1a1603734ef78e25285c379481634cf68dc560d8558d4d2bc6148c8838d0d23c4130d05084ad1bc833940108c6d13c4a010a500c250340f00805,
    0x1ff3dcef37ccf2fca70981cc34,
    0x1f93a4e1364d1324c12e4b12a4a124489204791a4591447316c3112c33044,
    0x7f4f53b4dd354cd314b52949d2548d2147d1d4650f42d0941d0540d3d1f7014,
    0x722b8aa2b1642995e2689a55896540945288c519445,
    0x779f77d3ef7b3e7793df75ddcf9cd7353c771cc4ff5b73d5af2f3ed67cdd65cd5693bf7358f2f5b76d5af6b594dfca76758ce7d976357cd9c876155f1fd7d5d37751b7557d4f1757e0724551d3f4dd3d5732f53327513270d31745524c3d14c5c0dc330f01504c1c,
    0x1f97a5e17e9d9745f27c0c97a9e8305e02e5da76081740aa5c5c81a5c0209b8145b01c931589a828052485980c92a6401962022600115e0680250a5ad500050250033480,
    0x1ef75dcf455,
    0x11b8c6,
    0x7fef7b9edfb5ecfb1ebfadeafa9e9fa5e8f9fe7799e5f93e478fe378be2787e17adbaee9b9ec1e7eddb66d5b3ecbb26c5b0ec1b,
    0x76ae8f83d8f43c8f03b8ec3c26a3f0683e8663b26439a76188f4180e49c05e3b8629a85c3a05a3985837a6418856380543785236a5c140ce5684e3605c630d69585294b4a349928484ad20ce618ce11b4e8219244106821081190081842403c0400c01,
    0x73abebf6f5bb6e5b76d5b36c5af6b5a969da568da16cf9f675b1e6d996af9569f93645a3e3d9fe778d69c57e4f8b6745353f8be6c4d5255514c4751d8f1374b11f47117431,
    0x1f3fafe3faee3b6ed3b2ee8b0ebbb82aba8ed8a4ed0a0e7bb0273ac26b98e5ba825392e9890e808ee339c22b88e6082b1382e4880e,
    0x5d796dbb5ed3b36c7b,
    0x7e7f1fa7e1f67c9f07b9ec7a9e87fbe6791fcf89faf79f8f71f2f69d87bbe8f59e4c51e2c49e0c41dec39dac631c031d4c5810c29d203810f21ca02bc6019c201302703007,
    0x1ee378bff58a7f387ff18be2d8ae278450d4861d86e178941d74e2107c1b03617764098541371623d4c0793c0d73417d574b706430144570ec17,
    0x1d9f27b9e8791e2781da761d6751d2741ce731c8711ee6a1be191a267992b71966498e631bc1fb8a621ba119bcee1006e0762,
    0x176118360b8,
    0x7e8f23a8e2368d2328c22e83a0a8133e4033c4,
    0x7981f05c073f4,
    0x1d0b22c0ae2b0a8290a02789c260942388a2188e9108022258d,
    0x67695a7c8da167da1c6d9965d9564d9163d8d6fd4b6fc096f43b0e41b91db70d413915bf49ce53cc2130d9f3bc016ac1b3,
    0x1624881a028,
    0x1f6799de6d9965f9,
    0x46e6182e,
    0x1fdb54c51fe6f97ef593eed91ee5a14dd9d4d5b36bd9ba5683a5d154,
    0x1f1ba6e1b46c9b06cb6e6b36c6a9a8699a46b0626a868181a6179a41885c6631e1699815a546584e9434e648660790c6380860ac46,
    0x1fdbd6edb96ddb56b5a969da568da166d9764d9163d8b61d836,
    0x7c5e9785fbf65d17cf01f050afaf,
    0x7f7f5fb7fff97cfedfdde7f87dbf67cffd5f3785cbf,
    0x1fbfe7f1fa7e1f67d1f27b9ec7a9e8791de769d6751d0739ca719c6b,
    0x7b7e5f77d5f37c5ef7b5eb7a5e778de177def075db7ac3f165fd1ec577e477155f51cc537c46f145ed13deb15e11ea46712de513e631845b1644975c49d4441a554f12c4582d452074310c811,
    0x783d0f03b1be1c86c3f9767e2e6170ca3a1063b0a62791a459124310841106c,
    0x1851b4550f4,
    0x1b11cc,
    0x7b4c56f57551525435,
    0x1e8b82d8b22c0aa2809a240822,
    0x7d0ec390cc2d2b4290aca70a4b13fd5bd940fa8593dbcf3547dd28cd30440dd34235274bc,
    0x645815454354932429,
    0x1ad6959d6156d535,
    0x62af9bc6,
    0x7fef7bbee7b7ed7b3ec7afeb7abe57e9e8795e3f81aed87e,
    0x1fbbceebb8edbb4ecbbcbc3aeeb3aaea3a6e93a2e839ee4058e53b05630ce2bae5599c798c6e80dc3,
    0x15f89ee583a,
    0x7efebf8fd3f2f52d0b3bc8f1bfe7,
    0x1d7ebf8fd5b27c1f,
    0x44b,
    0x7d0fffdfeff9fdff5fcfdbc5f31fbfedfafe9f9fe5f8fe1f7fdbffd59f57ff9fd11fcd0ffbd81e,
    0x1fb3cceb36cd332cc32ecabeccab26c9322c831ec731ac5b14cc9d2c9be62432223b3c1d0cccbb6cda1fa1c8eadc0e8d89e4d8b6e3835edd39cdb0cac6b58da8e835b4c6534ed90de32b4461b5a358c0d,
    0x47c,
    0x12b02c,
    0x798a71389723c7f19c5711c2f07c0f01c,
    0x6498250d3344d,
    0x7ddef79dd773dc77f3bf7d3b77b3af793a7773d4e7dccf1397799bce3d876d37f6b3775bda4d9d5f673df253966fc8cebc84d5d7cd3d4763c74cfd6f1b3671935cd535e0fc4ccbc44cf334c5c2cc931ccdd14c332f413,
    0x1f27e52a385,
    0x1c57fd765bd0f655,
    0x1fabcaeab8afbaaa9aa2a6a96a4a90a2282a,
    0x4d6,
    0x7eee374dcb6eda35aa5a8ed4286d137e12304cf93c112fa1,
    0x79ddf6bad773dc76fdb76bda767d9763d875fd7759d5f53d3f49d,
    0x5cb6ad8bfbd4b19ccb2afaf,
    0x1fefdbeef9bdef3bc6efbb6e9b66d7b4ecfb36cbb1ec5b,
    0x1d2face336cd332cc32ecb320bab28c9b24c8b20c731aca818c5b280530cc98027,
    0x7ffe71587e559ad91d3745dfcbdf,
    0x1f87c1e8781d8741c8701b86a1e32819876c90621cb2ec806cc706ac6866ce2d818b20ccad61505ec485cc405ac3858c3056c6aca1530814b10b91c61431e5106073b1e7330ab69c2161d6741e02810e729c6c59067508472100c2084409c0e00402,
    0x754cd2f4ecfbbe4f73e6f5395333d6f138d2f3d72fbb4eb3b6e9385273af29b94e33972137ce1c74db386d9354e3f7ed337fd1366cf36fcd367cb34d11f24cdf3505f14c7417014,
    0x169164410c419004,
    0x7f4f53b4f7394ef334e7314df2f4b535cad33ca52fc9d254af234851f4751b46517455134450f4350b42507436058,
    0x7cdf2b8ddb7aad372de2b0dbb76ab368dd2a6dcaa4d8370a6b56dba92db2aaa92a0a7a9aa52ba2e0b62d0b02b8ac2a8a82989a588965789456892560905488c5408852884518805,
    0x759ce719b669996a1a8f77cafb1cbf2dca727c8f19e7f1dc579576ed176f0fe6717c5709e4f05e3f0bc2703e1dc3c0781305c1c,
    0x7e0817c0797a06178059740417203970021465b82c0a8280982402a620225e0015c0125a00a5805800950120,
    0x1fd7d5ed795dd755cd715bd6b5a567595635855f5755b5765b966579565193e4b926459,
    0x1f3baee3b6ed3b2ec3aeeb3a8e9ba2e7b9ce6b98e5b94e4b90e3b8ce2396641886,
    0x71fbff1ab7ebfa7d1a269df5fd5f4fcff0e87ff4c3f0681f,
    0x1f9bc3f1ba3e9b83d8f86d0f23d9b03b8f46b0ea3c9a83a2b0698e4a7aa43b9a2372a03f058ab19e3e05c5529c3c86a668ec1a1983a064658e4189943804c548e0670503685e638d61698c3485860948f28ce139c83498a141881120a61846310c861042300c66084260042d,
    0x1fdbd6edb96ddb56cdbb1e4716d4731c46f6bc6d6b46b6ac696a46bac7a31b7a76af9f185a7e7461e6d9de645315f9115d95e3f8f1558be2c49e3585e2441e1d85105831,
    0x1ebf4fc3ecfabe8f83def73d8f4bccf2bc8f13c4b0bc0f,
    0x7dfeff9fdfffbd7f3ff6d379ee5b87d7b27cf7,
    0x1f9fc7e9f67d1f27b9ea799f8fdbe47d3e07cbec4bbecf71e6f93da79120f73d67811af49d8f6114453ce043ce4300a433ca7280242bc6021c401bc2013c0003c07,
    0x1fdfb7ddf37aeef7ade9b9de578ddf775d975dd37fc3fff4117e43dfdc330efcf79c23036e7f7417077d302f0d0478d92c097378900509f1c09517c501d4350641f0c011,
    0x688f93c4923a4e1367d1f07b9dedb1ea7a1e4792e07f0783e8743e05c7c8f6159e86d0666b8f2189b0171966b86c3498aab04e6a8ea131a8129a610a866a0e41cb82698e2101a0188dc1,
    0x777c5f38ade37,
    0x1,
    0x7f8fe7d9ee799d6719be6598e6197e5d9665594e5193e4d92e49916439e501c,
    0x7e5,
    0x1fdbd6edb96ddb56cdab6a5a768d9f6759b665976559363d8d675fd455d3745cf7ec3902df7025f101dc57b4037ac017a4270,
    0x7e9f27a9e2769d2729c26698a5e9,
    0x7f5de7d5ed739b66b9e56999e5b9,
    0x1fa8861184e,
    0x1febdaccf132dad39ce7b94e3374c76159b364d73,
    0x7a6e1b66d1b26f8706f06e6e8781b1b61a9a66d0626c8606c06e169a8bb0566a862b49a8141b839870339a415aec3a0da188ea469caa78ceb60cc62854950fef40c46104c3,
    0x6d6a5a768d9f6a69965d956645365c516545113c57e3d8d12d8b1,
    0x7a2e0be7d8bc7d0a67c8b0289ee279ec261ea251e8298927908e731e228088778867709a209d825092238807308a2,
    0x1fef37,
    0x70bc9eaba1fe091fc07afa089f80d8207c81e7c02e061ea059e8041e60880a778087700474808010027,
    0x1fdfd7edf97ddf57cdf17bded79de578de177ddd76dd9755d3785b3b6d8d615b75cd6d1bd4b70e836,
    0x7e4f13a4f9744fbba5c12a5f3a25797ed717ea61545417ca397eb314a5217cf19741fb301096a101661,
    0x7b4e51bc,
    0x1f93c4c12c4a1244811c4610883108419024,
    0x1df35c,
    0x1,
    0x1fd7d5ed795dd755cd7f8c56f5b56b5bcbfca5675956157d5d5f71b5657f05d7b055535cc115ac0f5940d52d610255f01d5b05c17b4429e154d005490,
    0x1b96c5a968591605715a532465,
    0x575,
    0x4caa982a,
    0x71e3f89e,
    0x7e1f07a1e0761d0721c06e1b06a1a066190621805e17054d6874360561c0d21b0d01a8ce198cc14012738c63000c5,
    0x1,
    0x52f23c67,
    0x7dfeff9fdff5fbfebfa7e1f7fc9f2dc5f,
    0x1,
    0x6508417087d30f4a5edc8f0ccaf22c1fe7489077914170921c83c4f91e2f8710c43e,
    0x1db34ccb30cbb2c5b32aca326c9322c831ec733e36b246f0f836314bd8d89c8e6388d4c719a34b163430cb598ec50ccc40ce638cac1886c108410a02c,
    0x1e737cd731cbf2dca727c8f1dc6715c4f0fc2f07c1703c460b807058,
    0x1fb3cceb38c8b0cc0b204,
    0x7fcf73bcdf35cc72fcaf3feefb9ed7b1e07314,
    0x1f37ade376dcb6edb368d9362d835ed6b56d434cd2346d0b429,
    0x7fdf77bde777dbf6bd9f65d8f61d7f5dd6f7f0f419decb925f772d4b3257712bca54b49f8a493d9ca5276232849987c978475d26c95894d72375322f512348361f4192c872,
    0x7efd93cfebf8fdbfe5bbfa51b50473d4f4bccf,
    0x7f5f57759d655855b55d4d506475,
    0x11a84afb82a,
    0x1febdaeeb9adeb5aceafab6a7a8e9fa5e91a2e83a,
    0x1fbbce8a72cc32cc9a929931ec731ca5b16a3b3e35286cf0fa3,
    0x65ed771db76bda767d9763d875fd4f63a,
    0x7ebeaf6bc2dcb51faf,
    0x1feff7,
    0x76cd32eca326c831ac6314c4b0ac23120380a0,
    0x1b729c9f23c7f1dce6dbcc6d9ca6d5c473f21f19af4b100f2d0a4270ec8fa943928c3725fc9ad49d01651fccaf25c0ff,
)


def unpack(number, bits):
    values = []
    while number > 1:
        values.append(number & ((1 << bits) - 1))
        number >>= bits
    return values


def kernel(aff, words, s_out, deg_out, table, block, mid, arrived, far_words, mask_rows, far_mask,
           col_sums, row_sums, row_shares, col_shares, near, far,
           load_sem, word_sem, leg_send, leg_recv, hop_send, final_sem,
           row_send, row_recv, col_send, col_recv, pair_sem, out_sem):
    row = lax.axis_index("row")
    col = lax.axis_index("col")
    me = row * SIDE + col
    partner = col * SIDE + row
    y, low, core = row // 4, (row // 2) % 2, row % 2
    high, x = col // 4, col % 4
    on_diagonal = row == col
    size = block.shape[0]
    chunk = size // CHUNKS
    groups = size // TILE

    def rows(n):
        return pl.ds(pl.multiple_of(n * chunk, chunk), chunk)

    def group(n):
        return pl.ds(pl.multiple_of(n * TILE, TILE), TILE)

    def place(cx, cy, cc):
        return (cy * 4 + low * 2 + cc) * SIDE + high * 4 + cx

    def mirror(device):
        return (device % SIDE) * SIDE + device // SIDE

    def to_partner(src, dst, sems):
        @pl.when(on_diagonal)
        def _():
            pltpu.make_async_copy(src, dst, sems.at[1]).start()

        @pl.when(jnp.logical_not(on_diagonal))
        def _():
            pltpu.make_async_remote_copy(
                src, dst, sems.at[0], sems.at[1], device_id=partner, device_id_type=LOGICAL
            ).start()

    def wait(ref, sem):
        pltpu.make_async_copy(ref, ref, sem).wait()

    def load(n):
        return pltpu.make_async_copy(aff.at[group(n)], block.at[group(n)], load_sem.at[n])

    to_partner(words, far_words, word_sem)

    kind = (((high % 2) * 4 + (y + 4 - high) % 4) * 4 + x) * 4 + low * 2 + core
    for outer in range(16):
        @pl.when(kind // 8 == outer)
        def _():
            for inner in range(8):
                @pl.when(kind % 8 == inner)
                def _():
                    sends = unpack(SENDS[outer * 8 + inner], 17)
                    relays = unpack(RELAYS[outer * 8 + inner], 10)
                    for n, value in enumerate(sends):
                        table[n] = value
                    table[CHUNKS] = len(relays)
                    for n, value in enumerate(relays):
                        table[CHUNKS + 1 + n] = value

    relayed = table[CHUNKS]

    def leg(n, carry):
        entry = table[n]
        relay = place(entry & 3, (y + ((entry >> 2) & 3)) % 4, (entry >> 4) & 1)
        slot = (entry >> 5) & 127
        number = entry >> 12

        @pl.when(slot == DIRECT)
        def _():
            pltpu.make_async_remote_copy(
                aff.at[rows(number)], arrived.at[rows(number)], leg_send.at[n], final_sem.at[number // 4],
                device_id=partner, device_id_type=LOGICAL,
            ).start()

        @pl.when(slot != DIRECT)
        def _():
            pltpu.make_async_remote_copy(
                aff.at[rows(number)], mid.at[rows(slot)], leg_send.at[n], leg_recv.at[slot],
                device_id=relay, device_id_type=LOGICAL,
            ).start()

        return carry

    def legs(first, last):
        @pl.when(jnp.logical_not(on_diagonal))
        def _():
            lax.fori_loop(first, last, leg, 0)

    def hop(n, carry):
        @pl.when(n < relayed)
        def _():
            entry = table[CHUNKS + 1 + n]
            source = place(entry & 3, (y + ((entry >> 2) & 3)) % 4, (entry >> 4) & 1)
            number = entry >> 5
            wait(mid.at[rows(n)], leg_recv.at[n])
            pltpu.make_async_remote_copy(
                mid.at[rows(n)], arrived.at[rows(number)], hop_send.at[n], final_sem.at[number // 4],
                device_id=mirror(source), device_id_type=LOGICAL,
            ).start()

        return carry

    legs(0, CHUNKS)

    def start_load(n, carry):
        load(n).start()
        return carry

    lax.fori_loop(0, groups, start_load, 0)

    @pl.when(on_diagonal)
    def _():
        def own(n, carry):
            pltpu.make_async_copy(aff.at[group(n)], arrived.at[group(n)], final_sem.at[n]).start()
            return carry

        lax.fori_loop(0, groups, own, 0)

    for t in range(groups):
        tile = col * groups + t
        bits = (words[pl.ds(tile // 30, 1), :] >> (tile % 30)) & 1
        mask_rows[t : t + 1, :] = bits.astype(jnp.float32)
    col_sums[...] = jnp.zeros_like(col_sums)

    def prune(n, carry):
        load(n).wait()
        mask = mask_rows[:, group(n)].T
        total = jnp.zeros((TILE, TILE), jnp.float32)
        for t in range(groups):
            lanes = slice(t * TILE, (t + 1) * TILE)
            kept = block[group(n), lanes] * mask[:, t : t + 1]
            block[group(n), lanes] = kept
            total += kept
            col_sums[:, lanes] += jnp.sum(kept, axis=0, keepdims=True)
        row_sums[:, group(n)] = jnp.sum(total.T, axis=0, keepdims=True)
        return carry

    lax.fori_loop(0, groups, prune, 0)
    row_shares[col] = row_sums[...]
    col_shares[row] = col_sums[...]

    def share(n, carry):
        other = (col + 1 + n) % SIDE
        pltpu.make_async_remote_copy(
            row_shares.at[col], row_shares.at[col], row_send.at[n], row_recv.at[col],
            device_id=row * SIDE + other, device_id_type=LOGICAL,
        ).start()
        other = (row + 1 + n) % SIDE
        pltpu.make_async_remote_copy(
            col_shares.at[row], col_shares.at[row], col_send.at[n], col_recv.at[row],
            device_id=other * SIDE + col, device_id_type=LOGICAL,
        ).start()
        return carry

    lax.fori_loop(0, SIDE - 1, share, 0)
    lax.fori_loop(0, MAX_RELAYED, hop, 0)

    def share_in(n, carry):
        other = (col + 1 + n) % SIDE
        wait(row_shares.at[other], row_recv.at[other])
        other = (row + 1 + n) % SIDE
        wait(col_shares.at[other], col_recv.at[other])
        return carry

    lax.fori_loop(0, SIDE - 1, share_in, 0)
    row_total, col_total = row_shares[0], col_shares[0]
    for n in range(1, SIDE):
        row_total += row_shares[n]
        col_total += col_shares[n]
    near[0] = row_total
    near[1] = col_total
    to_partner(near, far, pair_sem)

    wait(far_words, word_sem.at[1])
    for t in range(groups):
        tile = row * groups + t
        bits = (far_words[pl.ds(tile // 30, 1), :] >> (tile % 30)) & 1
        far_mask[t : t + 1, :] = bits.astype(jnp.float32)

    def store(n):
        return pltpu.make_async_copy(block.at[:, group(n)], s_out.at[:, group(n)], out_sem.at[n])

    def finish(n, carry):
        wait(arrived.at[group(n)], final_sem.at[n])
        for t in range(groups):
            span = slice(t * TILE, (t + 1) * TILE)
            mirrored = arrived[group(n), span].T * far_mask[t : t + 1, group(n)]
            block[span, group(n)] = 0.5 * (block[span, group(n)] + mirrored)
        store(n).start()
        return carry

    lax.fori_loop(0, groups, finish, 0)
    wait(far, pair_sem.at[1])
    deg_out[0:1, :] = 0.5 * (near[0] + far[1])
    deg_out[1:2, :] = 0.5 * (far[0] + near[1])

    @pl.when(jnp.logical_not(on_diagonal))
    def _():
        def sent(n, carry):
            wait(mid.at[rows(n)], leg_send.at[n])
            return carry

        lax.fori_loop(0, CHUNKS, sent, 0)
        wait(far_words, word_sem.at[0])
        wait(far, pair_sem.at[0])

    def hopped(n, carry):
        @pl.when(n < relayed)
        def _():
            wait(mid.at[rows(n)], hop_send.at[n])

        return carry

    lax.fori_loop(0, MAX_RELAYED, hopped, 0)

    def share_out(n, carry):
        wait(row_shares.at[col], row_send.at[n])
        wait(col_shares.at[row], col_send.at[n])
        return carry

    lax.fori_loop(0, SIDE - 1, share_out, 0)

    def stored(n, carry):
        store(n).wait()
        return carry

    lax.fori_loop(0, groups, stored, 0)


def on_device(affinity, keep_words):
    size, _ = affinity.shape
    groups = size // TILE
    words = keep_words.T
    vec = pltpu.VMEM((1, size), jnp.float32)
    dma = pltpu.SemaphoreType.DMA
    symmetric, degrees = pl.pallas_call(
        kernel,
        out_shape=(
            jax.ShapeDtypeStruct((size, size), jnp.float32),
            jax.ShapeDtypeStruct((2, size), jnp.float32),
        ),
        in_specs=[pl.BlockSpec(memory_space=pltpu.HBM), pl.BlockSpec(memory_space=pltpu.VMEM)],
        out_specs=(pl.BlockSpec(memory_space=pl.ANY), pl.BlockSpec(memory_space=pltpu.VMEM)),
        scratch_shapes=[
            pltpu.SMEM((CHUNKS + 1 + MAX_RELAYED,), jnp.int32),
            pltpu.VMEM((size, size), jnp.float32),
            pltpu.VMEM((MAX_RELAYED * size // CHUNKS, size), jnp.float32),
            pltpu.VMEM((size, size), jnp.float32),
            pltpu.VMEM(words.shape, jnp.int32),
            pltpu.VMEM((groups, size), jnp.float32),
            pltpu.VMEM((groups, size), jnp.float32),
            vec, vec,
            pltpu.VMEM((SIDE, 1, size), jnp.float32),
            pltpu.VMEM((SIDE, 1, size), jnp.float32),
            pltpu.VMEM((2, 1, size), jnp.float32),
            pltpu.VMEM((2, 1, size), jnp.float32),
            dma((groups,)), dma((2,)),
            dma((CHUNKS,)), dma((MAX_RELAYED,)), dma((MAX_RELAYED,)), dma((groups,)),
            dma((SIDE - 1,)), dma((SIDE,)), dma((SIDE - 1,)), dma((SIDE,)), dma((2,)), dma((groups,)),
        ],
        compiler_params=pltpu.CompilerParams(has_side_effects=True, vmem_limit_bytes=47 << 20),
        name="exchange",
    )(affinity, words)
    total = size * SIDE
    left, right = lax.rsqrt(degrees[0]), lax.rsqrt(degrees[1])
    normalized = total * symmetric * left[:, None] * right[None, :]
    return normalized, degrees[0] / total


def solution(mesh):
    in_specs = (P("row", "col"), P("row", None))
    out_specs = (P("row", "col"), P("row"))
    return jax.shard_map(
        on_device, mesh=mesh, in_specs=in_specs, out_specs=out_specs, check_vma=False
    )
```

```python
import functools

import jax
import jax.numpy as jnp
from jax import lax
from jax.experimental import pallas as pl
from jax.experimental.pallas import tpu as pltpu
from jax.sharding import PartitionSpec as P

TILE = 128
SIDE = 16
CHUNKS = 32
LOGICAL = pl.DeviceIdType.LOGICAL
DIRECT = 127
MAX_RELAYED = 71
SENDS = (
    0x1fff07bf83bfc1cfe0dff06bf833fc18fe0bff05bf82bfc14fe09ff04bf823fc10fe07ff03bf81bfc0cfe05ff02bf813fc08fe03ff01bf80bfc04fe01ff00bf803fc00fe0,
    0x1fff014073dfc1dfe0e7f06ff835fc19fe0c7f05ff82dfc14fe09ff054ad65fc11fe087f03ff81dfc0d5f167f02ff815fc09fe047f01ff80dfc04fe01ff00bf803fc00fe0,
    0x1e189a7f80c0e942a1f998c8907c5e240c4b95980093a56311e1d928c068542acf181d0c8b080e6366e121c8b8b438701a271434069ac28441243082b0188418ea0225001,
    0x15951fff8041c97373f7f077f812507cfe0dff050b4f5fc12273cff063f82dfc0301430e1bc74ebfc0c1739ff047f821fc0efe06ff0143cd5fc08fe000021ff8021064fe0,
    0x1f7f077f839fc1b780d7f065d031fc17700b7f055b00403b46809ff049783e93915a087f03d48080eae4c06ff030f00002ab32057f024a011fc071e037f0144807fc01020,
    0x1fff07bf83bfc1cfe0dff06bf833fc18fe0bff05bf82bfc14fe09ff04bf823fc10fe07ff03bf81bfc0cfe05ff02bf813fc08fe03ff01bf80bfc04fe01ff00bf803fc00fe0,
    0x1482cdda0bcce55622eb1950a99a0bb2246e2f913f836ba53522d2894510b2964f422c22938e8ac824c34281b90c0a44032b282f88f1c70944a41fe0405b18408a1640022,
    0x1703477f830097b392e7f06bf833fc17fe099515bf81a3c552b2f016d3f80c187121228527c1421fc0b1527ff024448814e70f267f0480742006afe00013a3f8040043fe0,
    0x1a06b653876ae29fe0f8c9d878eeaa351a3984b45184dfc0f42127f03858fc226c103901b34f87a1e6a0a30ff02ce06086230ecd049a0a0700e6206c29389c10f81280040,
    0x158957ff80a4d3efe050a377f839fc1bfe00807543db5fc19fe0c7f03846affc130b6b7f053f825fc11fe030c0c3f80610cffe06ff033f813fc08fe000031ff809fc02fe0,
    0x1fff07bf83bfc1cfe0dff06bf833fc18fe0bff05bf82bfc14fe09ff04bf823fc10fe07ff03bf81bfc0cfe05ff02bf813fc08fe03ff01bf80bfc04fe01ff00bf803fc00fe0,
    0x1fff07bf83bfc1cfe0dff06bf833fc17fe0b7f06135c20154fe09ff04bf823fc0ffe077f037f819fc0bfe057f027f811fc07fe037f017f809fc03fe017f0405fea78e0fe0,
    0x14ff07841fe7f965402ff0301afa96144e0e2284d20348612400c1e8447b36538f340b90e38b020520a2006908080bd63e081c0a88b8c12ce2a0414030886401c20e000c0,
    0x1d9e098241009f9157c1a0fd1474593e4119950dcd4644436137e863d4ac7810f40f780e0bc8c5a282b1d15070b02ed218230303840b80dca0c240f18ff00824420020031,
    0x1f7f02511fbfc1c742d7f065c0b657d86c2f8ed5d98adfc15602a7f04d68a5fc1154287f03d3884276e4626ff030f097fc0a30247f00403cffc062422ff0106087fc00042,
    0x1fff07bf83bfc1cfe0dff06bf833fc18fe0bff05bf82bfc14fe09ff04bf823fc10fe07ff03bf81bfc0cfe05ff02bf813fc08fe03ff01bf80bfc04fe01ff00bf803fc00fe0,
    0x1f7f0189218779dfe0e7f06ff835fc19fe0b7f057f829fc180449ff04bf823fc10fe07ff03bf81bfc0bfe0f82a2bf82e028018c4ff023f80ffc05fe027f00ff805fc01fe0,
    0x1bff05bf82bfc1347cd8f0f86469fc12fe08ff03bf81bfc0b2fc00067c0d32302afe02074c007de1029fe06010a3f80ffc06fe02ff0703447fc1d03e17f0600c43fc1a015,
    0x1797f17f805fc110c6e0696093183bd506250cf5c8b1027d61ecf8ee1c3bbc37941acd8291033ba2b9316cd08e404b32068e10c081f2c3b2407290ac685e18230003c300c,
    0x160f5fc5e32598a47f806478d4ee559d21cb14607f81c1518014a1362487e4419c1fc68e66c672624fa17c58c6544f0c298f0fc20342107c619870dc8971942704098001c,
    0x1f18cdd0b3473953ace16cd0db3267922ecd9eec7f826578d24cc1beac8b1c4b8ffe0b17ea3f82053aa16d60ce184b522f8716c286e0ff83e17e210c208e802b3a020102d,
    0x15052f58f4e10b5fe08ff043f81bfc1f45967f0717772a1be3d9ba56a3f82891ba51d9206e12f4dfc1649d7196eca647fc133bd5926bcc74a35a91fd2054884f4208a005d,
    0x1784ad880960eb51e26adf30cb7e5e41fe0f15928bb7a52492cde1391d03b64a4828dc16ecc58b43e5214230cd14836847b00e288ee905b72264310d708e88236e224002d,
    0x168d5fcb4e658721da58c5d04f62507e2538131bc275c407d21360e1a8ef8a217c1d348b1ec5cd059da1533891841f4820791133107603cc415d70b31841d814c00075013,
    0x1508c543a8c1702fe08869c832be1e0f0aa6049b42283fc0b06ae88d2023b8175e1c1d84d241281fc18161d03d1c0aac0b43048701d5c504a0a74121200d4c40720a100e1,
    0x1fff077f839fc1e136d7f06c35aa20d9fe0c7f04ff8281cd1fe080633ff81614d709667f027f811fc160763ff048159c2ca4fe050430bf80c0ccd03628130c058200c0fe0,
    0x1b92d44429dfc05fe07aaf6479989bcb0aaf8fb0bf83c36c738e0ff06071942f561a6000dd061ba32d3166305d4851b82ed0126d8ab1053b426cd0e6a87b24219012c3046,
    0x1ebf778c6b6f5d70b6cbc77dcf840c7c71ec3b769bf8208766de6ff0140daae5d46be9b770005e2d5d269e7b27419798bdce61e52b72d4f9095c949e39b718cf8835c31be,
    0x1f8dbf441ea32fcfe0dff06bf833fc18fe0bff03832edfc14fe0f06dc831e7fc10fe0604dbff8100f710a75ff03421ce1ae400b283babf813fc06fe017f007f80606e0fe0,
    0x1a073f05df0357915730c2d84dea316f199b957c445e42d6a09780a58815dc25600172082e81c1a217d11b4875ec3ed80c3f0f14055cc2ece117e09108269416d6002301b,
    0x1fb5fd8bafcd3fc62fb91ded7bc80af95afeb3fd563c40b5456f88ddcd3bf4c3f04afc2dfbd1be4a7ed42f728fb103d69bea32f41df9c9bcc4be516f483d8c3bc20be004f,
    0x191d7d117fa3cf039fe0e3cc2ef434ff117c8c3b426f02cfe0f740c79047ec28e307f4ff06c35ea20e5fe08873dc2ddc18ef0976053880fc005e1fe05033ac1dcc00e7037,
    0x1ea6a27f83e4b984043ff05cf928bf163c4f11e54e924b713384c81e44d90dfc1034427f00ff805fc0f3240ff034c138968e64807f02cb9368e8a2c4d22a2099183e85144,
    0x190c77c6476643e171a9524cc61c2ddd355c170c4651a54bc2f5b950c03c9425da25548875885504421fe038c2acb64a20af1552070b03d6815a3095103083f80c09d901e,
    0x1f8bf2428bc42e408ce8fbecb1ce12c206ce0ebe8a1f232f6267514d5491f02ae5006604a5089cc3f52207b89bc471e622e312a807bb459de1aeb127083d2039ddfc000c7,
    0x17842785517fc1a134d953840f3aa17f5dbca45f166ec89774fba9c5e0451208944bb20124c3d0009920d489a594165c616d3fb6165a8cec4008829b30f5c02d061567014,
    0x1f1ea34897a7685fe01ff07c68366a8b1a5c98a4489305a80fe0b15a3c69101aae184a11a0801742fea16498da703be42e89124809a542bd81e870a4304a10092e0b61004,
    0x19a42e7f82dfc15fe09232fc5f6288b4fe07a129bf81c80be6d969f2f1a65874a5fe01ff06996566cb76190ff075055464bb3b54972e0dd5048a0fe038f2c04d4808a2055,
    0x1e16b34c27e77381c6f1bcdc61ba6b35166d98cc851b453335cac93cbd62840a861c98abd2c296c3f2c50aa0dc8c525c1f2a48a4a3d04326036c732a409b10118a2f40049,
    0x1f1133bf83840c319b6842fcbd8814e5057d0f3080df034dd2965832802ecc19fb2763822d80fc200b923698932bf8241cd72168863547d9e10d41566033403d9204c8076,
    0x1f898e7f83a22300ecf07b4c40364e8b0cea0ce3c33222f8e0ac48ae301810278608c686a141b381e38241bff010132bfc0302cd048d878440b0a141005e1c30640621021,
    0x1b9a6f46c6a65a40549986e8b7625db929d7966e09f5c55b425d6146b48f544dbc151d980a4875049a71ddf8777835a015c61bd2906dbf824402315d589088474209a005d,
    0x177f033f83e8fcafe0f22f1ff80dfc1c38eea1f64dbb483d832eb9ef58bbaa73d428e1ff0488ba667c2fe0816f6df2a25b4f1ae691f2c4b9237c0fe0407f14238807c100e,
    0x1c4054ff83469dc77a8ff07cff9ffc0cfe0c98774efac59d737ea93750d793fc1231e80e76dd69c31cd21e2ff02c779421de0d640570ff805fc0709e0800981f81fc0401e,
    0x15ff065ea30c703fe0f0f86c832c5b941eca95e1419e453810cb893e34733a3a0c1ace0c85c801e438918cfa1a1c5b1c3f931c050ee40580c3788120001b904b34220210c,
    0x1b897f8345c45bd17ab115d45ee80df213b88c5f0569e195b13a6895fc2fc809f811a5104cc1ff238300ba5835302692117a05140250407ce054607a180508168a056001a,
    0x1d0293ff83e97f84af5ff0551bfc8bf442fe81a27f83883e7fe0d9efc8ebf273f036fb19fb8cbe65fe5fe0894fb0abc7fc02fe0b80907f801fc0824f691f986bd437e40ef,
    0x1da97e80daea1f8fe0aa77a7f82899ff49f9247f91fec10fd43f7a07f0ffda7df93bf61c7ccdfd469f031f4187b8afe204eb27f31178bf8083de71ff0ff01467c1fc0313f,
    0x1f0ae3c7b33fc16fe0d09e53f827fc0c0ecfb2a243321fc1d7c4e30a1c2336ba8efe0504e61c9080f8bfe0baba23f80dfc0102caaaa45610bfc03fe0924a0bf81a6e80fe0,
    0x1ebb2796530291f0fc998297f836dc943f58962c8e574c49c0dc8132bccd5c3cac255cab22c855220a8155b85634460e14aa0d820040c356c94820b53006041d6a5480015,
    0x1d21bf0620c0335168a05a90127a0e922e7c9ebb4190bfc03029c1abc4522c5efb143f88c3c91c3fc0a227f07c2469c1fc0b024986c384a202ae2009605c20420e0b17043,
    0x1f7f024260c317dfe0202673f837fc1afe0cff063f82ffc16fe0aff07c0d29fc13fe097f047f82005effe077f037f819fc0209b5ff02bf811fc07fe02ff00ff803fc00fe0,
    0x1509cf1a929fc1b664f0de698125fc0ffe0ca9a61712ea29d280b26a55413e46f346477f0411122828bfe0105cb4f9184e88fe048ea18690e1e85fe0200a002107fc01fe0,
    0x1f146aff832b0bb6f54ff069ad6cacbf0bdaaa29ff81a35385b5a292dd657835a5fe09262cd4d6088b14f507f03d355c74bd07d61b2a11d4c5ca41b550648c654401a1175,
    0x1eff0502279fc1bfe0cff063f82ffc16fe0aff04ff823fc1210e6ff0402b5433460ca5ff024897e23c5fe0793b0ff80e46ce06ed0aab0237c0242fe00ff0201b41fc04069,
    0x1d856608dfc11ecfe09046701f17fc0f13740a5e44f4e20e609728165847542cc90d6f8649017060cc2017b85483f802019d395a932e8856819b30fd8032c4375c09ad0bd,
    0x1303d6cd1f42f95327207b7813be8213307727a44b9fa6e102c7e1984853305e17200b0fbb499e83aec24778dbac81d42ae81c7c87f9c51d217850e7186b8419c406e0007,
    0x189a6e82f980d5f2f691230416a044de2d67903087e5c3cdd2b668e370a59634db276001564959430d823648b35c859028d61f6389354758a20d41b620734c658614c60d6,
    0x1f0387ff81c62c5266eff073f837fc1afe0cff00412b1fc17fe0b7f057f829fc13fe097f047f821fc0ffe06ff033f817fc0afe04ff023f80ffc06fe027f00ff805fc00fe0,
    0x1eff06d65b9fc1afe08a6363f82dfc15fe097f043f81ffc194f6f031fc3799fc0007b69f35d0d97fc143f647f0080f5405d33d63ff038d5925cc6fe027f00ff80a44c1fe0,
    0x1f9c870631dfc1d1c099fa2bf82c4a1238481aa3cc1283a1b02f696a2c99222a152873ff0684012468102b40da60300a2697080185a13f8180e020e430186403fc42e0064,
    0x1c1e0b19d6c703f431a1a0f8fc64603d3918160f0cc5c503b2b16930e89c56403923150e0dc7c522c351d140a0cc6c4c24311712860bc444810270b110308c1c420420031,
    0x1e7f06ff835fc18fe0b7f053f825fc19607e83f43f81ffc175c777f037f83ecaebfe057f05551ca1b69fe047f04d31fcaee302a082b44f9cffc0c36737f013f8003ee2fe0,
    0x1f7f07d8ddea4fcfe0dff0757df5fc18fe0b7f057f829fc13fe097f047f821fc1955777f033f817fc0afe069e3a7f811fc174973ff01bf80bfc04fe000938ff805fc01fe0,
    0x1fff07bf83bfc1cfe0dff06bf833fc18fe0bff05bf82bfc14fe09ff04bf823fc10fe07ff03bf81bfc0cfe05ff02bf813fc08fe03ff01bf80bfc04fe01ff00bf803fc00fe0,
    0x1fff077f839fc1afe0cff078b66ffc16fe0aff04ff825fc11fe087f03ff830592efe06ff033f817fc142dd57f027f811fc07fe037f017f809fc03fe017f06c4643fc00fe0,
    0x1e10f7c43b06a3e241a968f4806e23db1c1d09ee460664e36101686ed0304e17a514388f8c8205c2e230e32089881216222908d5068c0105016210633028bc08400a6c001,
    0x18981d8dcf00d9ffe0f7f077f81c5c742f3e7f04cb4d84c7bfe0d7f040a4f3fc0f27350d1b48cce24691739006dff82bfc050f35ff0183d11fc000741ff01034c5fc01033,
    0x1fff07a003bfc1c7e0dff069e833fc18760bff059d029fc1372097f045c02a7b8f6e081ca39a8022bad66067f02d6015fc094e047f01d200dfc053e027f00c7005fc00020,
    0x1fff07bf83bfc1cfe0dff06bf833fc18fe0bff05bf82bfc14fe09ff04bf823fc10fe07ff03bf81bfc0cfe05ff02bf813fc08fe03ff01bf80bfc04fe01ff00bf803fc00fe0,
    0x1dff067f82ffc1d662faa957f83c9e58562e2195120ac725a0ed919930c09c4e53fe08ff024a8880fa824287f018708a1a4ffe0104904209bfc0bfe057f00ff80e1320002,
    0x1cb917c5f70e05e5d2bb61716c96113b15dab01694ca6b856492827144fc9a7c4f352e886b0b4925c4001357f0383f6819a81d290569c6c8a3c4605d20910c2c841441012,
    0x1d1482012a2338402af188f0d04203db321a92864c05c2797261e948b04b304a34201b0e8b4302432331c1306e0c01a02a250607898ac48541e3f084000824304e1622061,
    0x1fff07bf83bfc1cfe0dff0083775fc19fe0c7f05ff82dfc15fe0a7f00c07e7fc12fe08ff043f81ffc0efe06ff033f817fc0afe04ff023f80ffc06fe02ff013f803fc00fe0,
    0x1fff07bf83bfc1cfe0dff06bf833fc18fe0bff05bf82bfc14fe09ff04bf823fc10fe07ff03bf81bfc0cfe05ff02bf813fc08fe03ff01bf80bfc04fe01ff00bf803fc00fe0,
    0x1f9d3f7f839fc1bfe0d7f063f82ffc16fe0aff053f827fc12fe0c895c7f80828d0fe07ff03bf81bfc0cfe05ff07895d5fc09fe047f01ff80dfc05fe01ff00bf803fc00fe0,
    0x1fff07bf83bfc1cfe0dff06bf833fc18fe0bff05bf81807e00e0aff053f827fc12fe08ff043f81ffc0efe06ff02ff8041b0afe04ff023f80ffc06fe02ff013f807fc01fe0,
    0x117f06c148609f537cf300683678ac01fe0ca807d842e941d5900000e14c2688164f089e0511c1e70124507180410418580d370595028c4124c0823038f0187c082405070,
    0x1f7f07628b9fc1b862d7f065f8b1fc177a2b7f055b8a9fc1362297f04568a1fc0f52277f0352899fc0b3a257f024d891fc072c237f0148089fc0318217f0043081fc1f086,
    0x1fff07bf83bfc1cfe0dff06bf833fc18fe0bff05bf82bfc14fe09ff04bf823fc10fe07ff03bf81bfc0cfe05ff02bf813fc08fe03ff01bf80bfc04fe01ff00bf803fc00fe0,
    0x1fff07bf82a067cfe0182c6ff833fc1d5ecc7f0691b2ffc1236cb7f03463160274fe09ff047f821fc0ffe077f033f815fc0004c4ff023f80ffc06fe0080c17f809fc02fe0,
    0x1c122b83e27fc12399b902c09654111c175fb463ff8082129fe0f3160ff836a98b1b9283420666c1c350748850f437b481992fc6820d03f0e0422fe0300087f8180180014,
    0x1f9d9b4433c6e6c0ece9a9c543ec1b860ace179c090f65a6f4afa01a3878f44e7228bc909ac60c7fc0a3ef983e041b30326938fb8b99c48d067e524fa879800b0443e4083,
    0x1b966243dca14fd17cb1461056ea498ffe0a106040624399f07488d61c35e0318dfe070b6705718299b13c509678150021fa11c1802643f1019980bc30464c1704098b01c,
    0x1103ca7f81847bc16b37f02c6b6a878a14dc9587c80304a0d188408ef8682e3e0e20cb0d814436832110cb206ef440261e070ac90580ff81e169b0608008042b400bba000,
    0x1fff07bf83bfc1cfe0dff06bf833fc18fe0bff05bf82bfc14fe09ff0001665fc11fe087f03ff81dfc0dfe067f02ff815fc09fe047f01ff80dfc05fe027f00ff805fc01fe0,
    0x1f21ea193b483bc462f9d92c498e9bdb3a22a5f64e0ac7fb7362a8dd30a36673b4302899ec8b8a063a20c6e9993898b04e4a0aa4899108b5e57a016d683d0c308c37a1002,
    0x1b9511bf82c65bf47da986904fe65dbe45d9166f4aca255bb23270d170f75a2c5a3bd2867a03c941c5937d7936e0bf583db403310478027d635a107b4856c0574e0443019,
    0x1f8cf50a8fa466602a204d0802bc23d3283083d4898f64270223e01f3c78f43a6e1a307f03060f2326b143c0a9a840ee22690e3b059a028ea126708388399418da0a63003,
    0x1d7f07c6eb3fc15fe0a7f07866a5fc11fe0d8853ff8301d4cfe05ff0745eac1948fe098555c0d8ffc1c15a804517f81a0d4e0fa4825282e8c0cc2fe007f010058605c103a,
    0x1f96d7a33b8dbc8fe0db5f6a23b2d3d882ebb3f4c52ba47567ceab1f51d3a4c3d168e828f3d639c0b4d46e2ff02d13986fca34e495f1c8b8c1fc40ee1ff007f8040bc002e,
    0x1f4277c5ebb01dc65edbc74c55f4edd85fe7873dd67acbdd547e6063d10796397909392171836c3fc0e09781c744bf881d650376937285f92054813e38b70c0f8009c2017,
    0x1c1486c52ca1bf712b99ce3419ec461510b915e03f8182f1022c713e7c58282e0a16c58ee1c4310338f0eb084c7828380b6908b189e101ac4139d08f883868100c0af9020,
    0x18146abf80ffc19172611693f83418f81329053b47f5e10f711240417c3dd22dbd0d73031702de215760b25823d4248a04f4072f037ec25dc102207d07f04c0c8600e103d,
    0x1fb1ff9d3c7fc1d70fe2ffedb3f2b7f76afb2afe8888e47d5202a29fc963f03e531c28a7fc133da87ee18278893103d01a41fe0283924dbc1fc0a04259af988bc8024218f,
    0x1f397fd87faddfc5dfdb47d7f834c9f4fe097f047f82ec5eefe0b2e7b3f826a9e9fe0c1a5c127de89ed3ff3ff06496d675ea31f2003a0afcdfc03fe017f0146fc3fc00fe0,
    0x12ff075293e8b99484f21e6119348a97444e20e5909367f943e41ff04cf12a829138491da40d11e6a80fe0698a38b9165a8c284494a2889103e871a430aa1041041681024,
    0x178b0f86c7a809c434d1d26cfd1431bf0dda1b258e5246493334818244bd18588e2b46850ac9d12102725440f214750c2c8111518a2642c44189809100025c1c480035031,
    0x1f93b3c60b84adb147d0fb64c1f032d52c7b0ab5c313c42ec0c6a07b48a9ce4b4d24798ebac21ba37c60a4805b2889dc2fc214a88dba479c006480662ff010018622e1024,
    0x167f06084fa80f51f3d010940e367cf41d3c9e3c86cee70ff277b1b39bf820286f1938993f0151c5cfe23717f0345cc001131f73881ac4cc2008a1132103a05dd201830f7,
    0x1fa6ae9097abf393e597f03ff83c96b638540ac3bf83892b5325da2ab3f8307ea9fe058484ca96e76b0205a17ab4bb4ffc0a1a5890a943949fc0308517f004094c0a00fe0,
    0x1f232e7f83a80b5fe0c1e2cbf815fc010563ff01416e874a2fe099b283f82268bc6198182fd0d5c5cb73d5db148c0e34c12f35558f2b4a55230ac1f54062985d6c09240b5,
    0x1a11cf0a8adfc06fe0503e8c0bfa325e145d8b968a0be56d9262889cdc90b02a55222208ac080a6264f1e2587cb870a41a4c142685924389013270a2101c9420821240042,
    0x138e5e02fc82ced0b370a6d817f434d529960a4fca59625332594837941cd41d31219c8c340666e2cc3053a0937875a41cdd1360015f0359011bb0961034981e5e08c1019,
    0x1482f796a66439d569fabcb06317fc0202e88ee28531e2b9b529e29ce5325a27974a9d25ca04b308f36469a9ec983b2477230cc386e510a4813903c9088b38b2400b85fe0,
    0x1f186f096babd3f2b170c56c8694254615ec222903fb459b717dc974d44f6855a30de9936d85e8409c71369126c06f5e45b10fa6906b047563da009a48e684079035a509d,
    0x1f98f694ba3fc1954ef17b61439dfc164ee57f01ff83a62d76aa37f0513389fc134aedabd0ff80a06b044e17f03d0381fc0d3ce922d2cd3b873c92cea96f20939817c10ae,
    0x1ba4758c7f21c89190a21707f81e4cf023f91f7205c26a94e1bf8a857c1d1a65db19730879c47ca107d37e2031f0d7b0108307f1027f80d1851da19e50872c17aa088001f,
    0x1e1ee3893f277982ecf0ffe809fedf0b20fb9be2873e037e616f68bf84107ad31428ca99e144bf6bb1126c409fd801c61fec4287a5c0833c8176004f996e1cca244f891cc,
    0x1e156403f6e217e11b71c4c437d6157f6b860b6ecd71429a80bdcae41c1f70a51d5b83096e9560a21a405da9265936284589fe0997448ce0619a203d7944341ec00da103b,
    0x1f0fac8cbf83ab12efb1ff83f83e224f28fd8797468a873f9162999fb08bf436b7102815fe0595c32b5125594f2473c643441ee68ffa05bcc2be50af084aa819441be7045,
    0x1dff04ff80c74f50b7e1c7fd96c60dcdfe0c1b7f966ee69e9fe02ff0755eec59e4fe09157e946c5fc140578137e536dc41e1fe007f044a7d635ef1df6195a84fd019e71fb,
    0x1fbba485b09fc187c4688e59e107fc1a348f3aa5cca0e0622fe0eb9a50c238e2912c8db6a41b132ce8e644ab2a2d6926c68a12c7afa03f818a2883a431fa242b0a3681084,
    0x1f8a6791c53fc1d411c8761ff836989a318a9a270f53090b711427f0510d6c88b239599f2c0cd626caf2f517f038ad5a54a50d46122ac85543ca817530728c254204a0015,
    0x1d7f074333e379c0acc7f03428fc2b9b08cbff024792dfc1906ca7f04bf82a27860438ff043f81ffc0efe0988e33f80e1f8bfe0284e2bf811fc03fe0100f1000c20380fe0,
    0x1a15268371c4c9d13398c1a42f1a09fffe0511273f8060599fe0c7f05ff82dfc111d7aff04bf821fc0bfe047f017f80e05e4fe07891f825182061fe0304183f804047b013,
    0x1faeae5716c3337585e2dae87336b2b5545c2aad141642b314e5f0be3ca27a2b8e1ac5aba286326a2a910c827aa0330e1f8608c6a4a901b1882a304c29aa880b02078000c,
    0x1d956fca77251be27d47f074976e4dbc23da116e887663db64d588e6e07f6035b51dd78c6c8fd5a29ae3756096ac675421a915d3876984f4a19a40fd183688174205a001d,
    0x1a06ec83357fc1e06e885ef05a7e233a129804d27f80ffc1810937f017f83a1f350c91ff03c2b45fc0e06dc85ca8136e3ab30a9b01cec0b9a0fa1066601ea00a41fc0400d,
    0x1b074c4176a291d0d917f0200768251b09990847c5e1a1d1e1585064704e1c54f705948546846183cf90d83044602e200d2b09828341c16080903018782483f8020513019,
    0x1388c18101a061dfe0e7f058a1860335266f15b5091b5fc13226f8cd28039dfc12206105a447997fc101c6002a23f83652c4fe0081c3c69b24ec90aac11b3059ae3ec50a6,
    0x1c160d9156e503e371a930fc6da6483d3318910f0c46480bb2b178e0e89c5474b923168b098b55628341d14890909d4e14231b52830c04c44082e0f10042b024420028011,
    0x1e83f1c08400704009fff05803bdfc011a6e7f06ff835fc19fe0c7f05ff82bfc14fe09ff04bf823fc10fe07ff03bf81bfc0cfe05ff02bf813fc08fe037f017f805fc0312a,
    0x1b26360f5b7fc173b690d1ebf82a80d125740b3a465e078df2facff053f81ffc13316699338a599fc1d0935861f8968ffc02fe0514318658a0c641161883700cc00161076,
    0x1b7f05c71e027992a07ff05469e65f182606a4a50903e46121870ff030803c420e167181fa4703a360b1e8e0882051f62ee70e088ab98281426e40e7284b8009f40e0202b,
    0x1b0a364ed3024fd1d69883781fe01cd5354706344b51e489f0d250436c3dcc30ac01f403334852418fc15648d2684d9608f70b638a2501d8800e5174182304058000c2017,
    0x140fb7999e2435a30b0ff06d81da3b595e728ab5d69fa7b7556758ad4d49fe96f24e7e23bc121e88aef427502f30f1dc76e914bc01918b1ce0744207b0090c29c416e0007,
    0x1f7f077f82e8cfcfe0d7f07d05f3fc1b3d781a3e3f82dfc15fe09ff050e5e5fc11fe07ff03bf81bfc0cfe05943abf8121d661571023a3f80ffc010772ff013f807fc00fe0,
)
RELAYS = (
    0x7accaf61ef321c32e1df2a1e3681db5c8d734d9070d8862ccf2c3786ada0dc1b72639b60db96436b581a964fa15e3585ef915c3af1215bda5595433850333404394832844513c030140d03c0208414,
    0x7ecc2f8ca236c923dcbb2accb6ed73acde8e4c9d383d0e2d9bf03613456b20fc96785d1af99603635c54bda358d2d43d85494e32bcc33b4a51bcd308c4a1cc8d,
    0x734bd2d4a5304b9254b11b4a1174990d4811c459074490c46b0545b064,
    0x7b4e53e4f1374d53a4ad3447d0f4690b4eb3f1ff014,
    0x73db76bda7735c8a5dbd69588a1d78a5568b7377562677137567c3763c9cd028717594d5b772132d4d2515b33153c54d333f0f32cc3709433,
    0x1df7d9d779967f59ed6f96c395c76fdd8ae29f7558f5fdc56d5477f380bd3a73659d65cc16f37f1f5b1578ace052899c7cd7c4d5732747d0f51c1548524c7c170530f01504c1c,
    0x1615a951525a0105af6404b4a5880c9801e02146970065680295804587409014a0,
    0x1fa7bdf27a9f8369f0305e8349ca760a175db2625a2740c834da55c572700a31f50d4b8b02a0,
    0x65e879fe779be5f95e4f91e3f8be279fb1f9065ed1b3ec7b,
    0x1ffbdeefb9edfb3ec7afeb7abea7a7eeef9bdef1b238de86d9b36c5bed01b,
    0x71aedb6addb36c5b83adb239db038dae1b8df6a86a365a6998de955a239858978e3e4594970e21784e56f983704e63d9813a5434f9159c5612b8c32f8d56c4e125883574861a0c139084154601f40300451,
    0x1e6b7afdb96d5ad6a5a56f0616e85d6e07616977e8a5e65db41cf986c85364a701bfac1a7a7e55771805de359ce7922aac5487b5413b631321841d9442a571411313c53d284400a02f09004,
    0x76eaba6e8ba0ebdeaf6b98eb6d6eb090ea8a3b708ee6ed822b82b5093b0b8e22ec0e,
    0x1fb7cfb3a8e7bbe2aed4e96fc2e886ef9742c0ae913a14,
    0x1e1f2fd9eefc9ea7a1eaf7ffb899e6f81f3879ed869d878bdbf95eb863e3851dd8931985c13039dec53180360d04b11729ce007cfd19cd11e0300800705c31,
    0x1f9fc7e9feffff47efff8c1f98f3f3f91dc7be167a62ff55297d31146e32c41e17bc30c56380b3290b8118940c7c753403df0980796420c7f4972c100064dd1dc2715c5d,
    0x767a1da761d2739f1821c47819e6718c62988619898,
    0x6c7a9e4789fe4f11e771d4731e8689926419b8f895801b8ed4f22c93a1,
    0x788aa228721081708c2f484110140301c,
    0x7e8f226862138330e80d07c,
    0x6f6ada768d9f6759965591675cb6dc3c26e730c0ae2a0a6280959a51f064c3664173,
    0x756af336c5a966d936168f635bd0fd47652456fcf90127d323416c400d,
    0x7f9be689224881a048,
    0x4c8,
    0x6547515e55134fd9668587e668d40681e,
    0x1afa8e9fa6e3283a93b34,
    0x786c9b56c1b36b1ad6a3686ada4d91ac1a8616799d69864159956804c9458a6a802a1ac26,
    0x1f9bc6e9b46fdae6edaa6bda9699a56f8606f07a1e0761699b6d057649949f914cc86e141b80434f635b6021896,
    0x1bdfcfe17bfa979fa5c970af2f,
    0x1d173fb7eafa7e22fdd829dca277c37,
    0x1ddef7ade97c1e57a9d2fa1df76debe91d9781d5771d178c27161e318450735dd125d9131cd84c5193c49121cd5274711483207411,
    0x71ef9ff7f5fc7edf87e5f67cdf279dfd0b1e1799ff175e275dfd169fb13df9151cb7dc7511df31c44abbc45806ad1b56b1,
    0x6e379263f878780e4640e6261124bd0e460b0c090d4,
    0x1f0fa3f1783d1bc4d1343fd39449944213ecff2ec,
    0x1dd655764942d435,
    0x1e5495cb31c,
    0x636dc372c435bbc3d52eb0244252b0b33e54df779425c89f240e2574fd1403d08855,
    0x1ecbf0f4392f8ba2e0bd3fd742ed75390b5c,
    0x69581585415d51a432,
    0x1cd6d59d6356d5ed5b52915849,
    0x15eabea7a1e5f95e37bc62f83e,
    0x1f79da8437ed5afeb7a5e6f87e,
    0x1cbb0eb3a8e9ba4e83a456ba2c4812e7146e5583a,
    0x1fbbebf3baee3b6ed3be5abbf6bf90ee9f432fae3,
    0x7afa7e4f8bdaf62c6bd9f27,
    0x1fbeafe7f3fb7e3fc98ef66d5f2bc5f1bc1f,
    0x1eff9fd7f3fc7edf9f2bf8fddf67fd557f19850df,
    0x112ffff7f7fbfdff5fc8f3fc1e,
    0x70cbb2ccab26c8b20c7b1ac5b14caf3a1430c88b6e289fa37b5cd534ac4b74319b033b6e31186a2342d,
    0x7ace33e5db34cfbfe2f9fcdeb7e3e8b6de0b2dc0b0db3767dbac3a36e7632839b63c936238354a635ae328cd60c9e30cb4,
    0x618761fc2613c2705c,
    0x1fe3dcd731c9f25c8718cf084debcfc,
    0x67d9763d7f5dd6f713676d35f693576534f6136f1d36cd1d6b5733f5535b4fc4cd1334cbc260b32649314c9d0cc4d,
    0x7f9fcfbdf4fd9df7b3c77bce4fc9e7389dcf79d4f5cccedcbceb39cdfb8cdfc875f36710d3cc7c1cc5d04c45,
    0x15b5bd5f4fdf543d,
    0x5a592255,
    0x1aaa4a7a9aa5a92a3a836,
    0x7aaf3bdee2b6ad2aca7288a,
    0x1f779dd770dc76edab64d9f62a9763d5a9fd6748d4f4ac,
    0x7daff78dd9fbddf6eacf6fdaf659834c952a9d437e5877de328ec4744bd7fc1,
    0x1c6ebb96e1b76dbb4edcb46cfb2bd1711c8b,
    0x7bbdefcb9ed8b42cbb03c7b,
    0x1b2f6cdf34cb32aca324c6622c6e5796b3605b0b94300c276dff4ae08fc27,
    0x1bafcceb38c8af2c85b0cbb26c831ec9edbb4acbd1740a,
    0x7c1e070cd06ccc06c1986217860c707f4685ccf53d3e933b5b161e4f74c6f334877cbcce1d127362f5428633431f3912bc3add39ed935cdfb4cdff81dc53cc614fda451cff24ce700da23942c2880400594,
    0x1fb3cceb38cfaf6cfefabcb2ac9b3f37b36beefb35b75bc4d8cb4edb7adafa4e53a96133339ccfe676cebf96d53cd23f91f4271ea244dbf34d672b1072fd0919efca50bc138472cc0e1e402,
    0x6f4a72d4772b4572944b2548d21475194551a461114310d40905401018,
    0x1ed394dd354cd2c4c53dc992742e174,
    0x1de759eeb2df2aedeaaaddaa8d8b72abab1cb2adca2a5e9f20a579db8f382d8b22ce9ca6f217b899c65e8257262594df4dd45588a5371220941e10ad90f013,
    0x799ea7ede376dfab0de2a6d836ddd29adc2adea718d976aa92a5c774ad873c27f0de773a227b026157c6dec21fa424720278905508853887c15c050dc1c,
    0x1b56b59d6558d5857d7c0217a0657605d720015995e6c0566804d6401660078180,
    0x1fd7d5f1745b1795d5665cd70089605c56a0796b998279a2639882ed31619702158a5605a54040109364c012439,
    0x6ceaba8e9ba4e8ba0e7b9da63adf56a7f87ddf2b95f47c7f1d81f,
    0x1f3b6ecbb9ac3b7abbbbfffbe6b6b9fd7fc68ebb4bfc1aa7f73e183f,
    0x7c6e8f46d8fd6c1bb6c8ec6b8f76d5a86cc711a8ef1baa26e850598eb1b5a7188de6c067a78e3a846de68e816996695abe6c61e58e1648d466f9814c4e34855e6d901398a32c4c10b8633d8482447e21823144210b41601801,
    0x786d9b26b9b96a9a46c5bd1e46f6dabe1d4606f04e5296d1ada4ae06968c71ebfac1619f19067e8d991499de704e839c6b43d113c4de558af4589e318a11c4410f8461d831,
    0x6efabe4f73d0fc7efb23e5f5efa7f5d7f03c9f,
    0x1dbe2f53fdbdfca722caf6ecb90ec5f,
    0x7c7f5fa7edf67b9f77f3f57bdf6fcbed7bbe47abe779be2493e077920fbfdf77bd875118f5dd2449e1f66e30740cf7757f640a431c8f674f954047478a03c014180b51bc550805f0640f,
    0x7fbf9ff7e1f97c9fdbeeec7a1f5b89f3bfbe17e3e8f69fff6df7f73e9fb416741157a427045e107c23e6c0443ee3c2dd3e4c0df254802c09013c150fc000c011,
    0x748ba288c1e28e5e8789eb7a5fe15ad27f0586f8d4641ba131866f0feed8743c8f41,
    0x7e4f1384d9387c9e0db9f77a9f589ae67c870391f01b0e66b8626b0681a0de6698ea984e69048688c060aa01,
    0x6b9a66596e5594e4d92e4990e534,
    0x1fe7d9e675937339c6579070f902879,
    0x7d669756a59e99da567d9b65d9364595465d5735cb7b40778c1d305db03c0d0,
    0x185ac9bda49ad99685ff445cb63dc9715c6a,
    0x1e25d5d2709b66a99a515865f94248a,
    0x7e9ea7b9ca779516f9b2679,
    0x14a91334c561186e,
    0x7eacccd6c4ef325876b4eb3a4d269cc36,
    0x726d1b06b1a8699af6e0606a59e6959a6d8721b85666da8190526bc59670506d0ea321e63745c36c49e1a9565446109bef1dd433c421,
    0x1f8786edb96e87e6feaa6ec567c07dadc62bc0dabe93567116b485e34450361a0928d763ac83,
    0x1a0a62909c780967789477098231d6229d4248847408e22880712c62,
    0x1e8b62f1f4281f2269f0241ee219e37b0aa2889a2a8160,
    0x1ffb97c5ef791f4b89ed795de785e0061dd7701275dd6041d2b380d64ed1729c804d4561941a,
    0x1b1fabf8287f03a099ed6e036081e37d03de85b2069df775b00b80c755cf6a8047c57321dad5a4416,
    0x74571545913f451125cd105490c52146511405,
    0x1f17a581da43944b7b561af0c10941c,
    0x7a4e1364c90481d07c,
    0x1f913244bc4a9264393544d0a4ff3dca3024,
    0x718dd735bd71ca56fc9d635855f57c1b5655553d4b56c1301d4230d490,
    0x7d8fcbf5f57b5e5755c56b5f4175e7135357782575bcc310bc055ac015,
    0x6457957971545d4085,
    0x685894e96963561515,
    0x13790a22946,
    0x1bf89e,
    0x1e0741c86e1a8601785c1e8de0c8d815b6e34844d384a1f1401d96c6,
    0x7a1d8701987e3d8e4168421e994700044,
    0x75f97dff6bd7f2fc7f,
    0x1fffbfe7f7ff5ccf19d97,
    0x610ce8f07f99e2f0b2249b43d09f,
    0x710ac290941f06c27e5c1504f0fc6c5de2c4712f85e,
    0x1eb32cc32ecb33bca326cd722ca720c9721c7319cc8d8cc0e8353183471233b1a93707c6188c38c5c30d582e0c20b01c,
    0x74ce72acdf2a5932dcaddec9f1ac8f16c7712c5f0fcf8fc3430bce8e2662ccc71b83760c61302bd0c6868828,
    0x1cfaec3331ec52be0b03c,
    0x1ffb9cf7838,
    0x1f771ed37bdcb71da76cd9f63dab61d777129b6f2aca728ca0d5f5f25353d6c9724c8982b51d3c86d2c8520b432,
    0x7edf378df436dff7b0c36fdbb658f49fdecb92a3694dc9bdd4a18cca2d676925e118374258483c74856275921241938112,
    0x1c3fcdabfb5d16959552453cef38a54,
    0x1f3f8fd3dcffd775d108d755a43902f214d52b879,
    0x77ac6ada9ea1a6e93a3284a,
    0x1febdaeeb9a3f82e76bf35688a0a83d0e826,
    0x1d773dbf66aa77e49758c5256c431fd4e88c,
    0x7aef3beafb7fdfb38ceab84d33ddaa70cfeaccef6e4a339d8337d6a5cac0ec3,
    0x1e276bbaeab7ae298ed2b22c77d3ecf,
    0x78b61c76,
    0x7bcdf33c37efcb731b8f32c772ac932487f9ac5309c4b17a94a702776c7c19026972680d02c8c014080,
    0x1ff33bf73cc9f26c8b37e47098ec06c1f0daaffb20e69fe4b70,
)


def unpack(number, bits):
    values = []
    while number > 1:
        values.append(number & ((1 << bits) - 1))
        number >>= bits
    return values


def kernel(aff, words, s_out, deg_out, table, block, mid, arrived, far_words, mask_rows, far_mask,
           col_sums, row_sums, row_shares, col_shares, near, far,
           load_sem, word_sem, leg_send, leg_recv, hop_send, final_sem,
           row_send, row_recv, col_send, col_recv, pair_sem, out_sem):
    row = lax.axis_index("row")
    col = lax.axis_index("col")
    me = row * SIDE + col
    partner = col * SIDE + row
    y, low, core = row // 4, (row // 2) % 2, row % 2
    high, x = col // 4, col % 4
    on_diagonal = row == col
    size = block.shape[0]
    chunk = size // CHUNKS
    groups = size // TILE

    def rows(n):
        return pl.ds(pl.multiple_of(n * chunk, chunk), chunk)

    def group(n):
        return pl.ds(pl.multiple_of(n * TILE, TILE), TILE)

    def place(cx, cy, cc):
        return (cy * 4 + low * 2 + cc) * SIDE + high * 4 + cx

    def mirror(device):
        return (device % SIDE) * SIDE + device // SIDE

    def to_partner(src, dst, sems):
        @pl.when(on_diagonal)
        def _():
            pltpu.make_async_copy(src, dst, sems.at[1]).start()

        @pl.when(jnp.logical_not(on_diagonal))
        def _():
            pltpu.make_async_remote_copy(
                src, dst, sems.at[0], sems.at[1], device_id=partner, device_id_type=LOGICAL
            ).start()

    def wait(ref, sem):
        pltpu.make_async_copy(ref, ref, sem).wait()

    def load(n):
        return pltpu.make_async_copy(aff.at[group(n)], block.at[group(n)], load_sem.at[n])

    to_partner(words, far_words, word_sem)

    kind = (((high % 2) * 4 + (y + 4 - high) % 4) * 4 + x) * 4 + low * 2 + core
    for outer in range(16):
        @pl.when(kind // 8 == outer)
        def _():
            for inner in range(8):
                @pl.when(kind % 8 == inner)
                def _():
                    sends = unpack(SENDS[outer * 8 + inner], 17)
                    relays = unpack(RELAYS[outer * 8 + inner], 10)
                    for n, value in enumerate(sends):
                        table[n] = value
                    table[CHUNKS] = len(relays)
                    for n, value in enumerate(relays):
                        table[CHUNKS + 1 + n] = value

    relayed = table[CHUNKS]

    def leg(n, carry):
        entry = table[n]
        relay = place(entry & 3, (y + ((entry >> 2) & 3)) % 4, (entry >> 4) & 1)
        slot = (entry >> 5) & 127
        number = entry >> 12

        @pl.when(slot == DIRECT)
        def _():
            pltpu.make_async_remote_copy(
                aff.at[rows(number)], arrived.at[rows(number)], leg_send.at[n], final_sem.at[number // 4],
                device_id=partner, device_id_type=LOGICAL,
            ).start()

        @pl.when(slot != DIRECT)
        def _():
            pltpu.make_async_remote_copy(
                aff.at[rows(number)], mid.at[rows(slot)], leg_send.at[n], leg_recv.at[slot],
                device_id=relay, device_id_type=LOGICAL,
            ).start()

        return carry

    def legs(first, last):
        @pl.when(jnp.logical_not(on_diagonal))
        def _():
            lax.fori_loop(first, last, leg, 0)

    def hop(n, carry):
        @pl.when(n < relayed)
        def _():
            entry = table[CHUNKS + 1 + n]
            source = place(entry & 3, (y + ((entry >> 2) & 3)) % 4, (entry >> 4) & 1)
            number = entry >> 5
            wait(mid.at[rows(n)], leg_recv.at[n])
            pltpu.make_async_remote_copy(
                mid.at[rows(n)], arrived.at[rows(number)], hop_send.at[n], final_sem.at[number // 4],
                device_id=mirror(source), device_id_type=LOGICAL,
            ).start()

        return carry

    legs(0, CHUNKS)

    def start_load(n, carry):
        load(n).start()
        return carry

    lax.fori_loop(0, groups, start_load, 0)

    @pl.when(on_diagonal)
    def _():
        def own(n, carry):
            pltpu.make_async_copy(aff.at[group(n)], arrived.at[group(n)], final_sem.at[n]).start()
            return carry

        lax.fori_loop(0, groups, own, 0)

    for t in range(groups):
        tile = col * groups + t
        bits = (words[pl.ds(tile // 30, 1), :] >> (tile % 30)) & 1
        mask_rows[t : t + 1, :] = bits.astype(jnp.float32)
    col_sums[...] = jnp.zeros_like(col_sums)

    def prune(n, carry):
        load(n).wait()
        mask = mask_rows[:, group(n)].T
        total = jnp.zeros((TILE, TILE), jnp.float32)
        for t in range(groups):
            lanes = slice(t * TILE, (t + 1) * TILE)
            kept = block[group(n), lanes] * mask[:, t : t + 1]
            block[group(n), lanes] = kept
            total += kept
            col_sums[:, lanes] += jnp.sum(kept, axis=0, keepdims=True)
        row_sums[:, group(n)] = jnp.sum(total.T, axis=0, keepdims=True)
        return carry

    lax.fori_loop(0, groups, prune, 0)
    row_shares[col] = row_sums[...]
    col_shares[row] = col_sums[...]

    def share(n, carry):
        other = (col + 1 + n) % SIDE
        pltpu.make_async_remote_copy(
            row_shares.at[col], row_shares.at[col], row_send.at[n], row_recv.at[col],
            device_id=row * SIDE + other, device_id_type=LOGICAL,
        ).start()
        other = (row + 1 + n) % SIDE
        pltpu.make_async_remote_copy(
            col_shares.at[row], col_shares.at[row], col_send.at[n], col_recv.at[row],
            device_id=other * SIDE + col, device_id_type=LOGICAL,
        ).start()
        return carry

    lax.fori_loop(0, SIDE - 1, share, 0)
    lax.fori_loop(0, MAX_RELAYED, hop, 0)

    def share_in(n, carry):
        other = (col + 1 + n) % SIDE
        wait(row_shares.at[other], row_recv.at[other])
        other = (row + 1 + n) % SIDE
        wait(col_shares.at[other], col_recv.at[other])
        return carry

    lax.fori_loop(0, SIDE - 1, share_in, 0)
    row_total, col_total = row_shares[0], col_shares[0]
    for n in range(1, SIDE):
        row_total += row_shares[n]
        col_total += col_shares[n]
    near[0] = row_total
    near[1] = col_total
    to_partner(near, far, pair_sem)

    wait(far_words, word_sem.at[1])
    for t in range(groups):
        tile = row * groups + t
        bits = (far_words[pl.ds(tile // 30, 1), :] >> (tile % 30)) & 1
        far_mask[t : t + 1, :] = bits.astype(jnp.float32)

    def store(n):
        return pltpu.make_async_copy(block.at[:, group(n)], s_out.at[:, group(n)], out_sem.at[n])

    def finish(n, carry):
        wait(arrived.at[group(n)], final_sem.at[n])
        for t in range(groups):
            span = slice(t * TILE, (t + 1) * TILE)
            mirrored = arrived[group(n), span].T * far_mask[t : t + 1, group(n)]
            block[span, group(n)] = 0.5 * (block[span, group(n)] + mirrored)
        store(n).start()
        return carry

    lax.fori_loop(0, groups, finish, 0)
    wait(far, pair_sem.at[1])
    deg_out[0:1, :] = 0.5 * (near[0] + far[1])
    deg_out[1:2, :] = 0.5 * (far[0] + near[1])

    @pl.when(jnp.logical_not(on_diagonal))
    def _():
        def sent(n, carry):
            wait(mid.at[rows(n)], leg_send.at[n])
            return carry

        lax.fori_loop(0, CHUNKS, sent, 0)
        wait(far_words, word_sem.at[0])
        wait(far, pair_sem.at[0])

    def hopped(n, carry):
        @pl.when(n < relayed)
        def _():
            wait(mid.at[rows(n)], hop_send.at[n])

        return carry

    lax.fori_loop(0, MAX_RELAYED, hopped, 0)

    def share_out(n, carry):
        wait(row_shares.at[col], row_send.at[n])
        wait(col_shares.at[row], col_send.at[n])
        return carry

    lax.fori_loop(0, SIDE - 1, share_out, 0)

    def stored(n, carry):
        store(n).wait()
        return carry

    lax.fori_loop(0, groups, stored, 0)


def on_device(affinity, keep_words):
    size, _ = affinity.shape
    groups = size // TILE
    words = keep_words.T
    vec = pltpu.VMEM((1, size), jnp.float32)
    dma = pltpu.SemaphoreType.DMA
    symmetric, degrees = pl.pallas_call(
        kernel,
        out_shape=(
            jax.ShapeDtypeStruct((size, size), jnp.float32),
            jax.ShapeDtypeStruct((2, size), jnp.float32),
        ),
        in_specs=[pl.BlockSpec(memory_space=pltpu.HBM), pl.BlockSpec(memory_space=pltpu.VMEM)],
        out_specs=(pl.BlockSpec(memory_space=pl.ANY), pl.BlockSpec(memory_space=pltpu.VMEM)),
        scratch_shapes=[
            pltpu.SMEM((CHUNKS + 1 + MAX_RELAYED,), jnp.int32),
            pltpu.VMEM((size, size), jnp.float32),
            pltpu.VMEM((MAX_RELAYED * size // CHUNKS, size), jnp.float32),
            pltpu.VMEM((size, size), jnp.float32),
            pltpu.VMEM(words.shape, jnp.int32),
            pltpu.VMEM((groups, size), jnp.float32),
            pltpu.VMEM((groups, size), jnp.float32),
            vec, vec,
            pltpu.VMEM((SIDE, 1, size), jnp.float32),
            pltpu.VMEM((SIDE, 1, size), jnp.float32),
            pltpu.VMEM((2, 1, size), jnp.float32),
            pltpu.VMEM((2, 1, size), jnp.float32),
            dma((groups,)), dma((2,)),
            dma((CHUNKS,)), dma((MAX_RELAYED,)), dma((MAX_RELAYED,)), dma((groups,)),
            dma((SIDE - 1,)), dma((SIDE,)), dma((SIDE - 1,)), dma((SIDE,)), dma((2,)), dma((groups,)),
        ],
        compiler_params=pltpu.CompilerParams(has_side_effects=True, vmem_limit_bytes=47 << 20),
        name="exchange",
    )(affinity, words)
    total = size * SIDE
    left, right = lax.rsqrt(degrees[0]), lax.rsqrt(degrees[1])
    normalized = total * symmetric * left[:, None] * right[None, :]
    return normalized, degrees[0] / total


def solution(mesh):
    in_specs = (P("row", "col"), P("row", None))
    out_specs = (P("row", "col"), P("row"))
    return jax.shard_map(
        on_device, mesh=mesh, in_specs=in_specs, out_specs=out_specs, check_vma=False
    )
```

```python
import functools

import jax
import jax.numpy as jnp
from jax import lax
from jax.experimental import pallas as pl
from jax.experimental.pallas import tpu as pltpu
from jax.sharding import PartitionSpec as P

TILE = 128
SIDE = 16
CHUNKS = 32
LOGICAL = pl.DeviceIdType.LOGICAL
DIRECT = 127
MAX_RELAYED = 69
SENDS = (
    0x1fff07bf83bfc1cfe0dff06bf833fc18fe0bff05bf82bfc14fe09ff04bf823fc10fe07ff03bf81bfc0cfe05ff02bf813fc08fe03ff01bf80bfc04fe01ff00bf803fc00fe0,
    0x1fff0200f3dfc1dfe0e7f0180737fc1afe0cff063f82ffc15fe0a7f0589d67fc12fe08ff043f81ffc0e6316ff033f817fc0afe04ff01ff80bfc04fe01ff00bf803fc00fe0,
    0x1d979aff80a12942a1f9a8cc987c62240c4b13980013a5231221e128c078542acf1a1d0f8b070e43a6e161c8a8b44070122914340799c30441243062b8188428ea0226001,
    0x15151dcd4c61c94313fff07bf810487dfe0e7f04494f7fc1afe0cff063f82dfc0401430f1b86cebfc0c1339ff04bf821fc0ffe06ff01434d7fc09fe000221ff8020c62fe0,
    0x1f7f077f837fc1a760cff061d02ffc16720e0cdd5b80203b46a09ff049883e93915c087f03ff80a16ae5206ff031180002ab3c057f024d011fc0726037f0107007fc02060,
    0x1fff07bf83bfc1cfe0dff06bf833fc18fe0bff05bf82bfc14fe09ff04bf823fc10fe07ff03bf81bfc0cfe05ff02bf813fc08fe03ff01bf80bfc04fe01ff00bf803fc00fe0,
    0x1402ce198bece57622f31954a1980fb2266eae913f838b256502da894d18b49a50402ca293ce8a8824d34289d90c0a44032b26271892460944241fe0386b18388a1640002,
    0x1783477f82a05793d2e7f06bf831fc17fe091415bf81840532b2f056d3f80a187023230527c1423fc0a15277f024448814e70f26ff06c0f42006bfe00013a3f8040443fe0,
    0x1a06b613074b227fe0f8c9dc78eca2351a3984b41104bfc0e4011ff04460fc226d123900b30e87a1e6a0a30ff02cd85e82240ece059a0b0720e6206c3168a408f60e80000,
    0x158857ff8104d3efe0509377f839fc1bfe02017583db5fc19fe0c7f0383eaffc140b6aff04ff825fc11fe038d0c3f80410cffe06ff033f813fc06fe0000317f807fc01fe0,
    0x1fff07bf83bfc1cfe0dff06bf833fc18fe0bff05bf82bfc14fe09ff04bf823fc10fe07ff03bf81bfc0cfe05ff02bf813fc08fe03ff01bf80bfc04fe01ff00bf803fc00fe0,
    0x1fff07bf83bfc1cfe0dff06bf831fc17fe0b7f0652dc20154fe09ff04bf821fc0ffe077f037f819fc0bfe057f027f811fc07fe037f017f809fc03fe017f04457ea70e0fe0,
    0x15ff07441fc879650037f0281af89a14480da484910348611400b9d8408332538e2c0a91e34a01e4e091e0f86c080bd83a081a0988b9412ce2a0314020786001c20e000e0,
    0x1d9f098241009ff157b1a0f9246e5d3c3f19940e4dc624838137e863d4ac7414f40f778c0c8845c242b1d15080b036d21c230103850c015ca0c240d16ff0082c420420031,
    0x1f7f02501fbfc1c742d7f065c8b657d86e2f8ed5da0abfc146029ff0584ba5fc1158287f03d50862f6e4e26ff0310897fc0a3c247f00403cffc062e22ff0109085fc00122,
    0x1fff07bf83bfc1cfe0dff06bf833fc18fe0bff05bf82bfc14fe09ff04bf823fc10fe07ff03bf81bfc0cfe05ff02bf813fc08fe03ff01bf80bfc04fe01ff00bf803fc00fe0,
    0x1f82a2ca21e7f9efe0eff06ff835fc19fe0c7f05ff82dfc1c064aff053f827fc12fe08ff043f81dfc0dfe0198e33f80e028016c57f027f811fc06fe02ff013f805fc01fe0,
    0x1dff067f831fc1647c69245ff82bfc13fe08ff043f81ffc142dc5046309f78048efe020a49c07f41c2bfe09040a3f80dfc05fe04810fc1c47fc02fe00ff0740c41fc1e015,
    0x1816f13f803fc110c6f07970ab1a4bd308258bf649b1227d722cf8ee1c43ba33941ccd039182bb62b9216cc08e3c4b2c028e10c283f303b2a0b2a0ac405e0c230003c200c,
    0x168e5e05e3e618c47f90546cccf85d9d117d16607f81c1115034b9462d07ec4983019a106786f1e3d9917c50d64c4f0e29910fc303420ffca19890dc8171902704098001c,
    0x1f99ce0fb32739538ce16cc8db2c67902ecda1ec7f828538d22cd1ceac831c438ffe0b99ea7f8265faa16d60fe1c33502f8412c286e0ff83c13e20cc308e80133a020100d,
    0x15922fd974a10b8fe0a7f04bf81dfc0dfe057f07987729dbd3b9b256a3f82a91bb55d8a16e9374dfc174bd7996f0a647fc133dd6136c0c75239a71fd2054883f4200a005d,
    0x1984ae8889c0eb82025abf34d37e5e551e20ff030c37c524a2cde93918fbb8464928dc97ed058b63e5214218ad1c836c43af0e280ce94636e264412d407e882b62064002d,
    0x170c5fcace4586c19a68b5d847604c7e2737911c42f563c7d2130836a8df901d7c1f348b1ec74ce59da1b330a1e454c8207811328e75c3cc411d50b31841d014c00073013,
    0x150ac4832a21a62fe06859c02ab8234e08a287c740003fc0b06ad07d1c1bb2175f1c1b04d241281fc1e1a1a03d2002a60b44048601d6c604c0677161180d5450700a0f121,
    0x1f7f077f837fc1f156d7f07045a61cd8fe0aff04bf82218d0fe068533ff81610d90d667f027f811fc170b637f0581d9c28a5fe050330bf80e08d405620130c058200c0fe0,
    0x1b11d443a9ffc06fe0829f6c81989fda1e6f8db0ff8163b4832e17f064719227581a6080ddc61bc32d5166285d5051ba2ed2126e0ab0053a626cd0e6707b28218e1ac4046,
    0x1fbf764c6baf5dc0b6d3c779cf840c7b71ebbb761bf8208766de3ff01405aae1d46be9b670005e2d5d269e83273d979ab9ce61e5ab731579295ca47e41b718cf8835c31de,
    0x1f8dbf449fc2efcfe0dff06bf833fc17fe0b7f0342aebfc14fe0805de039e7fc11fe0584dbbf8100b720c767f03c21ce16e400b283babf813fc06fe017f007f80606e0fe0,
    0x1b083f855f4317813730c2d445ee2d6e179d977c83de01429097a0a58c15e225600172862f456de217c13b6875e446d80c330fb4065ac36ce117f0910826901ed4002203b,
    0x1d94dd4c2fed3fd62fb92de97bc806f95aff33fd95bc20b5454f98ddc933f8bff04afc2dfbc92e2afed42f728fad03d89bea36f4a1fa0a3ce53e51af303d8c3bc407e002f,
    0x1a1d7d92ffa38ef3dfe0d3c82ef430ff157c8b3ac26f028fe13730b79047ee24e309f6ff06c3de620e7fe08873d435e018ee0b76053881fc009e1fe05043a425ca00e8057,
    0x1f27a33f83e4398424e26a59012ebf143e4e8fe48f12ab7113a4da5a40e111fc0f3643ff017f807fc0e344d23a2cc905fc0d5e80ff028b901fc092c49a0a1861320784104,
    0x188b73c0efa683f171b9326cbe2029de375a980e0351c58bc2f59160d04c9621da2355077647d504021fe048d2b08e4820ad13528509c3d6619a2075183083f80c09d603e,
    0x1f8bf3028bc46e308ce8fbf0b1cc12c206cd0ebeca1f232f8267494d5889ee2ee5006504a5081ce3f521e7a89bc469e622e40ca807bbc51dc1aed107082d2c31d1fc000a7,
    0x1b8c46c5513fc14134f153880f389d7f61bca45f566f0897a4fba9c5c8450c089649b2012403d26696e0d4898584165e596d39b5935a8aec6008821b0016302d0e1165014,
    0x1f9fa3c917a7686fe017f064b2f86a8a1c5c19a40892e5e80fe0b16a38711012ad1a4a13a1009742fec16498fa6c4be43a8914488ca5423d622870a4285a0c093c0601004,
    0x1a242e7f82dfc1e4159a32d7f82288b2fe08212a3f81e80bf17d71e2f0fd5a70a5fe027f00ff8186cba5f917f061765660b75795142ec9d5240a0fe0386298354200bd13d,
    0x1d16b44ca7e73391c6f1bcdc61ba6736166e15ccc51b64f345eac11cc16a800a891c97afd38216a3b2d52a90bc8c52481b2a48a5a5d08225836c830a388b14118c3341049,
    0x1f91343f83a40c519b7832f8bd8810e3057e0f3080df434db29650228016cc19f92764012dc0fc200b8256a88337f82818d621688534c7d9c10d21765833303d9204c7076,
    0x1f0a8eff83a223010cf86b6048384a8c0aea8ae343b22278b0cc508e3828101f860ac909a1423341e39221b7f0101b29fc0302cb848cc70440b09121004e1c385e0621041,
    0x1d9b6fc6c7469a4074c196e4af6c61b729d9976d4976059b123d7156b4875851be191e190ac7f544da81dd9067744c4e49a619d2906bff8283c2315d4880883f4209a005d,
    0x16ff033f83e87c9fe0f20f1ff80dfc1b3aee9ff64e3b47bd734ec1df58c3aa6fd42ce1ff04493a65bc2fe0915f71f2a05f4f18e710f2c4b9437c0fe0408f141b880bc100e,
    0x1cc0557f83a6ddc77aa7f03bf81bfc09fe0d1977ce7ae5dd835eb1574ccf91fc1231e88e76dd69e35d025e37f030779621de0d650570ff805fc070be0800942781fc0401e,
    0x19ff059e22ac303fe0f928408b34538c20cc93e3419f04b810cba11e247b3c46081cce8f85c7838361230488ee186b1c378518c58ce3c680e2f8a160000b905b362a0214c,
    0x1c077f8346245bd15ab115cc5eea0dee13b90b5f04e9e195911a8085fc27c809f40fa58f4dc1ff4342d09a6045281e92117b05140250407ce054605a1805080e8a096001a,
    0x1c0293bf83e93fa4af5ff05d1bfc8bf442fe81a27f83883e6fe0d9ffccf3f277f036fa9bfbccbe463e5fe0894fb4abc7fc02fe0b01907f801fc0a20f612fa06bce2fe40ef,
    0x1da97dc0db2a1fe277c2779bf82899e3fe09a47fd1fea5cfd2179227f10fdc7dfa3df61d7d8e7d669f135f5187bcbfe004ed2df414787f80e49e923f20c79467c1fc0213f,
    0x1f0ce44532ffc15fe0d89e53f821fc0e10cfb2a283b1ffc1c7a4eb1a1c2334ba8cfe0584e65b1080f89fe0c2ba23f80dfc0104cb2aa49510bfc03fe09a5a0bf81a8280fe0,
    0x1e382756530251f11ca98297f836cc944559172c4ed74ac9e0fc8112b8d55e40ad295ca622c955028a9155b86630360e10a31355024102e2c94820953006041d664880015,
    0x1b09aec620c0334168a83a90127e0e922e7f1dbbc190bfc03029d1bbcc523266fd123b96bb889c3fc0c207e07c2461c1fc0a024806c2c4a222ee2009685c20420e0b18043,
    0x1f7f0281e0e397dfe0202673f835fc19fe0c7f05ff82dfc15fe0a7f07c0d27fc12fe08ff043f81c09effe06ff06c1fd9fc0209b5ff027f811fc06fe02ff00ff803fc00fe0,
    0x1588cf1a129fc1b644f90e698127fc11fe0ca9a61692ea29d2a0b27a55393c2f8efe0922a41091e6e8afe0106cb4c9184a88fe048da1c610c2285fe0201a000907fc01fe0,
    0x1f146b3f832b0bb6f54ff069b56cacbf0bda2a2a3f81a3d386b59292dd9d7a2da6fe08a82d56d608cb353507f03d3d5c78bc07d51c29d1d4a54a41b558848c654405a1175,
    0x1eff03c226023bcfe0d7f067f831fc17fe0b7f057f829fc1210e9ff038235233460ca8ff02c917e23cdfe0613b17f80e36ca06ed8da8ff83c0242fe00ff0201b41fc04069,
    0x1f056647df80decfe08846741f17fc0e1574095e0574e24e60b728165c4f542cc90d6d06490170608c2017a05483f802019f3b5b172ecb56615b50fd8072c8375e09ad0bd,
    0x1803d64d9f83b96347286b3d613e8a14327b81f48c1fc7a112a7d9b84c7330621d0afd0fbb899ea3aeb24750dba481cc2ae81c760b81c51da17840e7186b8419c40ae0007,
    0x19156e827980d5f2d6892378ada044dd2967903086e5c3cdc27668e304169634db2560015648d9430d821648b35c7d9028d61d63893546d8c20d419620734c5d8614c50b6,
    0x1f8387bf81c6ac61e6eff073f837fc1afe0cff00412b1fc17fe0b7f057f829fc13fe097f047f821fc0ffe06ff033f817fc0afe04ff023f80ffc05fe027f00ff805fc00fe0,
    0x1f7f0696db9fc1bfe09a6367f81e88d8fe0aff053f823fc17496e831fc27a1fc0007b61c3590d9dfc123f65ff0080f5205c8fe03ff034e59454c5fe027f00ff80c44c1fe0,
    0x1f9c86c6321fc1a1e091ea27f832560f3a489aa38c12e421d02f615a2ca92636142873ff0604814468102b40ca58300a2695080185a13f81a120210430287003fc42e00a4,
    0x1b9f0b1a56a743f3d199a0f8e462643d3517970f0c45a543b2b15930e89454443921148f0e0745030361b138b0d0644c24321512870c04448102e0b118308814420820031,
    0x1e7f06ff835fc18fe0b7f053f825fc19607e83f43f81ffc175c777f037f83ec6ecfe05ff05549ca1b6afe04ff04d19fcaae302a081b44f9d1fc063273ff013f80046e2fe0,
    0x192c3fd95e0a0fbfe0d7f07975f3fc18fe0bff05bf82bfc14fe09ff047f81ffc0efe067f0754dd7fc0afe069e3a7f811fc1c4573ff01bf80bfc04fe000838ff805fc01fe0,
    0x1fff07bf83bfc1cfe0dff06bf833fc18fe0bff05bf82bfc14fe09ff04bf823fc10fe07ff03bf81bfc0cfe05ff02bf813fc08fe03ff01bf80bfc04fe01ff00bf803fc00fe0,
    0x1fff077f839fc1bfe0cff078a66dfc15fe0a7f04ff825fc11fe087f03ff81dfc0dfe067f02ff815fc1739d4ff0687e51fc07fe037f017f809fc03fe017f0604643fc00fe0,
    0x1a0cf7c987a6e3e221d198ec806c5a391a1c0aedc58664e3c0ce508ed430501ba516388f8c8205e362310320998812182e2608d5878c0105216210833848b808400e6d001,
    0x181a1e4dcf40d9ffe0f7f077f81a5c75333e7f04cb4d4487bfe0c7f03ca4effc0e27348f1ac84ce28681739026dbf829fc060f38ff0100759fc000941ff0142cc5fc01033,
    0x1fff07a103bfc1c820dff069f833fc187a0bff059e029fc1376097f045d02a778f72081da39b0022bad6a067f02d9015fc0958047f01d400dfc0548027f00cf805fc001a0,
    0x1fff07bf83bfc1cfe0dff06bf833fc18fe0bff05bf82bfc14fe09ff04bf823fc10fe07ff03bf81bfc0cfe05ff02bf813fc08fe03ff01bf80bfc04fe01ff00bf803fc00fe0,
    0x1e7f06bf833fc1b622faa957f83ca258502ea294918ac765710da1b934c89c5653fe08ff024a09617a722287f01468881a4ffe01049042099fc0afe047f00ff80c1320002,
    0x1cb51717caed05b5d2b2f1695c9c1d3e1bd8ac1612c9e94534125864c0e492704d312f8b6a894ba29a001347f0505f6a1da71f2905698648a384c09d20b10c2c841441012,
    0x1d1381c12a42f8402af188f0c84203db2e1a8f860b05e2396261e948ac3b324a34201b8e8b428263631181304e0c01a02e2504070a8b048541e3f08400182428501622061,
    0x1fff07bf83bfc1cfe0dff0083775fc19fe0c7f05ff82dfc15fe0a7f00c07e7fc12fe08ff043f81ffc0efe06ff033f817fc0afe04ff023f80ffc06fe02ff013f803fc00fe0,
    0x1fff07bf83bfc1cfe0dff06bf833fc18fe0bff05bf82bfc14fe09ff04bf823fc10fe07ff03bf81bfc0cfe05ff02bf813fc08fe03ff01bf80bfc04fe01ff00bf803fc00fe0,
    0x1fa03f7f839fc1afe0cff063f82ffc16fe0aff053f827fc12fe0d895c7f80828d0fe07ff03bf81bfc0cfe05ff078a5d5fc09fe047f01ff80dfc05fe01ff00bf803fc00fe0,
    0x1fff07bf83bfc1cfe0dff06bf833fc18fe0bff05bf8280be01c0aff04ff825fc11fe087f03ff81dfc0dfe067f02ff8061b0afe04ff023f80ffc06fe02ff013f805fc01fe0,
    0x117f074148605f233cf3107c3e76bc01fe0cad0717c2ea41a5d00000e1642a8c165308a20513c206c134b071903d0c18600d3f0594028dc124c082f0391018940824050d0,
    0x1f7f07618b9fc1b7e2d7f065e8b1fc17742aff051b8ac275366297f04570a1fc0f52277f0353099fc0b42257f024d091fc072c237f0149089fc031e217f0045081fc1f066,
    0x1fff07bf83bfc1cfe0dff06bf833fc18fe0bff05bf82bfc14fe09ff04bf823fc10fe07ff03bf81bfc0cfe05ff02bf813fc08fe03ff01bf80bfc04fe01ff00bf803fc00fe0,
    0x1fff07bf82e067dfe0182c73f837fc1a4eccff0550b31fc102ecb7f03483140274fe09ff04bf823fc0ffe077f033f817fc0000c4ff023f80ffc06fe0080c17f809fc02fe0,
    0x1b8e2bc3e15fc14279b092cc765c111f0d1f336303e881127fe0eae60ff83699891992834204e6418350748840f037b479993bc8022e057160422fe0300083f81a0581014,
    0x1c09e2c333e7271223f1b9c15bea1b8408ce999bc80f8566e4afa01a3468f64e7228bd109b060d5fc093cf984e0413323a6832fb8a99c48cc5fe522fb0798003043fe3083,
    0x1c9463c45cc14ff1bcb926445eec418dfe0a0e60c0e26319809480b62435dc2987fe06096786716219d17c507648150225fc15c20026c4710159a0bc2836541f04058001c,
    0x1205cabf81847b914b3ff02c7b6a838914dc1587c782e460e1a8409ef8602c3a0d16cd04a9443682e100cb186ef440261e0608c885807f824169c060780808234013bb000,
    0x1fff07bf83bfc1cfe0dff06bf833fc18fe0bff05bf82bfc14fe09ff0001665fc11fe087f03ff81dfc0dfe067f02ff815fc09fe047f01ff80dfc05fe027f00ff805fc01fe0,
    0x1ea3ea983b88bbe422b86b6cf0929bd93823a4f58d8b087b334270bd30a36a77b12e2a1aec0b0a45fa20c6f9693480b43e4408a58a9187b5e57a014d403d0c308a2ba1002,
    0x1b1311bf83065bf4bdb9869057ea5dbd49d9966d00ce255be29280e1710758305b3dd1867c84494245a39d7926e4c75a39a909210278427d631a007b4056b84f4e0445039,
    0x1f109cca8fe2fc502a205d0c02ba27d2283083d4498f83e70223d01f3c80f6366e1c307f03460f2326b143c0a9a840ee22690e3b059a028ea1267083a0399818d80a62003,
    0x1cff07c66b1fc17fe0aff0785ea9fc13fe0e0853bf8361d4dfe05ff07456b4194afe0b0551ff82410d113a784517f8180d5011a402524368c0cc2fe007f010058605c105a,
    0x1f95d7a23bae3c8fe0e37f6e13b4dbd982ec35f506aae4f5678eab3f4dcba4cbd164e829f3d5b980b4e44e2ff02cfb9a6bca2ee494f1c838c27c40ce1ff007f80407c004e,
    0x1f4077c8ebaf9dc69edbb75855f4e1d863e7873dd6faab5d44fe5863cd0f942d7905391e71c36c3fc0c09781b744bf8815650377157246f9a05480fe30970c178005c2017,
    0x1c948604aec4a1710b998e3019ea42120eb894e03f8102b0d1ec790e7c33e8320a14c58de183b0e2f8e0ab106c7828360f6906b188e1012c2179d08f803870100a06fa020,
    0x19986abf80ffc1b132715693f82818fa1128853c89f6010f90f240412c67522dbe0f730317435de11780d26023dc248a04f6072f837f01dda0c2205d0ff0540c8600e003d,
    0x1f2eff5dbc7fc1c72fdacfe9c3f0a7f76cfb28fe4908c47d51e2a27fcd6bfe3a521a28a4fbd3bd883ee16280992d03da1e41fe0381920dbc1fc0a042498f9483c402440ef,
    0x1eba7f16ff6ddfa55fcb57dff830cdf5fe0a7f04bf82cc9f0fe09af7b7f822b1eafe0f1d5bd1fdc8dec3ff4ff07c86d67de835f20039cafcdfc03fe017f0146fc3fc00fe0,
    0x12ff079393e8f9d4c4e22e6929307a97484da1e59193283954241ff04cf9286e923a4898a40d91e5a80fe0695a38c9184e8b2c450fa24890e3a881e4309a1051041681024,
    0x178d090957c889c1b1da0274e50e2dbf07db1e268d52870932f489a248a51c60902546050b48d14102b2144932186d10388211528c264344624980b108625c14400095011,
    0x1e10b4450b63eda347b8eb58c9e82ad52e7909b2c313e3eed0e6807b4ca9cc4f4e267e8dba829bc43c70a4784b3081f22fc210ac0cba479c0064806627f01401862ae1004,
    0x177f06c8cf07df92139800a8161a09961f3ea03d474f878f41b3d1c3a40e2e6cf11939183a3f82058fe1d737f03c5cd848e1fe02081ac4cc004870f318e3884dca019f01c,
    0x1fa7af1096ec73b4058ff043f83c9ab83a5389c33f83a96b5345d21aabf83282a8fe068484c996c6aae1e5a17abc934dfc0b185911a90414bfc030a517f00409520600fe0,
    0x1fa22dff83c7cb4fe0d1e2b7f811fc010362ff0101ef070a2fe0a9b283f82464bd6798172f1965e54b33d5db148c1632c1313755902b8b55434ac2153072a46d6c0927095,
    0x1a11ce471adfc0cfe0483e8c0bfe365b262f0c96890ba52d8222788cd480b82e531e2209ac870ae2a501a2506cb460a2224b162705920488e0f260e2101c9428821240042,
    0x140d5dc2fc828eb0b370a6d01ff830d62996894fc9598213525948379c1cd41d32219d0b340767028c30539893786da220dd1160015ec358a11b90b6103498165e08c1019,
    0x1302f795a683f9c529fabcb85b13fc0202e98de2c53202b9a4e9eaace52a5a2797489da6ca84b308f36449aa0c9c3b247b240cc406e44f246138f3a9084b3092400b85fe0,
    0x1d960e89eb2bd3725a48b558868e155f5f9aa32d06eba5dbc1fdc2a4cc776459a30be8956c05f4409cf13d7136f9155a45aa11a6106ac47503da009a30e684078a31a40bd,
    0x18ff0695399fc1852ee96b5d4395fc154eef9ef23f80dfc196ca27f04d33bcc3524aedacd0ff80a0ab046e17f03d0381fc0e3aea23d2cc3b86fc92aeb17f1c8b9a1bc108e,
    0x1c24764bff61c8d170a22707f81e44f21ff99f730542aa9501bf8a7578151c65cb13f28679c47cc0c7f35e2021f4c7ae108309f1027f0051251da1be4077281fac088001f,
    0x1f9fe3493f87b962ace8efe9c22e06ec1efd9ce246bea6f8616fc8bf84087ccb1126c998e144bf0af0f24c409fd001c61feb388724c0833c8176004f916e1caa204f8a1ac,
    0x1e9463cde64217c0fb69b4e437d2157f69860d6ecd71429ab0fdd2a41c276c951e5583086e1460a1da405da9165d16284188fe0996444ce0615a203d81243826c009a103b,
    0x1f1df7c61721e5336fb1fc83f83673d234fe1ffbcb3f07bed28fd0caac9be86bfd102818fdc49501eb10c5612f2473c62b55082712f9c5bd42fe50ef083a9819441be4025,
    0x1fff073f8227cf90f7d9e7dc25c615c9fe0c1d7f55eec71e7fe02ff07907e461e4fe08177e936c5fc15057715787f81a49e0fe09a95d0b7d43def23f61d5ac67d021e625b,
    0x1f3aa686b09fc17804f89e59f107fc15328eb9a50c2100622fe0e38a44ba36de8f2c8cb6a41b930d68d6849b3a298124c68c12c730a03f816b68740431ea24330a3281064,
    0x1e8a67d2455fc1e471c8561ff836ac9a338b9a270b52c8cb80f427f051256a84b33f591f2c4d55e68b033517f038b55a50a50146112ac855238a811530728c1d4204a0015,
    0x1dff078333e379d0accff02c30f8339a08cbff024692dfc1806caff04ff828278604397f047f81ffc0efe0808e37f80e1b8cfe0283e2bf811fc03fe0100f1000c20380fe0,
    0x1a1325c3f20449e11398d1ac2f1c11fcfe050f26ff806059afe0cff063f82dfc111d7aff04bf819fc09fe03ff017f81005e4fe07891fc3d1a2061fe0304183f804047d013,
    0x1fb0ae5716a43365a5f2ead16178b6b2505d2cae0731e37314c5e8ce34a2762f8c18c5a6a285b26a6a710cb88e183b121f8508c827a901b1c86a304c41da880b020b8000c,
    0x1f156c0667851bf27d47f07497744daf159b926ec8f6845b85159906e487643db61dd68c6d515582dae39558a6c4675421a917d387698574a19a413d1836881f4201a003d,
    0x1a06ec82b59fc1e06e985ef05a7e2339129885d2bf80ffc1810937f017f83a1f350c91ff0402345fc0d06dd05ca4136c32af0a9b81cec0b9c0fa1066581ea00a41fc0402d,
    0x1c074c4176a2d1f0d917f0280768291d0999894785e1e211c158707403f82060f905958646c4e1a4cfa1184054583e240d290d830441c2e080d0505860248c0e020517019,
    0x1408c1810120619286f7f05c99860336246e7f05489be5ad3206a0ad28039dfc121e6104a447199fc101a6003a2ff83a56c5fe0081c3c61b652cd0aad11b1c51b03ac4066,
    0x1c180e52d6a583f3f19940dc65a2483e3b17110f4cc6080bc31168e0ecac5470ba29160b0a0bd5628361f1389090ad4c18221f52830d05c4608320f10062bc1c420029011,
    0x1903f1c00400f03009fff06003bdfc02186eff073f837fc1afe0cff05ff82dfc15fe0a7f04ff823fc10fe07ff03bf81bfc0cfe05ff02bf813fc08fe037f013f803fc0510a,
    0x1b24364fdb7fc183d678c1ebf82680d123740c3a465e074df33abff053f81dfc15336618348b59bfc1e0b35871f0ae8dfc02fe051331c758a0c641161873740cc00161076,
    0x1aff04869fa2b8d3a467f068b83e36f92a0823a60a03c32f118707f05c902c5f09167705fbc8038320a1c8202f9451e82eeb160989ba0400e1ae2047182b9828360e0102b,
    0x1b09364e53424fe1f6a0835cd5201cd32b46863448d1c309f15750437445d034bc09f4894b075241cfb1563882603d9e04f50b62862181d8800eb01f182304058000c2017,
    0x1410b7da1e04f5332bea5bf989dc475b60728bb6571f8777754758cd5141c3fc124c7d22bc521ea86ef427482f34e1d872ea14bc0191ca9cc0b441c7b0090c29c41ae0007,
    0x1fff07bf82a88fdfe0e7f060f5f7fc143b75963ebf833fc17fe0b7f04ff825fc11fe087f03ff81dfc0dfe04943b3f80a15661171033abf811fc010573ff013f807fc00fe0,
)
RELAYS = (
    0x1e32cbd0701b079ca872ca078ddf36d9074d6a221c35eed724c706c3ab73cb72836064383623c15617bea5915216b5cf815c35bda33867c6956548c8140ced010632144f00c4503d541040503402,
    0x7eceb2abba34caa3bcc32cccb6edb37839b363b524dd0dac7924fb8f257b62fb1464de29463e8578d8d53dc5615834b50f414e32bccd20ca51bcd308c4a23473,
    0x7f4e5354e12f4c92d4b92947d284552f8910f4791c4610b4510647b05453044,
    0x7e4f53a4cd3649d3048d13441094fb3f1ff014,
    0x73db769d9763dcd702b56b5876028d5c2dcddd6095d58ad37d6bc971022f67365633871fc5ed353c9f35151c74d534cce53ccfc2cc370cc25,
    0x1df75dc759fbf7f5743d5d6719af742be7759f6c27f755bd7d33f69cd95e2e4e758f345ccddcb9615994c2acdbc6517c662533d5732747d0f53c1f0c51549314c5c0f01504c1c,
    0x5a58a585b7545a01259816d880e580129780a570069215a0874e0114490d429014c0,
    0x1ff7e9f27e0ea7c0c977de27a0da780c26c5d02a9db60592720b32d5414898d700ab038b82a0,
    0x63e879fe779be5f95e4f91e3f8de279fb1f99b3991b3ec7b,
    0x7fef7bbee7b7ecfb1ebfadeafa9e9fbbbe6f3ba6cae2f9bb56cdb16c1b,
    0x73afdb8aedb56bdb83c8eb6c0e768dae3c0616b8683a25b6826235d9e36a6c170e7e4d949985fe60e01315437859e459a14190930cf557a515848337991338b5259215740600ce430488310551807d14401,
    0x1e6b7af5b76c5ad6a5a56f85f6f05d67a7a1d7b815959681b6161b415a6fe55b21b7a8197b31885be555ce359c182a049c528635a4845413a0763b4c959151491313c53d28440290280bc04,
    0x1cbacea3a4eddf298ba8f7396eb6d2eb890ea8a2296cee68a1b2382b5093b0b8bb4880e,
    0x7cfd3aae53be29ecce76fc2e886ee0bc5c884e7e0f4,
    0x1e9f2fd1eefc9e5fb1e87abe1fe624781f389bf1869d678bdbfa5eb851e7833e38931f8541075e1107318c3418029d2c35d203f41f19cb1080f80c01701c31,
    0x7e7f1ffffbff8e1fdfc1fb889fcfefdc7d6187b5ed86539f49d74451f7f31b8d32f0cb290d82ec560e7b023003d18cf640740b98b1dd64097400b03747715c1911c5d,
    0x181d8749d0731ca721c47c620669966318a62195819ba2,
    0x747c9f07a1fe4e922771d6739ea6899464199826006dbb02c93a1,
    0x768a22685a1081f08c374641101c0500c,
    0x1e22086a0ac560e81509c,
    0x1ddb56c5ad69da1675996558f68dcb66e7e2f0b62b8aa278979d427484e5064c364c153,
    0x1cdaf6b72b68d9b65d916168d6fd476ed569158492b7f3fc016ec00d,
    0x759a65e9224881a048,
    0x4c8,
    0x18d21457974552566185e668d40681e,
    0x1b7a8ea7a6e8283ab524e,
    0x1d9b26edae6d5ac6bda86b5aad93626d0701a86367d9e6a064159976784c955a602982a1ac26,
    0x1f9bc6e9b46c1bf6a9b169da56f866691bc1e8616e05c6d859651929f914cb8506f00ed3d8b6d008688496,
    0x1d97afc5fbfd7ea5adc970af0f,
    0x1d17ffc7e6fa7e2268bf7bde1f30837,
    0x1ddf37c5e97d1e77b9e57a1d2f75e6765ebe81d7779d578425169d17844f77c5475c4f841c974c4d14649121cd5274711483207411,
    0x1cfbe7fdfc7e5f87d9f57c9ed7a9e37dc2477ddb7fc627f45874dfb1e4771d44b739f3115f11bc4abac45806a91bd671,
    0x1b8e6678f6750e24c09c4512f4708e4e3024e70d4,
    0x7e3f0fe5e8f86e0fc4f1763d93f4f53eb69964213ecf04ec,
    0x1f56357e4942d435,
    0x1ed495af2cc,
    0x7b0e4ab0bee5095bd54697dc8910a4a62d4cdfed5de48932388bf2c0bd1c0221543d,
    0x1fcbd2fc3c2ecba2d0bd3fd6e2e577378bdc,
    0x19d5c5415f51a432,
    0x715bd605ad6556d66d7350915849,
    0x57a9fa3e6f97e578fe2783e,
    0x7fea439e76b3ebfb56b7a9eb987e,
    0x76ed3b2ec3aeeaba8e93a456ba2c6014e5148e4d83a,
    0x7ebfbbceebb8e9bbe5738eee7bf6e9f03b0cbe,
    0x1ebedfc3e4fe99ef52cabe9f87,
    0x1fbf89f3fdfc7ebf97d9b3bd3f2bc7f1bc1f,
    0x7bfe7f5fcff1fbfe7f8fe1f67d5fe55d4ae4bf,
    0x11affff7fbcdfebf77d3fdd11f23c1e,
    0x1c32cca324c8b20c7b1cc5b24f5312ce8568bf1b883607d0dcd6b4cc6352dc0c8c21ac33b6a31188a1b42d,
    0x1f338cdb3e5d33e2f1e6cfb7c2eb7e3d8b8dc3702bb6cdc8f27a378ea9ee39b64d98e2d6094a9396d2ab1c2b5a3278c3450d4,
    0x1961d8360dc2707c,
    0x1c637ca725c871dc6714cf880debcbc,
    0x69d9f63d875fdbcdddacdbd676738cd7d7cddc6cd5d5cded54d3d4cd4d4f1133cc9834c9c2ccfd264931cc332343d,
    0x7dde77f3ee7d3f73b3fa793e7389dcf99df753d7333cf313b4e9376e536f2133f0dd74d0d1705304c25,
    0x1f55cd7f55d4743d,
    0x1616a8dd478,
    0x64a829ca5a92a2590a,
    0x78ad2beecaacaa2a6a6286a,
    0x1ff7bde772dd76edb366db1ebd8aa9d8f5dd5f4ad4f4ac,
    0x73af774dd9f7dcf71db2add9f56a63599974694a8ed677de2a8cc3f42bbffc1,
    0x75bbee9b8edfb6ed1b6acfb6bd1711c8b,
    0x7bbe6f3b9ed7b82d6b26d0b16c0f,
    0x6abaff8cf736cc31ebb328c931b88b1d96e5ece81ac4656c0309decb0087c27,
    0x76bf7eebf33bfeb34c9af2cbb236ab26c831cc96d7b32c7d1742a,
    0x7c1e06ecd06ccc06c1986217874b831c1685acf5161f4d4cdcfb4ccd21df35bbcce1d1374b6ca1ace33a90ec187546bd6b84efc74d938127b3ad734ce1b3cda469c03005df6954724cff31cbf688c50b0a26d004,
    0x7cceb38cdb32cc33fb9b3cb931cce4f535b313c2fdbb4f1ba4d6d9cdcb83efb7cea56cccccd33f54eff8ee6744f9c9fe27d08d38fde7a899f59cac39f143a467c70b309c4e03879008bc,
    0x734a72f4872d4572944b274851d46517455164450842d02415004,
    0x1fd3d4ed394c1374ff2a4d5264ad1584e014,
    0x1de739ceb2db368df2b1ae2a4dd2a2dcaaeab72caaf21e9722a7a95e6edfce0a77d8b0275dbcb098a672825953c47e224dd25608a53701e4884510ad90f013,
    0x1ee799ba7edfebcde374dfabaa9b71d8376acfa9cc2abd736aa9f24a435dd7ee3c873c2479dc27ba295f226157c17ae298977809c24151c50865408051f05705c1c,
    0x1c56f5ad6758d585f81f5f0360315b5c8175b80056e599566a04564016600701a0,
    0x1fd7b5e9785c1795b2f75a9755e8285d0335916c0796d9982b9a265988219782cd600a5755e958149480e03a4d912439,
    0x72ebbaceaba6e93a2e839ee4e8eeb7e9f87dbf3e95f2387f1d81f,
    0x7eeebb6ed6afad3adaf7f0ea6afef9b7fe995ac7f94afc1a37fb3d183f,
    0x7c6e8f66c9bd6d8fb6c8ec6ddae399b56a0f2acc6f198e26d8545b4623ada3179aba78f018e9a37c6de905c658e7e59a5687931859236859e518e375921578a3384e618cb12844e24423358481f886144210b40605801,
    0x7a6e1b46c1b96a9a46c5bcae4771bdb6ad47e181bc1a5925c44e5a2ba19da71cfb1eb0611a05a6af9b18da5e705263215131d0f3c4fe4d8d12bc6b3189e458811c4410f87611831,
    0x193e2f4bcafd7e5b97fe74efa7fdc4f7fc9f,
    0x1fbfcfa3fff9bfbfe6cef22ddb2646f0ec5f,
    0x1e9fb7e1f47ddee7cdfefc5ed7f3f6f9df2f99e37812ef9ee8f79e4f7122f75ebf7bd675dd2466daf41e104121d6c17f3bd3f6f550290a74c08f4651e280f00d06021c751bc2017c550640f,
    0x7c7e5f67eef57c1ec7a1f5bebe277df4fabd8765f1fa7d8fcc117ac127312703ddf0740db8f9701123c2dd3e44095200df3404f2c0350003f0c011,
    0x1aa2888a1e8b1fb789de7ade97f854b51fc17196651ba139886f0feee0783d0f61,
    0x1f9384d9324f9f8783767a9f77d6267b2e47c072381ec3b86a3a1ac199a83a06066990a985068846680c060a9e1,
    0x1ae6999e5f976579464d9265b40e4b4,
    0x1f6799de759b65393e41c028b91e7f4,
    0x1eda568d9a9759e56d996458d665cb63d1574ecd72de501de306cc175c0d0,
    0x6a9e5a767a619859f97d9765dff0258f7fd09715c6a,
    0x1e25d5ca709c66a97a4b5965994246a,
    0x7e9ea7f9d27b949739ba6f9,
    0x16a91334c561186e,
    0x68adcf53ccf131daf3b4cc6acc36,
    0x746c1ae6a9a6691b1681a96f05e69db6171b21b0661759668860149936b4723399a1a8e1190d9170c9e544aa458611dc26fbd433c421,
    0x7e6f1f67e1bf6febb6b1be1e6bd182d8772fc4d07e3d596bc916180e5168da68a531558cb38c43,
    0x198a42889a7809e261dc249da231d6229d4248847408e2308070ac42,
    0x7c2e0ba7d8b22c9f0241ee219f37b0aa2a0982b8140,
    0x7fec5377c5ed799e479ae5785de775da759db7881e055d276818039d4b3811729cb62ec604d4561941a,
    0x7d7e1f07e2fe0f0287e8207cda97e03ded81c77df4095b208597751ee05d8f6b0047bd476a5732a4416,
    0x705d1185517b4610e531524cd0a52146511405,
    0x7a5d97a7f92e54946b935a1af0254843c,
    0x7c4e9344c10481d09c,
    0x1f93846c992a1204bd0e45d31c2925ca3024,
    0x772f5795d56f5a5675956fc7c1b565575b71553d4b5641501d61c08c35,
    0x7d8fd7b5dd735d62d5e42354d4d525718fef30c434d156f0056b0,
    0x176579916056952521670,
    0x685994c97163559555,
    0x65e378ea22946,
    0x49e,
    0x1d8741c06a198641805a158620407a33044d286a3f1401d9706,
    0x1f87c1e06e1b2e21c8eed704219192700044,
    0x69f8fe1f63d9f2fc7f,
    0x1f7fbf71f97e7c872bd77,
    0x1de8907f97e371d4348924509f,
    0x1dc330b42b0a42307c2de5c1fc3c13c5c59e3c4712f85e,
    0x1f33acd32ecb33dcab37c9b2dc9329c8323c731dcd0d6cc8f034f2e34b1e34311c724bc58c8c1f1035983c30dd82e0c20b01c,
    0x70ca97bca335c95e2c9f1ec6b25c6321c6f17c530ec373839190b331e67e04b130c6d8c6848828,
    0x1df96c3b2fed52de0702c,
    0x7de1e39e,
    0x1afbfde376df775dc371daf6ad97712876b27f6729b6327497d735b25756d649723c88d374d21b4982c8720b432,
    0x1fb7cdeb7f0f43ded372dfca7df4af48f6cdecb92a35dddcb52a609c9359db4a784f538a48254605c94856224fd7c81940132,
    0x7effd7b5bbee5ad62f954c433e5423ce2,
    0x1f574fa57042354443d04595950bcae2e494,
    0x79adeb5ab69fa6691a2a86a,
    0x7faf6bba8ea1a6613a2282e0a83a0f426,
    0x72da2b9dd771d9f63d6b38453089431fd6e8ac,
    0x7aefabadbabfdfeb8cdb2ecf76847268c933bd8337dcf5ec4258ac0ec3,
    0x729c2eeb92e0972dfb4ac8b1de8f,
    0x1dae87bbc76,
    0x7bc8ff9cf6f5cbf34cb325cab21c9b2487319c7f98c4b07c9c1f25689d7c1b05c960268d02c8c014080,
    0x7fbfb3dceb30c8e06c173d0cfcfaf4aff066bfecbb0,
)


def unpack(number, bits):
    values = []
    while number > 1:
        values.append(number & ((1 << bits) - 1))
        number >>= bits
    return values


def kernel(aff, words, s_out, deg_out, table, block, mid, arrived, far_words, mask_rows, far_mask,
           col_sums, row_sums, row_shares, col_shares, near, far,
           load_sem, word_sem, leg_send, leg_recv, hop_send, final_sem,
           row_send, row_recv, col_send, col_recv, pair_sem, out_sem):
    row = lax.axis_index("row")
    col = lax.axis_index("col")
    me = row * SIDE + col
    partner = col * SIDE + row
    y, low, core = row // 4, (row // 2) % 2, row % 2
    high, x = col // 4, col % 4
    on_diagonal = row == col
    size = block.shape[0]
    chunk = size // CHUNKS
    groups = size // TILE

    def rows(n):
        return pl.ds(pl.multiple_of(n * chunk, chunk), chunk)

    def group(n):
        return pl.ds(pl.multiple_of(n * TILE, TILE), TILE)

    def place(cx, cy, cc):
        return (cy * 4 + low * 2 + cc) * SIDE + high * 4 + cx

    def mirror(device):
        return (device % SIDE) * SIDE + device // SIDE

    def to_partner(src, dst, sems):
        @pl.when(on_diagonal)
        def _():
            pltpu.make_async_copy(src, dst, sems.at[1]).start()

        @pl.when(jnp.logical_not(on_diagonal))
        def _():
            pltpu.make_async_remote_copy(
                src, dst, sems.at[0], sems.at[1], device_id=partner, device_id_type=LOGICAL
            ).start()

    def wait(ref, sem):
        pltpu.make_async_copy(ref, ref, sem).wait()

    def load(n):
        return pltpu.make_async_copy(aff.at[group(n)], block.at[group(n)], load_sem.at[n])

    to_partner(words, far_words, word_sem)

    kind = (((high % 2) * 4 + (y + 4 - high) % 4) * 4 + x) * 4 + low * 2 + core
    for outer in range(16):
        @pl.when(kind // 8 == outer)
        def _():
            for inner in range(8):
                @pl.when(kind % 8 == inner)
                def _():
                    sends = unpack(SENDS[outer * 8 + inner], 17)
                    relays = unpack(RELAYS[outer * 8 + inner], 10)
                    for n, value in enumerate(sends):
                        table[n] = value
                    table[CHUNKS] = len(relays)
                    for n, value in enumerate(relays):
                        table[CHUNKS + 1 + n] = value

    relayed = table[CHUNKS]

    def leg(n, carry):
        entry = table[n]
        relay = place(entry & 3, (y + ((entry >> 2) & 3)) % 4, (entry >> 4) & 1)
        slot = (entry >> 5) & 127
        number = entry >> 12

        @pl.when(slot == DIRECT)
        def _():
            pltpu.make_async_remote_copy(
                aff.at[rows(number)], arrived.at[rows(number)], leg_send.at[n], final_sem.at[number // 4],
                device_id=partner, device_id_type=LOGICAL,
            ).start()

        @pl.when(slot != DIRECT)
        def _():
            pltpu.make_async_remote_copy(
                aff.at[rows(number)], mid.at[rows(slot)], leg_send.at[n], leg_recv.at[slot],
                device_id=relay, device_id_type=LOGICAL,
            ).start()

        return carry

    def legs(first, last):
        @pl.when(jnp.logical_not(on_diagonal))
        def _():
            lax.fori_loop(first, last, leg, 0)

    def hop(n, carry):
        @pl.when(n < relayed)
        def _():
            entry = table[CHUNKS + 1 + n]
            source = place(entry & 3, (y + ((entry >> 2) & 3)) % 4, (entry >> 4) & 1)
            number = entry >> 5
            wait(mid.at[rows(n)], leg_recv.at[n])
            pltpu.make_async_remote_copy(
                mid.at[rows(n)], arrived.at[rows(number)], hop_send.at[n], final_sem.at[number // 4],
                device_id=mirror(source), device_id_type=LOGICAL,
            ).start()

        return carry

    legs(0, CHUNKS)

    def start_load(n, carry):
        load(n).start()
        return carry

    lax.fori_loop(0, groups, start_load, 0)

    @pl.when(on_diagonal)
    def _():
        def own(n, carry):
            pltpu.make_async_copy(aff.at[group(n)], arrived.at[group(n)], final_sem.at[n]).start()
            return carry

        lax.fori_loop(0, groups, own, 0)

    for t in range(groups):
        tile = col * groups + t
        bits = (words[pl.ds(tile // 30, 1), :] >> (tile % 30)) & 1
        mask_rows[t : t + 1, :] = bits.astype(jnp.float32)
    col_sums[...] = jnp.zeros_like(col_sums)

    def prune(n, carry):
        load(n).wait()
        mask = mask_rows[:, group(n)].T
        total = jnp.zeros((TILE, TILE), jnp.float32)
        for t in range(groups):
            lanes = slice(t * TILE, (t + 1) * TILE)
            kept = block[group(n), lanes] * mask[:, t : t + 1]
            block[group(n), lanes] = kept
            total += kept
            col_sums[:, lanes] += jnp.sum(kept, axis=0, keepdims=True)
        row_sums[:, group(n)] = jnp.sum(total.T, axis=0, keepdims=True)
        return carry

    lax.fori_loop(0, groups, prune, 0)
    row_shares[col] = row_sums[...]
    col_shares[row] = col_sums[...]

    def share(n, carry):
        other = (col + 1 + n) % SIDE
        pltpu.make_async_remote_copy(
            row_shares.at[col], row_shares.at[col], row_send.at[n], row_recv.at[col],
            device_id=row * SIDE + other, device_id_type=LOGICAL,
        ).start()
        other = (row + 1 + n) % SIDE
        pltpu.make_async_remote_copy(
            col_shares.at[row], col_shares.at[row], col_send.at[n], col_recv.at[row],
            device_id=other * SIDE + col, device_id_type=LOGICAL,
        ).start()
        return carry

    lax.fori_loop(0, SIDE - 1, share, 0)
    lax.fori_loop(0, MAX_RELAYED, hop, 0)

    def share_in(n, carry):
        other = (col + 1 + n) % SIDE
        wait(row_shares.at[other], row_recv.at[other])
        other = (row + 1 + n) % SIDE
        wait(col_shares.at[other], col_recv.at[other])
        return carry

    lax.fori_loop(0, SIDE - 1, share_in, 0)
    row_total, col_total = row_shares[0], col_shares[0]
    for n in range(1, SIDE):
        row_total += row_shares[n]
        col_total += col_shares[n]
    near[0] = row_total
    near[1] = col_total
    to_partner(near, far, pair_sem)

    wait(far_words, word_sem.at[1])
    for t in range(groups):
        tile = row * groups + t
        bits = (far_words[pl.ds(tile // 30, 1), :] >> (tile % 30)) & 1
        far_mask[t : t + 1, :] = bits.astype(jnp.float32)

    def store(n):
        return pltpu.make_async_copy(block.at[:, group(n)], s_out.at[:, group(n)], out_sem.at[n])

    def finish(n, carry):
        wait(arrived.at[group(n)], final_sem.at[n])
        for t in range(groups):
            span = slice(t * TILE, (t + 1) * TILE)
            mirrored = arrived[group(n), span].T * far_mask[t : t + 1, group(n)]
            block[span, group(n)] = 0.5 * (block[span, group(n)] + mirrored)
        store(n).start()
        return carry

    lax.fori_loop(0, groups, finish, 0)
    wait(far, pair_sem.at[1])
    deg_out[0:1, :] = 0.5 * (near[0] + far[1])
    deg_out[1:2, :] = 0.5 * (far[0] + near[1])

    @pl.when(jnp.logical_not(on_diagonal))
    def _():
        def sent(n, carry):
            wait(mid.at[rows(n)], leg_send.at[n])
            return carry

        lax.fori_loop(0, CHUNKS, sent, 0)
        wait(far_words, word_sem.at[0])
        wait(far, pair_sem.at[0])

    def hopped(n, carry):
        @pl.when(n < relayed)
        def _():
            wait(mid.at[rows(n)], hop_send.at[n])

        return carry

    lax.fori_loop(0, MAX_RELAYED, hopped, 0)

    def share_out(n, carry):
        wait(row_shares.at[col], row_send.at[n])
        wait(col_shares.at[row], col_send.at[n])
        return carry

    lax.fori_loop(0, SIDE - 1, share_out, 0)

    def stored(n, carry):
        store(n).wait()
        return carry

    lax.fori_loop(0, groups, stored, 0)


def on_device(affinity, keep_words):
    size, _ = affinity.shape
    groups = size // TILE
    words = keep_words.T
    vec = pltpu.VMEM((1, size), jnp.float32)
    dma = pltpu.SemaphoreType.DMA
    symmetric, degrees = pl.pallas_call(
        kernel,
        out_shape=(
            jax.ShapeDtypeStruct((size, size), jnp.float32),
            jax.ShapeDtypeStruct((2, size), jnp.float32),
        ),
        in_specs=[pl.BlockSpec(memory_space=pltpu.HBM), pl.BlockSpec(memory_space=pltpu.VMEM)],
        out_specs=(pl.BlockSpec(memory_space=pl.ANY), pl.BlockSpec(memory_space=pltpu.VMEM)),
        scratch_shapes=[
            pltpu.SMEM((CHUNKS + 1 + MAX_RELAYED,), jnp.int32),
            pltpu.VMEM((size, size), jnp.float32),
            pltpu.VMEM((MAX_RELAYED * size // CHUNKS, size), jnp.float32),
            pltpu.VMEM((size, size), jnp.float32),
            pltpu.VMEM(words.shape, jnp.int32),
            pltpu.VMEM((groups, size), jnp.float32),
            pltpu.VMEM((groups, size), jnp.float32),
            vec, vec,
            pltpu.VMEM((SIDE, 1, size), jnp.float32),
            pltpu.VMEM((SIDE, 1, size), jnp.float32),
            pltpu.VMEM((2, 1, size), jnp.float32),
            pltpu.VMEM((2, 1, size), jnp.float32),
            dma((groups,)), dma((2,)),
            dma((CHUNKS,)), dma((MAX_RELAYED,)), dma((MAX_RELAYED,)), dma((groups,)),
            dma((SIDE - 1,)), dma((SIDE,)), dma((SIDE - 1,)), dma((SIDE,)), dma((2,)), dma((groups,)),
        ],
        compiler_params=pltpu.CompilerParams(has_side_effects=True, vmem_limit_bytes=47 << 20),
        name="exchange",
    )(affinity, words)
    total = size * SIDE
    left, right = lax.rsqrt(degrees[0]), lax.rsqrt(degrees[1])
    normalized = total * symmetric * left[:, None] * right[None, :]
    return normalized, degrees[0] / total


def solution(mesh):
    in_specs = (P("row", "col"), P("row", None))
    out_specs = (P("row", "col"), P("row"))
    return jax.shard_map(
        on_device, mesh=mesh, in_specs=in_specs, out_specs=out_specs, check_vma=False
    )
```
